32 devices in a mesh: seq: 16 (over z, x, core), batch: 2 (over y).
Axes of the slice: x: 2, y: 2, z: 4, core: 2. Of those that a mesh axis runs over, the one named last changes fastest.
Arguments:
- inputs: bfloat16 [2, 4096, 1024], P('batch', 'seq'), may hold values from -6 to 6
- grad_out: bfloat16 [2, 4096, 1024], P('batch', 'seq'), may hold values from -6 to 6
- spectrum: float32 [2, 32, 256, 1024], P(None, 'seq', None, 'batch'), may hold values from -6 to 6
- first_moment: float32 [2, 32, 256, 1024], P(None, 'seq', None, 'batch'), may hold values from -2 to 2
- second_moment: float32 [2, 32, 256, 1024], P(None, 'seq', None, 'batch'), may hold values from 0.1 to 4
Outputs:
- new_spectrum: float32 [2, 32, 256, 1024], P(None, 'seq', None, 'batch')
- new_first: float32 [2, 32, 256, 1024], P(None, 'seq', None, 'batch')
- new_second: float32 [2, 32, 256, 1024], P(None, 'seq', None, 'batch')
- filtered: bfloat16 [2, 4096, 1024], P('batch', 'seq')
The draws below stay inside these ranges and needn't reach their ends.
All inputs are finite; a program needn't handle non-finite values.
Results may differ from the reference program's by a relative error of at most 0.0055.
Values may be sent and summed in bfloat16 or wider, within the bound.
No kernel may reach another device: no remote copies, remote signals or barrier semaphores. Data moves between devices by JAX's collectives and lax.ppermute only.
A program may use at most 64 MiB of HBM per device.

```python
import math
import jax
import jax.numpy as jnp
from jax import lax

H = 1024
SEQ_DEV = 256
SEQ = 4096
BATCH = 2
FREQ_OUTER = 32


def strengthened(array, own_key, source, target, blocks, factor):
    owner, partner = [(jnp.arange(array.shape[position]) // (array.shape[position] // blocks)).reshape([-1 if axis == position else 1 for axis in range(array.ndim)]) for position in (source, target)]
    chosen = jax.random.permutation(own_key, blocks)[partner]
    strong = (owner == chosen) | (owner == (partner + blocks // 2) % blocks)
    return jnp.where(strong, factor * array, array)


def block_levels(rng, dims, cuts, low, high):
    def one(axis_at, parts):
        heights = jax.random.uniform(jax.random.fold_in(jax.random.fold_in(rng, 6), axis_at), (parts,), jnp.float32, low / len(cuts), high / len(cuts))
        return jnp.repeat(jnp.exp(heights), dims[axis_at] // parts).reshape((-1,) + (1,) * (len(dims) - axis_at - 1))

    loudness = one(*cuts[0])
    for cut in cuts[1:]:
        loudness = loudness * one(*cut)
    return loudness


def gaussian(rng, extent, scale, bound, cuts=(), kind=jnp.bfloat16):
    values = scale * jax.random.normal(rng, extent, jnp.float32)
    if cuts:
        values = values * block_levels(rng, extent, cuts, -0.22, 0.18)
    return jnp.clip(values, -bound, bound).astype(kind)


def bell_draw_with(own_key, shape, spread, limit, pieces, heavy, held_as=jnp.bfloat16):
    array = spread * jax.random.normal(own_key, shape, jnp.float32)
    if pieces:
        array = array * block_levels(own_key, shape, pieces, -0.22, 0.18)
    return jnp.clip(strengthened(array, jax.random.fold_in(own_key, 3), *heavy), -limit, limit).astype(held_as)


def setup_inputs(seed: int = 0) -> dict:
    streams_of = jax.random.split(jax.random.key(seed), 6)
    return {
        "inputs": gaussian(streams_of[0], (BATCH, SEQ, H), 1.0, 6.0, ((0, 2), (1, 16))),
        "grad_out": bell_draw_with(streams_of[1], (BATCH, SEQ, H), 1.0, 6.0, ((0, 2), (1, 16)), (0, 2, 2, 2.0)),
        "spectrum": gaussian(streams_of[2], (2, FREQ_OUTER, SEQ_DEV, H), 1.0, 6.0, ((1, 16), (3, 2)), jnp.float32),
        "first_moment": gaussian(streams_of[3], (2, FREQ_OUTER, SEQ_DEV, H), 0.3, 2.0, ((1, 16), (3, 2)), jnp.float32),
        "second_moment": jnp.clip(jnp.exp(math.log(4.0) - 3.6888794 * jax.random.uniform(streams_of[4], (2, FREQ_OUTER, SEQ_DEV, H), jnp.float32) ** block_levels(streams_of[4], (2, FREQ_OUTER, SEQ_DEV, H), ((1, 16), (3, 2)), -0.2, 0.2)), 0.1, 4.0),
    }


def spectra(sequence):
    padded = jnp.concatenate([sequence.astype(jnp.float32), jnp.zeros((SEQ, H), jnp.float32)], axis=0)
    transform = jnp.fft.fft(padded, axis=0)
    return transform.reshape(SEQ_DEV, FREQ_OUTER, H).transpose(1, 0, 2)

def reference(inputs, grad_out, spectrum, first_moment, second_moment):
    full_length = 2 * SEQ

    def accumulate(carry, pair):
        signal_spec = spectra(pair[0])
        grad_spec = spectra(pair[1])
        product = jnp.conj(signal_spec) * grad_spec
        term = jnp.stack([jnp.real(product), jnp.imag(product)]) / full_length
        return (carry + term, None)
    start_grad = jnp.zeros((2, FREQ_OUTER, SEQ_DEV, H), jnp.float32)
    grad, unused = lax.scan(accumulate, start_grad, (inputs, grad_out))
    new_first = 0.9 * first_moment + 0.1 * grad
    new_second = 0.99 * second_moment + 0.01 * grad * grad
    new_spectrum = spectrum - 0.5 * jnp.tanh(new_first / (jnp.sqrt(new_second) + 1e-06))
    complex_filter = new_spectrum[0] + 1j * new_spectrum[1]

    def reapply(sequence):
        product = spectra(sequence) * complex_filter
        ordered = product.transpose(1, 0, 2).reshape(full_length, H)
        result = jnp.real(jnp.fft.ifft(ordered, axis=0))[:SEQ]
        return result.astype(jnp.bfloat16)
    filtered = lax.map(reapply, inputs)
    return (new_spectrum, new_first, new_second, filtered)
```

```python
import functools
import math

import jax
import jax.numpy as jnp
import numpy as np
from jax import lax
from jax.experimental import pallas as pl
from jax.experimental.pallas import tpu as pltpu
from jax.sharding import PartitionSpec as P

step_rate = 0.5
epsilon = 1e-06
sub = 16
lane = 128


def turn_table(numer, modulus):
    phase = 2.0 * math.pi * (numer % modulus) / modulus
    return np.cos(phase), np.sin(phase)


def twist_table(outer, points):
    half = outer // 2
    index = np.arange(half + 1)[:, None] * np.arange(points)[None, :]
    cos, sin = turn_table(index, outer * points)
    return np.stack([cos, sin], axis=1).astype(np.float32)


def point_matrices(points, scale_back):
    index = np.arange(points)[:, None] * np.arange(points)[None, :]
    cos, sin = turn_table(index, points)
    ahead = np.block([[cos, -sin], [sin, cos]])
    back = np.block([[cos, sin], [-sin, cos]]) * scale_back
    return ahead.astype(np.float32), back.astype(np.float32)


def times_phase(re, im, turns, count):
    if turns == 0:
        return re, im
    if 4 * turns == count:
        return im, -re
    cos = math.cos(2.0 * math.pi * turns / count)
    sin = math.sin(2.0 * math.pi * turns / count)
    return re * cos + im * sin, im * cos - re * sin


def half_spectrum(values):
    total = 2 * len(values)
    if total == 2:
        return [(values[0], None), (values[0], None)]
    even = half_spectrum(values[0::2])
    odd = half_spectrum(values[1::2])
    quarter = total // 4
    out = [None] * (total // 2 + 1)
    for index in range(quarter + 1):
        even_re, even_im = even[index]
        odd_re, odd_im = odd[index]
        if index == 0:
            out[0] = (even_re + odd_re, None)
            out[total // 2] = (even_re - odd_re, None)
        elif index == quarter:
            out[index] = (even_re, -odd_re)
        else:
            turned_re, turned_im = times_phase(odd_re, odd_im, index, total)
            out[index] = (even_re + turned_re, even_im + turned_im)
            out[total // 2 - index] = (even_re - turned_re, turned_im - even_im)
    return out


def real_segments(bins):
    count = 2 * (len(bins) - 1)
    if count == 2:
        return [bins[0][0] + bins[1][0]]
    quarter = count // 4
    even = [None] * (quarter + 1)
    odd = [None] * (quarter + 1)
    for index in range(quarter + 1):
        low_re, low_im = bins[index]
        high_re, high_im = bins[count // 2 - index]
        if index == 0:
            even[0] = (low_re + high_re, None)
            odd[0] = (low_re - high_re, None)
        elif index == quarter:
            even[index] = (low_re, None)
            odd[index] = (-low_im, None)
        else:
            even[index] = (low_re + high_re, low_im - high_im)
            diff_re, diff_im = low_re - high_re, low_im + high_im
            cos = math.cos(2.0 * math.pi * index / count)
            sin = math.sin(2.0 * math.pi * index / count)
            odd[index] = (diff_re * cos - diff_im * sin, diff_re * sin + diff_im * cos)
    first = real_segments(even)
    second = real_segments(odd)
    return [item for pair in zip(first, second) for item in pair]


both_last = (((1,), (1,)), ((), ()))
both_first = (((0,), (0,)), ((), ()))


def square_eye(points, flipped):
    row = lax.broadcasted_iota(jnp.int32, (points, points), 0)
    col = lax.broadcasted_iota(jnp.int32, (points, points), 1)
    picked = jnp.where(flipped, points - 1 - col, col)
    return jnp.where(row == picked, 1.0, 0.0).astype(jnp.bfloat16)


def pack_kernel(signal_ref, cotangent_ref, out_ref, *, narrow):
    points, width = signal_ref.shape
    eye = square_eye(width, False)
    for part, source in enumerate((signal_ref, cotangent_ref)):
        turned = lax.dot_general(eye, source[...], both_last, preferred_element_type=jnp.float32)
        turned = turned.astype(jnp.bfloat16).reshape(width // narrow, narrow, points)
        out_ref[:, part * narrow : (part + 1) * narrow, :] = turned


def pack_call(signal, cotangent, narrow):
    points, channels = signal.shape
    width = math.gcd(channels, 256)
    return pl.pallas_call(
        functools.partial(pack_kernel, narrow=narrow),
        grid=(channels // width,),
        in_specs=[pl.BlockSpec((points, width), lambda step: (0, step))] * 2,
        out_specs=pl.BlockSpec((width // narrow, 2 * narrow, points), lambda step: (step, 0, 0)),
        out_shape=jax.ShapeDtypeStruct((channels // narrow, 2 * narrow, points), jnp.bfloat16),
        name="pack",
    )(signal, cotangent)


def unpack_kernel(in_ref, out_ref):
    eye = square_eye(out_ref.shape[0], False)
    out_ref[...] = lax.dot_general(
        eye, in_ref[...], both_last, preferred_element_type=jnp.float32
    ).astype(jnp.bfloat16)


def unpack_call(rows):
    channels, points = rows.shape
    width = math.gcd(channels, 256)
    return pl.pallas_call(
        unpack_kernel,
        grid=(channels // width,),
        in_specs=[pl.BlockSpec((width, points), lambda step: (step, 0))],
        out_specs=pl.BlockSpec((points, width), lambda step: (0, step)),
        out_shape=jax.ShapeDtypeStruct((points, channels), jnp.bfloat16),
        name="unpack",
    )(rows)


def forward_kernel(in_ref, twist_ref, matrix_ref, grad_ref, spectra_ref, mid_ref, *, scale):
    sequences, segments, pair_rows, points = in_ref.shape
    narrow = pair_rows // 2
    rows = sequences * narrow
    tiles = pair_rows // sub
    residue = pl.program_id(0)

    @pl.when(residue == 0)
    def _():
        def tile_step(step, carry):
            which = step // tiles
            piece = step % tiles
            start = pl.multiple_of(piece * sub, sub)
            target = (piece // (tiles // 2)) * rows + which * narrow
            target = pl.multiple_of(target + (piece % (tiles // 2)) * sub, sub)
            for left in range(0, points, lane):
                values = [
                    in_ref[which, seg, pl.ds(start, sub), left : left + lane].astype(jnp.float32)
                    for seg in range(segments)
                ]
                for index, (re, im) in enumerate(half_spectrum(values)):
                    cos = twist_ref[index, 0:1, left : left + lane]
                    sin = twist_ref[index, 1:2, left : left + lane]
                    if im is None:
                        new_re, new_im = re * cos, -(re * sin)
                    else:
                        new_re, new_im = re * cos + im * sin, im * cos - re * sin
                    mid_ref[index, pl.ds(target, sub), left : left + lane] = new_re.astype(jnp.bfloat16)
                    mid_ref[index, pl.ds(target, sub), points + left : points + left + lane] = (
                        new_im.astype(jnp.bfloat16)
                    )
            return carry

        lax.fori_loop(0, sequences * tiles, tile_step, 0)

    full = jnp.dot(mid_ref[residue], matrix_ref[0], preferred_element_type=jnp.float32)
    full = full + jnp.dot(mid_ref[residue], matrix_ref[1], preferred_element_type=jnp.float32)
    signal_re, signal_im = full[:rows, :points], full[:rows, points:]
    cotan_re, cotan_im = full[rows:, :points], full[rows:, points:]
    spectra_ref[0, 0] = signal_re
    spectra_ref[0, 1] = signal_im
    real_term = signal_re * cotan_re + signal_im * cotan_im
    imag_term = signal_re * cotan_im - signal_im * cotan_re
    real_sum = jnp.sum(real_term.reshape(sequences, narrow, points), axis=0) * scale
    imag_sum = jnp.sum(imag_term.reshape(sequences, narrow, points), axis=0) * scale
    grad_ref[residue, 0] = real_sum.astype(jnp.bfloat16)
    grad_ref[residue, 1] = imag_sum.astype(jnp.bfloat16)

    @pl.when(jnp.logical_and(residue > 0, residue < segments))
    def _():
        grad_ref[2 * segments - residue, 0] = real_sum.astype(jnp.bfloat16)
        grad_ref[2 * segments - residue, 1] = (-imag_sum).astype(jnp.bfloat16)


def forward_call(arrived, twist, matrices):
    sequences, segments, pair_rows, points = arrived.shape
    narrow = pair_rows // 2
    outer = 2 * segments
    rows = sequences * narrow
    fixed4 = lambda step: (0, 0, 0, 0)
    fixed3 = lambda step: (0, 0, 0)
    return pl.pallas_call(
        functools.partial(forward_kernel, scale=1.0 / (outer * points)),
        grid=(segments + 1,),
        in_specs=[
            pl.BlockSpec(arrived.shape, fixed4),
            pl.BlockSpec(twist.shape, fixed3),
            pl.BlockSpec(matrices.shape, fixed3),
        ],
        out_specs=[
            pl.BlockSpec((outer, 2, narrow, points), fixed4),
            pl.BlockSpec((1, 2, rows, points), lambda step: (step, 0, 0, 0)),
        ],
        out_shape=[
            jax.ShapeDtypeStruct((outer, 2, narrow, points), jnp.bfloat16),
            jax.ShapeDtypeStruct((segments + 1, 2, rows, points), jnp.float32),
        ],
        scratch_shapes=[pltpu.VMEM((segments + 1, 2 * rows, 2 * points), jnp.bfloat16)],
        name="forward",
    )(arrived, twist, matrices)


def update_kernel(
    flip_ref, grad_ref, spec_ref, first_ref, second_ref, new_spec_ref, new_first_ref, new_second_ref, out_ref
):
    points, width = spec_ref.shape[2:]
    blocks, _, _, narrow, _ = grad_ref.shape
    eye = square_eye(points, flip_ref[pl.program_id(0)] > 0)
    for part in range(2):
        sent = grad_ref[:, 0, part].reshape(width, points)
        grad = lax.dot_general(eye, sent, both_last, preferred_element_type=jnp.float32)
        new_first = 0.9 * first_ref[part, 0] + 0.1 * grad
        new_second = 0.99 * second_ref[part, 0] + 0.01 * grad * grad
        new_spec = spec_ref[part, 0] - step_rate * jnp.tanh(new_first / (jnp.sqrt(new_second) + epsilon))
        new_spec_ref[part, 0] = new_spec
        new_first_ref[part, 0] = new_first
        new_second_ref[part, 0] = new_second
        turned = lax.dot_general(
            new_spec.astype(jnp.bfloat16), eye, both_first, preferred_element_type=jnp.float32
        )
        out_ref[:, 0, part] = turned.astype(jnp.bfloat16).reshape(blocks, narrow, points)


def update_call(flips, sent, spectrum, first_moment, second_moment, width):
    groups, local_outer, _, narrow, points = sent.shape
    channels = spectrum.shape[3]
    blocks = width // narrow
    state = pl.BlockSpec((2, 1, points, width), lambda row, col, flags: (0, row, 0, col))
    wire = pl.BlockSpec((blocks, 1, 2, narrow, points), lambda row, col, flags: (col, row, 0, 0, 0))
    return pl.pallas_call(
        update_kernel,
        grid_spec=pltpu.PrefetchScalarGridSpec(
            num_scalar_prefetch=1,
            grid=(local_outer, channels // width),
            in_specs=[wire, state, state, state],
            out_specs=[state, state, state, wire],
        ),
        out_shape=[jax.ShapeDtypeStruct(spectrum.shape, jnp.float32)] * 3
        + [jax.ShapeDtypeStruct(sent.shape, jnp.bfloat16)],
        name="update",
    )(flips, sent, spectrum, first_moment, second_moment)


def inverse_kernel(spectra_ref, filter_ref, twist_ref, matrix_ref, out_ref, mid_ref):
    sequences, segments, narrow, points = out_ref.shape
    rows = sequences * narrow
    residue = pl.program_id(0)
    mirror = lax.rem(2 * segments - residue, 2 * segments)
    paired = jnp.where(jnp.logical_and(residue > 0, residue < segments), 1.0, 0.0)
    filter_re = filter_ref[residue, 0].astype(jnp.float32) + paired * filter_ref[mirror, 0].astype(jnp.float32)
    filter_im = filter_ref[residue, 1].astype(jnp.float32) - paired * filter_ref[mirror, 1].astype(jnp.float32)
    signal_re = spectra_ref[0, 0].reshape(sequences, narrow, points)
    signal_im = spectra_ref[0, 1].reshape(sequences, narrow, points)
    mixed_re = (signal_re * filter_re - signal_im * filter_im).reshape(rows, points)
    mixed_im = (signal_re * filter_im + signal_im * filter_re).reshape(rows, points)
    mixed = jnp.concatenate([mixed_re.astype(jnp.bfloat16), mixed_im.astype(jnp.bfloat16)], axis=1)
    full = jnp.dot(mixed, matrix_ref[0], preferred_element_type=jnp.float32)
    full = full + jnp.dot(mixed, matrix_ref[1], preferred_element_type=jnp.float32)
    cos = twist_ref[residue, 0:1]
    sin = twist_ref[residue, 1:2]
    mid_ref[residue, 0] = full[:, :points] * cos - full[:, points:] * sin
    mid_ref[residue, 1] = full[:, :points] * sin + full[:, points:] * cos

    @pl.when(residue == segments)
    def _():
        tiles = narrow // sub

        def tile_step(step, carry):
            which = step // tiles
            start = pl.multiple_of((step % tiles) * sub, sub)
            source = pl.multiple_of(step * sub, sub)
            for left in range(0, points, lane):
                bins = [
                    tuple(mid_ref[index, part, pl.ds(source, sub), left : left + lane] for part in range(2))
                    for index in range(segments + 1)
                ]
                for seg, value in enumerate(real_segments(bins)):
                    out_ref[which, seg, pl.ds(start, sub), left : left + lane] = value.astype(jnp.bfloat16)
            return carry

        lax.fori_loop(0, sequences * tiles, tile_step, 0)


def inverse_call(spectra, filters, twist, matrices):
    residues, _, rows, points = spectra.shape
    segments = residues - 1
    narrow = filters.shape[2]
    sequences = rows // narrow
    fixed4 = lambda step: (0, 0, 0, 0)
    fixed3 = lambda step: (0, 0, 0)
    return pl.pallas_call(
        inverse_kernel,
        grid=(residues,),
        in_specs=[
            pl.BlockSpec((1, 2, rows, points), lambda step: (step, 0, 0, 0)),
            pl.BlockSpec(filters.shape, fixed4),
            pl.BlockSpec(twist.shape, fixed3),
            pl.BlockSpec(matrices.shape, fixed3),
        ],
        out_specs=pl.BlockSpec((sequences, segments, narrow, points), fixed4),
        out_shape=jax.ShapeDtypeStruct((sequences, segments, narrow, points), jnp.bfloat16),
        scratch_shapes=[pltpu.VMEM((residues, 2, rows, points), jnp.float32)],
        name="inverse",
    )(spectra, filters, twist, matrices)


def pack_plain(signal, cotangent, narrow):
    points, channels = signal.shape
    both = jnp.stack([signal, cotangent]).reshape(2, points, channels // narrow, narrow)
    return both.transpose(2, 0, 3, 1).reshape(channels // narrow, 2 * narrow, points)


def split_dot(values, matrices):
    first = jnp.dot(values, matrices[0], preferred_element_type=jnp.float32)
    return first + jnp.dot(values, matrices[1], preferred_element_type=jnp.float32)


def forward_plain(arrived, twist, matrices):
    sequences, segments, pair_rows, points = arrived.shape
    narrow = pair_rows // 2
    rows = sequences * narrow
    parts = arrived.reshape(sequences, segments, 2, narrow, points).astype(jnp.float32)
    parts = parts.transpose(1, 2, 0, 3, 4).reshape(segments, 2 * rows, points)
    bins = half_spectrum([parts[seg] for seg in range(segments)])
    re = jnp.stack([item[0] for item in bins])
    im = jnp.stack([jnp.zeros_like(item[0]) if item[1] is None else item[1] for item in bins])
    cos, sin = twist[:, 0][:, None], twist[:, 1][:, None]
    mid = jnp.concatenate([re * cos + im * sin, im * cos - re * sin], axis=2).astype(jnp.bfloat16)
    full = split_dot(mid, matrices)
    signal_re, signal_im = full[:, :rows, :points], full[:, :rows, points:]
    cotan_re, cotan_im = full[:, rows:, :points], full[:, rows:, points:]
    shape = (segments + 1, sequences, narrow, points)
    scale = 1.0 / (2 * segments * points)
    real = jnp.sum((signal_re * cotan_re + signal_im * cotan_im).reshape(shape), axis=1) * scale
    imag = jnp.sum((signal_re * cotan_im - signal_im * cotan_re).reshape(shape), axis=1) * scale
    real = jnp.concatenate([real, real[1:segments][::-1]])
    imag = jnp.concatenate([imag, -imag[1:segments][::-1]])
    grad = jnp.stack([real, imag], axis=1).astype(jnp.bfloat16)
    return grad, jnp.stack([signal_re, signal_im], axis=1)


def update_plain(flips, sent, spectrum, first_moment, second_moment):
    groups, local_outer, _, narrow, points = sent.shape
    flipped = (flips > 0)[None, :, None, None]
    arrived = sent.astype(jnp.float32).transpose(2, 1, 4, 0, 3).reshape(spectrum.shape)
    grad = jnp.where(flipped, arrived[:, :, ::-1], arrived)
    new_first = 0.9 * first_moment + 0.1 * grad
    new_second = 0.99 * second_moment + 0.01 * grad * grad
    new_spec = spectrum - step_rate * jnp.tanh(new_first / (jnp.sqrt(new_second) + epsilon))
    out = jnp.where(flipped, new_spec[:, :, ::-1], new_spec).astype(jnp.bfloat16)
    out = out.reshape(2, local_outer, points, groups, narrow).transpose(3, 1, 0, 4, 2)
    return new_spec, new_first, new_second, out


def inverse_plain(spectra, filters, twist, matrices):
    residues, _, rows, points = spectra.shape
    segments = residues - 1
    narrow = filters.shape[2]
    sequences = rows // narrow
    wide = filters.astype(jnp.float32)
    mirrored = jnp.concatenate([jnp.zeros_like(wide[:1]), wide[segments + 1 :][::-1], jnp.zeros_like(wide[:1])])
    filter_re = (wide[: segments + 1, 0] + mirrored[:, 0])[:, None]
    filter_im = (wide[: segments + 1, 1] - mirrored[:, 1])[:, None]
    shape = (residues, sequences, narrow, points)
    signal_re, signal_im = spectra[:, 0].reshape(shape), spectra[:, 1].reshape(shape)
    mixed_re = (signal_re * filter_re - signal_im * filter_im).reshape(residues, rows, points)
    mixed_im = (signal_re * filter_im + signal_im * filter_re).reshape(residues, rows, points)
    full = split_dot(jnp.concatenate([mixed_re, mixed_im], axis=2).astype(jnp.bfloat16), matrices)
    cos, sin = twist[:, 0][:, None], twist[:, 1][:, None]
    mid_re = full[..., :points] * cos - full[..., points:] * sin
    mid_im = full[..., :points] * sin + full[..., points:] * cos
    out = jnp.stack(real_segments([(mid_re[index], mid_im[index]) for index in range(residues)]))
    out = out.reshape(segments, sequences, narrow, points).transpose(1, 0, 2, 3)
    return out.astype(jnp.bfloat16)


def high_low(matrix):
    high = matrix.astype(jnp.bfloat16)
    low = (matrix - high.astype(np.float32)).astype(jnp.bfloat16)
    return np.stack([high, low])


def per_device(inputs, grad_out, spectrum, first_moment, second_moment):
    seq_count = lax.axis_size("seq")
    batch_count = lax.axis_size("batch")
    batch_rows, points, channels = inputs.shape
    narrow = channels // (seq_count * batch_count)
    local_outer = spectrum.shape[1]
    outer = 2 * seq_count
    tiled = narrow % sub == 0 and points % lane == 0 and batch_rows == 1
    twist = jnp.asarray(twist_table(outer, points))
    ahead, back = point_matrices(points, 1.0 / (outer * points))
    ahead, back = jnp.asarray(high_low(ahead)), jnp.asarray(high_low(back))

    pack = pack_call if tiled else pack_plain
    packed = jnp.stack([pack(inputs[row], grad_out[row], narrow) for row in range(batch_rows)], axis=1)
    arrived = lax.all_to_all(packed, ("batch", "seq"), split_axis=0, concat_axis=0, tiled=True)
    arrived = arrived.reshape(batch_count, seq_count, batch_rows, 2 * narrow, points)
    arrived = arrived.transpose(0, 2, 1, 3, 4).reshape(-1, seq_count, 2 * narrow, points)
    sequences = arrived.shape[0]

    grad, spectra = (forward_call if tiled else forward_plain)(arrived, twist, ahead)
    grad = grad.reshape(seq_count, local_outer, 2, narrow, points)
    sent = lax.all_to_all(grad, "seq", split_axis=0, concat_axis=0, tiled=True)

    residues = lax.axis_index("seq") * local_outer + jnp.arange(local_outer, dtype=jnp.int32)
    flips = (residues > seq_count).astype(jnp.int32)
    update = functools.partial(update_call, width=256) if tiled else update_plain
    new_spectrum, new_first, new_second, filters = update(flips, sent, spectrum, first_moment, second_moment)
    filters = lax.all_to_all(filters, "seq", split_axis=0, concat_axis=0, tiled=True)
    filters = filters.reshape(outer, 2, narrow, points)

    rows = (inverse_call if tiled else inverse_plain)(spectra, filters, twist, back)
    rows = rows.reshape(batch_count, batch_rows, seq_count, narrow, points).transpose(0, 2, 1, 3, 4)
    rows = rows.reshape(batch_count * seq_count, batch_rows, narrow, points)
    rows = lax.all_to_all(rows, ("batch", "seq"), split_axis=0, concat_axis=0, tiled=True)
    if tiled:
        filtered = unpack_call(rows.reshape(channels, points))[None]
    else:
        filtered = rows.transpose(1, 3, 0, 2).reshape(batch_rows, points, channels)
    return new_spectrum, new_first, new_second, filtered


def solution(mesh):
    return jax.shard_map(
        per_device,
        mesh=mesh,
        in_specs=(
            P("batch", "seq", None),
            P("batch", "seq", None),
            P(None, "seq", None, "batch"),
            P(None, "seq", None, "batch"),
            P(None, "seq", None, "batch"),
        ),
        out_specs=(
            P(None, "seq", None, "batch"),
            P(None, "seq", None, "batch"),
            P(None, "seq", None, "batch"),
            P("batch", "seq", None),
        ),
        check_vma=False,
    )
```

```python
import functools
import math

import jax
import jax.numpy as jnp
import numpy as np
from jax import lax
from jax.experimental import pallas as pl
from jax.experimental.pallas import tpu as pltpu
from jax.sharding import PartitionSpec as P

step_rate = 0.5
epsilon = 1e-06
sub = 16
lane = 128


def turn_table(numer, modulus):
    phase = 2.0 * math.pi * (numer % modulus) / modulus
    return np.cos(phase), np.sin(phase)


def twist_table(outer, points):
    half = outer // 2
    index = np.arange(half + 1)[:, None] * np.arange(points)[None, :]
    cos, sin = turn_table(index, outer * points)
    return np.stack([cos, sin], axis=1).astype(np.float32)


def point_matrices(points, scale_back):
    index = np.arange(points)[:, None] * np.arange(points)[None, :]
    cos, sin = turn_table(index, points)
    ahead = np.block([[cos, -sin], [sin, cos]])
    back = np.block([[cos, sin], [-sin, cos]]) * scale_back
    return ahead.astype(np.float32), back.astype(np.float32)


def times_phase(re, im, turns, count):
    if turns == 0:
        return re, im
    if 4 * turns == count:
        return im, -re
    cos = math.cos(2.0 * math.pi * turns / count)
    sin = math.sin(2.0 * math.pi * turns / count)
    return re * cos + im * sin, im * cos - re * sin


def half_spectrum(values):
    total = 2 * len(values)
    if total == 2:
        return [(values[0], None), (values[0], None)]
    even = half_spectrum(values[0::2])
    odd = half_spectrum(values[1::2])
    quarter = total // 4
    out = [None] * (total // 2 + 1)
    for index in range(quarter + 1):
        even_re, even_im = even[index]
        odd_re, odd_im = odd[index]
        if index == 0:
            out[0] = (even_re + odd_re, None)
            out[total // 2] = (even_re - odd_re, None)
        elif index == quarter:
            out[index] = (even_re, -odd_re)
        else:
            turned_re, turned_im = times_phase(odd_re, odd_im, index, total)
            out[index] = (even_re + turned_re, even_im + turned_im)
            out[total // 2 - index] = (even_re - turned_re, turned_im - even_im)
    return out


def real_segments(bins):
    count = 2 * (len(bins) - 1)
    if count == 2:
        return [bins[0][0] + bins[1][0]]
    quarter = count // 4
    even = [None] * (quarter + 1)
    odd = [None] * (quarter + 1)
    for index in range(quarter + 1):
        low_re, low_im = bins[index]
        high_re, high_im = bins[count // 2 - index]
        if index == 0:
            even[0] = (low_re + high_re, None)
            odd[0] = (low_re - high_re, None)
        elif index == quarter:
            even[index] = (low_re, None)
            odd[index] = (-low_im, None)
        else:
            even[index] = (low_re + high_re, low_im - high_im)
            diff_re, diff_im = low_re - high_re, low_im + high_im
            cos = math.cos(2.0 * math.pi * index / count)
            sin = math.sin(2.0 * math.pi * index / count)
            odd[index] = (diff_re * cos - diff_im * sin, diff_re * sin + diff_im * cos)
    first = real_segments(even)
    second = real_segments(odd)
    return [item for pair in zip(first, second) for item in pair]


both_last = (((1,), (1,)), ((), ()))
both_first = (((0,), (0,)), ((), ()))


def square_eye(points, flipped):
    row = lax.broadcasted_iota(jnp.int32, (points, points), 0)
    col = lax.broadcasted_iota(jnp.int32, (points, points), 1)
    picked = jnp.where(flipped, points - 1 - col, col)
    return jnp.where(row == picked, 1.0, 0.0).astype(jnp.bfloat16)


whole = pl.BlockSpec(memory_space=pltpu.VMEM)
roomy = pltpu.CompilerParams(vmem_limit_bytes=24 << 20)


def pack_kernel(signal_ref, cotangent_ref, out_ref, *, narrow, width):
    points, channels = signal_ref.shape
    for part, source in enumerate((signal_ref, cotangent_ref)):
        for left in range(0, channels, width):
            turned = source[:, left : left + width].T.reshape(width // narrow, narrow, points)
            first = left // narrow
            out_ref[first : first + width // narrow, part * narrow : (part + 1) * narrow, :] = turned


def pack_call(signal, cotangent, narrow):
    points, channels = signal.shape
    return pl.pallas_call(
        functools.partial(pack_kernel, narrow=narrow, width=math.gcd(channels, 256)),
        in_specs=[whole, whole],
        out_specs=whole,
        out_shape=jax.ShapeDtypeStruct((channels // narrow, 2 * narrow, points), jnp.bfloat16),
        compiler_params=roomy,
        name="pack",
    )(signal, cotangent)


def unpack_kernel(in_ref, out_ref):
    out_ref[...] = in_ref[...].T


def unpack_call(rows):
    channels, points = rows.shape
    width = math.gcd(channels, 512)
    return pl.pallas_call(
        unpack_kernel,
        grid=(channels // width,),
        in_specs=[pl.BlockSpec((width, points), lambda step: (step, 0))],
        out_specs=pl.BlockSpec((points, width), lambda step: (0, step)),
        out_shape=jax.ShapeDtypeStruct((points, channels), jnp.bfloat16),
        compiler_params=roomy,
        name="unpack",
    )(rows)


def over_chunks(emit, segments, chunk):
    emit(0, 1, False)
    emit(segments, 1, False)
    count = (segments - 1) // chunk

    def step(index, carry):
        emit(1 + index * chunk, chunk, True)
        return carry

    lax.fori_loop(0, count, step, 0)
    if (segments - 1) % chunk:
        emit(1 + count * chunk, (segments - 1) % chunk, True)


def split_dot(values, matrices):
    first = jnp.dot(values, matrices[0], preferred_element_type=jnp.float32)
    return first + jnp.dot(values, matrices[1], preferred_element_type=jnp.float32)


def forward_kernel(in_ref, twist_ref, matrix_ref, grad_ref, spectra_ref, mid_ref, *, scale, chunk):
    sequences, segments, pair_rows, points = in_ref.shape
    narrow = pair_rows // 2
    rows = sequences * narrow
    tiles = pair_rows // sub

    def tile_step(step, carry):
        which = step // tiles
        piece = step % tiles
        start = pl.multiple_of(piece * sub, sub)
        target = (piece // (tiles // 2)) * rows + which * narrow
        target = pl.multiple_of(target + (piece % (tiles // 2)) * sub, sub)
        for left in range(0, points, lane):
            here = slice(left, left + lane)
            after = slice(points + left, points + left + lane)
            values = [
                in_ref[which, seg, pl.ds(start, sub), here].astype(jnp.float32) for seg in range(segments)
            ]
            for index, (re, im) in enumerate(half_spectrum(values)):
                cos = twist_ref[index, 0:1, here]
                sin = twist_ref[index, 1:2, here]
                if im is None:
                    new_re, new_im = re * cos, -(re * sin)
                else:
                    new_re, new_im = re * cos + im * sin, im * cos - re * sin
                mid_ref[index, pl.ds(target, sub), here] = new_re.astype(jnp.bfloat16)
                mid_ref[index, pl.ds(target, sub), after] = new_im.astype(jnp.bfloat16)
        return carry

    lax.fori_loop(0, sequences * tiles, tile_step, 0)

    def emit(base, count, paired):
        values = mid_ref[pl.ds(base, count)].reshape(count * 2 * rows, 2 * points)
        full = split_dot(values, matrix_ref).reshape(count, 2 * rows, 2 * points)
        for extra in range(count):
            residue = base + extra
            signal_re, signal_im = full[extra, :rows, :points], full[extra, :rows, points:]
            cotan_re, cotan_im = full[extra, rows:, :points], full[extra, rows:, points:]
            spectra_ref[residue, 0] = signal_re
            spectra_ref[residue, 1] = signal_im
            real_term = signal_re * cotan_re + signal_im * cotan_im
            imag_term = signal_re * cotan_im - signal_im * cotan_re
            real_sum = jnp.sum(real_term.reshape(sequences, narrow, points), axis=0) * scale
            imag_sum = jnp.sum(imag_term.reshape(sequences, narrow, points), axis=0) * scale
            grad_ref[residue, 0] = real_sum.astype(jnp.bfloat16)
            grad_ref[residue, 1] = imag_sum.astype(jnp.bfloat16)
            if paired:
                grad_ref[2 * segments - residue, 0] = real_sum.astype(jnp.bfloat16)
                grad_ref[2 * segments - residue, 1] = (-imag_sum).astype(jnp.bfloat16)

    over_chunks(emit, segments, chunk)


def forward_call(arrived, twist, matrices):
    sequences, segments, pair_rows, points = arrived.shape
    narrow = pair_rows // 2
    outer = 2 * segments
    rows = sequences * narrow
    return pl.pallas_call(
        functools.partial(forward_kernel, scale=1.0 / (outer * points), chunk=5),
        in_specs=[whole, whole, whole],
        out_specs=[whole, whole],
        out_shape=[
            jax.ShapeDtypeStruct((outer, 2, narrow, points), jnp.bfloat16),
            jax.ShapeDtypeStruct((segments + 1, 2, rows, points), jnp.float32),
        ],
        scratch_shapes=[pltpu.VMEM((segments + 1, 2 * rows, 2 * points), jnp.bfloat16)],
        compiler_params=roomy,
        name="forward",
    )(arrived, twist, matrices)


def moved(grad, spec, first, second):
    new_first = 0.9 * first + 0.1 * grad
    new_second = 0.99 * second + 0.01 * grad * grad
    return spec - step_rate * jnp.tanh(new_first / (jnp.sqrt(new_second) + epsilon)), new_first, new_second


def filter_kernel(flip_ref, grad_ref, spec_ref, first_ref, second_ref, out_ref):
    _, local_outer, points, width = spec_ref.shape
    for row in range(local_outer):
        eye = square_eye(points, flip_ref[row] > 0)
        for part in range(2):
            sent = grad_ref[:, row, part].reshape(width, points)
            grad = lax.dot_general(eye, sent, both_last, preferred_element_type=jnp.float32)
            new_spec, _, _ = moved(grad, spec_ref[part, row], first_ref[part, row], second_ref[part, row])
            turned = lax.dot_general(
                new_spec.astype(jnp.bfloat16), eye, both_first, preferred_element_type=jnp.float32
            )
            out_ref[:, row, part] = turned.astype(jnp.bfloat16).reshape(grad_ref.shape[0], -1, points)


def filter_call(flips, sent, spectrum, first_moment, second_moment):
    return pl.pallas_call(
        filter_kernel,
        in_specs=[pl.BlockSpec(memory_space=pltpu.SMEM), whole, whole, whole, whole],
        out_specs=whole,
        out_shape=jax.ShapeDtypeStruct(sent.shape, jnp.bfloat16),
        compiler_params=roomy,
        name="filter",
    )(flips, sent, spectrum, first_moment, second_moment)


def update_kernel(
    flip_ref, grad_ref, spec_ref, first_ref, second_ref, new_spec_ref, new_first_ref, new_second_ref
):
    points, width = spec_ref.shape[2:]
    eye = square_eye(points, flip_ref[pl.program_id(0)] > 0)
    for part in range(2):
        sent = grad_ref[:, 0, part].reshape(width, points)
        grad = lax.dot_general(eye, sent, both_last, preferred_element_type=jnp.float32)
        new_spec, new_first, new_second = moved(
            grad, spec_ref[part, 0], first_ref[part, 0], second_ref[part, 0]
        )
        new_spec_ref[part, 0] = new_spec
        new_first_ref[part, 0] = new_first
        new_second_ref[part, 0] = new_second


def update_call(flips, sent, spectrum, first_moment, second_moment):
    groups, local_outer, _, narrow, points = sent.shape
    channels = spectrum.shape[3]
    state = pl.BlockSpec((2, 1, points, channels), lambda row, flags: (0, row, 0, 0))
    wire = pl.BlockSpec((groups, 1, 2, narrow, points), lambda row, flags: (0, row, 0, 0, 0))
    return pl.pallas_call(
        update_kernel,
        grid_spec=pltpu.PrefetchScalarGridSpec(
            num_scalar_prefetch=1,
            grid=(local_outer,),
            in_specs=[wire, state, state, state],
            out_specs=[state, state, state],
        ),
        out_shape=[jax.ShapeDtypeStruct(spectrum.shape, jnp.float32)] * 3,
        compiler_params=roomy,
        name="update",
    )(flips, sent, spectrum, first_moment, second_moment)


def inverse_kernel(spectra_ref, filter_ref, twist_ref, matrix_ref, out_ref, mid_ref, *, chunk):
    sequences, segments, narrow, points = out_ref.shape
    rows = sequences * narrow

    def mixed(residue, paired):
        filter_re = filter_ref[residue, 0].astype(jnp.float32)
        filter_im = filter_ref[residue, 1].astype(jnp.float32)
        if paired:
            filter_re = filter_re + filter_ref[2 * segments - residue, 0].astype(jnp.float32)
            filter_im = filter_im - filter_ref[2 * segments - residue, 1].astype(jnp.float32)
        signal_re = spectra_ref[residue, 0].reshape(sequences, narrow, points)
        signal_im = spectra_ref[residue, 1].reshape(sequences, narrow, points)
        mixed_re = (signal_re * filter_re - signal_im * filter_im).reshape(rows, points)
        mixed_im = (signal_re * filter_im + signal_im * filter_re).reshape(rows, points)
        return jnp.concatenate([mixed_re.astype(jnp.bfloat16), mixed_im.astype(jnp.bfloat16)], axis=1)

    def emit(base, count, paired):
        values = jnp.concatenate([mixed(base + extra, paired) for extra in range(count)], axis=0)
        full = split_dot(values, matrix_ref).reshape(count, rows, 2 * points)
        for extra in range(count):
            residue = base + extra
            cos = twist_ref[residue, 0:1]
            sin = twist_ref[residue, 1:2]
            mid_ref[residue, 0] = full[extra, :, :points] * cos - full[extra, :, points:] * sin
            mid_ref[residue, 1] = full[extra, :, :points] * sin + full[extra, :, points:] * cos

    over_chunks(emit, segments, chunk)
    tiles = narrow // sub

    def tile_step(step, carry):
        which = step // tiles
        start = pl.multiple_of((step % tiles) * sub, sub)
        source = pl.multiple_of(step * sub, sub)
        for left in range(0, points, lane):
            here = slice(left, left + lane)
            bins = [
                tuple(mid_ref[index, part, pl.ds(source, sub), here] for part in range(2))
                for index in range(segments + 1)
            ]
            for seg, value in enumerate(real_segments(bins)):
                out_ref[which, seg, pl.ds(start, sub), here] = value.astype(jnp.bfloat16)
        return carry

    lax.fori_loop(0, sequences * tiles, tile_step, 0)


def inverse_call(spectra, filters, twist, matrices):
    residues, _, rows, points = spectra.shape
    segments = residues - 1
    narrow = filters.shape[2]
    sequences = rows // narrow
    return pl.pallas_call(
        functools.partial(inverse_kernel, chunk=5),
        in_specs=[whole, whole, whole, whole],
        out_specs=whole,
        out_shape=jax.ShapeDtypeStruct((sequences, segments, narrow, points), jnp.bfloat16),
        scratch_shapes=[pltpu.VMEM((residues, 2, rows, points), jnp.float32)],
        compiler_params=roomy,
        name="inverse",
    )(spectra, filters, twist, matrices)


def pack_plain(signal, cotangent, narrow):
    points, channels = signal.shape
    both = jnp.stack([signal, cotangent]).reshape(2, points, channels // narrow, narrow)
    return both.transpose(2, 0, 3, 1).reshape(channels // narrow, 2 * narrow, points)


def forward_plain(arrived, twist, matrices):
    sequences, segments, pair_rows, points = arrived.shape
    narrow = pair_rows // 2
    rows = sequences * narrow
    parts = arrived.reshape(sequences, segments, 2, narrow, points).astype(jnp.float32)
    parts = parts.transpose(1, 2, 0, 3, 4).reshape(segments, 2 * rows, points)
    bins = half_spectrum([parts[seg] for seg in range(segments)])
    re = jnp.stack([item[0] for item in bins])
    im = jnp.stack([jnp.zeros_like(item[0]) if item[1] is None else item[1] for item in bins])
    cos, sin = twist[:, 0][:, None], twist[:, 1][:, None]
    mid = jnp.concatenate([re * cos + im * sin, im * cos - re * sin], axis=2).astype(jnp.bfloat16)
    full = split_dot(mid, matrices)
    signal_re, signal_im = full[:, :rows, :points], full[:, :rows, points:]
    cotan_re, cotan_im = full[:, rows:, :points], full[:, rows:, points:]
    shape = (segments + 1, sequences, narrow, points)
    scale = 1.0 / (2 * segments * points)
    real = jnp.sum((signal_re * cotan_re + signal_im * cotan_im).reshape(shape), axis=1) * scale
    imag = jnp.sum((signal_re * cotan_im - signal_im * cotan_re).reshape(shape), axis=1) * scale
    real = jnp.concatenate([real, real[1:segments][::-1]])
    imag = jnp.concatenate([imag, -imag[1:segments][::-1]])
    grad = jnp.stack([real, imag], axis=1).astype(jnp.bfloat16)
    return grad, jnp.stack([signal_re, signal_im], axis=1)


def gradient_plain(flips, sent, shape):
    arrived = sent.astype(jnp.float32).transpose(2, 1, 4, 0, 3).reshape(shape)
    return jnp.where((flips > 0)[None, :, None, None], arrived[:, :, ::-1], arrived)


def filter_plain(flips, sent, spectrum, first_moment, second_moment):
    groups, local_outer, _, narrow, points = sent.shape
    grad = gradient_plain(flips, sent, spectrum.shape)
    new_spec, _, _ = moved(grad, spectrum, first_moment, second_moment)
    out = jnp.where((flips > 0)[None, :, None, None], new_spec[:, :, ::-1], new_spec).astype(jnp.bfloat16)
    return out.reshape(2, local_outer, points, groups, narrow).transpose(3, 1, 0, 4, 2)


def update_plain(flips, sent, spectrum, first_moment, second_moment):
    return moved(gradient_plain(flips, sent, spectrum.shape), spectrum, first_moment, second_moment)


def inverse_plain(spectra, filters, twist, matrices):
    residues, _, rows, points = spectra.shape
    segments = residues - 1
    narrow = filters.shape[2]
    sequences = rows // narrow
    wide = filters.astype(jnp.float32)
    mirrored = jnp.concatenate([jnp.zeros_like(wide[:1]), wide[segments + 1 :][::-1], jnp.zeros_like(wide[:1])])
    filter_re = (wide[: segments + 1, 0] + mirrored[:, 0])[:, None]
    filter_im = (wide[: segments + 1, 1] - mirrored[:, 1])[:, None]
    shape = (residues, sequences, narrow, points)
    signal_re, signal_im = spectra[:, 0].reshape(shape), spectra[:, 1].reshape(shape)
    mixed_re = (signal_re * filter_re - signal_im * filter_im).reshape(residues, rows, points)
    mixed_im = (signal_re * filter_im + signal_im * filter_re).reshape(residues, rows, points)
    full = split_dot(jnp.concatenate([mixed_re, mixed_im], axis=2).astype(jnp.bfloat16), matrices)
    cos, sin = twist[:, 0][:, None], twist[:, 1][:, None]
    mid_re = full[..., :points] * cos - full[..., points:] * sin
    mid_im = full[..., :points] * sin + full[..., points:] * cos
    out = jnp.stack(real_segments([(mid_re[index], mid_im[index]) for index in range(residues)]))
    out = out.reshape(segments, sequences, narrow, points).transpose(1, 0, 2, 3)
    return out.astype(jnp.bfloat16)


def high_low(matrix):
    high = matrix.astype(jnp.bfloat16)
    low = (matrix - high.astype(np.float32)).astype(jnp.bfloat16)
    return np.stack([high, low])


def per_device(inputs, grad_out, spectrum, first_moment, second_moment):
    seq_count = lax.axis_size("seq")
    batch_count = lax.axis_size("batch")
    batch_rows, points, channels = inputs.shape
    narrow = channels // (seq_count * batch_count)
    local_outer = spectrum.shape[1]
    outer = 2 * seq_count
    tiled = narrow % sub == 0 and points % lane == 0 and batch_rows == 1
    twist = jnp.asarray(twist_table(outer, points))
    ahead, back = point_matrices(points, 1.0 / (outer * points))
    ahead, back = jnp.asarray(high_low(ahead)), jnp.asarray(high_low(back))

    pack = pack_call if tiled else pack_plain
    packed = jnp.stack([pack(inputs[row], grad_out[row], narrow) for row in range(batch_rows)], axis=1)
    arrived = lax.all_to_all(packed, ("batch", "seq"), split_axis=0, concat_axis=0, tiled=True)
    arrived = arrived.reshape(batch_count, seq_count, batch_rows, 2 * narrow, points)
    arrived = arrived.transpose(0, 2, 1, 3, 4).reshape(-1, seq_count, 2 * narrow, points)
    sequences = arrived.shape[0]

    grad, spectra = (forward_call if tiled else forward_plain)(arrived, twist, ahead)
    grad = grad.reshape(seq_count, local_outer, 2, narrow, points)
    sent = lax.all_to_all(grad, "seq", split_axis=0, concat_axis=0, tiled=True)

    residues = lax.axis_index("seq") * local_outer + jnp.arange(local_outer, dtype=jnp.int32)
    flips = (residues > seq_count).astype(jnp.int32)
    states = (spectrum, first_moment, second_moment)
    filters = (filter_call if tiled else filter_plain)(flips, sent, *states)
    filters = lax.all_to_all(filters, "seq", split_axis=0, concat_axis=0, tiled=True)
    new_spectrum, new_first, new_second = (update_call if tiled else update_plain)(flips, sent, *states)
    filters = filters.reshape(outer, 2, narrow, points)

    rows = (inverse_call if tiled else inverse_plain)(spectra, filters, twist, back)
    rows = rows.reshape(batch_count, batch_rows, seq_count, narrow, points).transpose(0, 2, 1, 3, 4)
    rows = rows.reshape(batch_count * seq_count, batch_rows, narrow, points)
    rows = lax.all_to_all(rows, ("batch", "seq"), split_axis=0, concat_axis=0, tiled=True)
    if tiled:
        filtered = unpack_call(rows.reshape(channels, points))[None]
    else:
        filtered = rows.transpose(1, 3, 0, 2).reshape(batch_rows, points, channels)
    return new_spectrum, new_first, new_second, filtered


def solution(mesh):
    return jax.shard_map(
        per_device,
        mesh=mesh,
        in_specs=(
            P("batch", "seq", None),
            P("batch", "seq", None),
            P(None, "seq", None, "batch"),
            P(None, "seq", None, "batch"),
            P(None, "seq", None, "batch"),
        ),
        out_specs=(
            P(None, "seq", None, "batch"),
            P(None, "seq", None, "batch"),
            P(None, "seq", None, "batch"),
            P("batch", "seq", None),
        ),
        check_vma=False,
    )
```

```python
import functools
import math

import jax
import jax.numpy as jnp
import numpy as np
from jax import lax
from jax.experimental import pallas as pl
from jax.experimental.pallas import tpu as pltpu
from jax.sharding import PartitionSpec as P

step_rate = 0.5
epsilon = 1e-06
sub = 16
lane = 128


def turn_table(numer, modulus):
    phase = 2.0 * math.pi * (numer % modulus) / modulus
    return np.cos(phase), np.sin(phase)


def twist_table(outer, points):
    half = outer // 2
    index = np.arange(half + 1)[:, None] * np.arange(points)[None, :]
    cos, sin = turn_table(index, outer * points)
    return np.stack([cos, sin], axis=1).astype(np.float32)


def point_matrices(points, scale_back):
    index = np.arange(points)[:, None] * np.arange(points)[None, :]
    cos, sin = turn_table(index, points)
    ahead = np.block([[cos, -sin], [sin, cos]])
    back = np.block([[cos, sin], [-sin, cos]]) * scale_back
    return ahead.astype(np.float32), back.astype(np.float32)


def times_phase(re, im, turns, count):
    if turns == 0:
        return re, im
    if 4 * turns == count:
        return im, -re
    cos = math.cos(2.0 * math.pi * turns / count)
    sin = math.sin(2.0 * math.pi * turns / count)
    return re * cos + im * sin, im * cos - re * sin


def half_spectrum(values):
    total = 2 * len(values)
    if total == 2:
        return [(values[0], None), (values[0], None)]
    even = half_spectrum(values[0::2])
    odd = half_spectrum(values[1::2])
    quarter = total // 4
    out = [None] * (total // 2 + 1)
    for index in range(quarter + 1):
        even_re, even_im = even[index]
        odd_re, odd_im = odd[index]
        if index == 0:
            out[0] = (even_re + odd_re, None)
            out[total // 2] = (even_re - odd_re, None)
        elif index == quarter:
            out[index] = (even_re, -odd_re)
        else:
            turned_re, turned_im = times_phase(odd_re, odd_im, index, total)
            out[index] = (even_re + turned_re, even_im + turned_im)
            out[total // 2 - index] = (even_re - turned_re, turned_im - even_im)
    return out


def real_segments(bins):
    count = 2 * (len(bins) - 1)
    if count == 2:
        return [bins[0][0] + bins[1][0]]
    quarter = count // 4
    even = [None] * (quarter + 1)
    odd = [None] * (quarter + 1)
    for index in range(quarter + 1):
        low_re, low_im = bins[index]
        high_re, high_im = bins[count // 2 - index]
        if index == 0:
            even[0] = (low_re + high_re, None)
            odd[0] = (low_re - high_re, None)
        elif index == quarter:
            even[index] = (low_re, None)
            odd[index] = (-low_im, None)
        else:
            even[index] = (low_re + high_re, low_im - high_im)
            diff_re, diff_im = low_re - high_re, low_im + high_im
            cos = math.cos(2.0 * math.pi * index / count)
            sin = math.sin(2.0 * math.pi * index / count)
            odd[index] = (diff_re * cos - diff_im * sin, diff_re * sin + diff_im * cos)
    first = real_segments(even)
    second = real_segments(odd)
    return [item for pair in zip(first, second) for item in pair]


both_last = (((1,), (1,)), ((), ()))
both_first = (((0,), (0,)), ((), ()))


def square_eye(points, flipped):
    row = lax.broadcasted_iota(jnp.int32, (points, points), 0)
    col = lax.broadcasted_iota(jnp.int32, (points, points), 1)
    picked = jnp.where(flipped, points - 1 - col, col)
    return jnp.where(row == picked, 1.0, 0.0).astype(jnp.bfloat16)


whole = pl.BlockSpec(memory_space=pltpu.VMEM)
roomy = pltpu.CompilerParams(vmem_limit_bytes=24 << 20)


def pack_kernel(signal_ref, cotangent_ref, out_ref, *, narrow, width):
    points, channels = signal_ref.shape
    for part, source in enumerate((signal_ref, cotangent_ref)):
        for left in range(0, channels, width):
            turned = source[:, left : left + width].T.reshape(width // narrow, narrow, points)
            first = left // narrow
            out_ref[first : first + width // narrow, part * narrow : (part + 1) * narrow, :] = turned


def pack_call(signal, cotangent, narrow):
    points, channels = signal.shape
    return pl.pallas_call(
        functools.partial(pack_kernel, narrow=narrow, width=math.gcd(channels, 256)),
        in_specs=[whole, whole],
        out_specs=whole,
        out_shape=jax.ShapeDtypeStruct((channels // narrow, 2 * narrow, points), jnp.bfloat16),
        compiler_params=roomy,
        name="pack",
    )(signal, cotangent)


def unpack_kernel(in_ref, out_ref):
    out_ref[...] = in_ref[...].T


def unpack_call(rows):
    channels, points = rows.shape
    width = math.gcd(channels, 512)
    return pl.pallas_call(
        unpack_kernel,
        grid=(channels // width,),
        in_specs=[pl.BlockSpec((width, points), lambda step: (step, 0))],
        out_specs=pl.BlockSpec((points, width), lambda step: (0, step)),
        out_shape=jax.ShapeDtypeStruct((points, channels), jnp.bfloat16),
        compiler_params=roomy,
        name="unpack",
    )(rows)


def over_chunks(emit, segments, chunk):
    emit(0, 1, False)
    emit(segments, 1, False)
    count = (segments - 1) // chunk

    def step(index, carry):
        emit(1 + index * chunk, chunk, True)
        return carry

    lax.fori_loop(0, count, step, 0)
    if (segments - 1) % chunk:
        emit(1 + count * chunk, (segments - 1) % chunk, True)


def split_dot(values, matrices):
    first = jnp.dot(values, matrices[0], preferred_element_type=jnp.float32)
    return first + jnp.dot(values, matrices[1], preferred_element_type=jnp.float32)


def forward_kernel(in_ref, twist_ref, matrix_ref, grad_ref, spectra_ref, mid_ref, *, scale, chunk):
    sequences, segments, pair_rows, points = in_ref.shape
    narrow = pair_rows // 2
    rows = sequences * narrow
    tiles = pair_rows // sub

    def tile_step(step, carry):
        which = step // tiles
        piece = step % tiles
        start = pl.multiple_of(piece * sub, sub)
        target = (piece // (tiles // 2)) * rows + which * narrow
        target = pl.multiple_of(target + (piece % (tiles // 2)) * sub, sub)
        for left in range(0, points, lane):
            here = slice(left, left + lane)
            after = slice(points + left, points + left + lane)
            values = [
                in_ref[which, seg, pl.ds(start, sub), here].astype(jnp.float32) for seg in range(segments)
            ]
            for index, (re, im) in enumerate(half_spectrum(values)):
                cos = twist_ref[index, 0:1, here]
                sin = twist_ref[index, 1:2, here]
                if im is None:
                    new_re, new_im = re * cos, -(re * sin)
                else:
                    new_re, new_im = re * cos + im * sin, im * cos - re * sin
                mid_ref[index, pl.ds(target, sub), here] = new_re.astype(jnp.bfloat16)
                mid_ref[index, pl.ds(target, sub), after] = new_im.astype(jnp.bfloat16)
        return carry

    lax.fori_loop(0, sequences * tiles, tile_step, 0)

    def emit(base, count, paired):
        values = mid_ref[pl.ds(base, count)].reshape(count * 2 * rows, 2 * points)
        full = split_dot(values, matrix_ref).reshape(count, 2 * rows, 2 * points)
        for extra in range(count):
            residue = base + extra
            signal_re, signal_im = full[extra, :rows, :points], full[extra, :rows, points:]
            cotan_re, cotan_im = full[extra, rows:, :points], full[extra, rows:, points:]
            spectra_ref[residue, 0] = signal_re
            spectra_ref[residue, 1] = signal_im
            real_term = signal_re * cotan_re + signal_im * cotan_im
            imag_term = signal_re * cotan_im - signal_im * cotan_re
            real_sum = jnp.sum(real_term.reshape(sequences, narrow, points), axis=0) * scale
            imag_sum = jnp.sum(imag_term.reshape(sequences, narrow, points), axis=0) * scale
            grad_ref[residue, 0] = real_sum.astype(jnp.bfloat16)
            grad_ref[residue, 1] = imag_sum.astype(jnp.bfloat16)
            if paired:
                grad_ref[2 * segments - residue, 0] = real_sum.astype(jnp.bfloat16)
                grad_ref[2 * segments - residue, 1] = (-imag_sum).astype(jnp.bfloat16)

    over_chunks(emit, segments, chunk)


def forward_call(arrived, twist, matrices):
    sequences, segments, pair_rows, points = arrived.shape
    narrow = pair_rows // 2
    outer = 2 * segments
    rows = sequences * narrow
    return pl.pallas_call(
        functools.partial(forward_kernel, scale=1.0 / (outer * points), chunk=5),
        in_specs=[whole, whole, whole],
        out_specs=[whole, whole],
        out_shape=[
            jax.ShapeDtypeStruct((outer, 2, narrow, points), jnp.bfloat16),
            jax.ShapeDtypeStruct((segments + 1, 2, rows, points), jnp.float32),
        ],
        scratch_shapes=[pltpu.VMEM((segments + 1, 2 * rows, 2 * points), jnp.bfloat16)],
        compiler_params=roomy,
        name="forward",
    )(arrived, twist, matrices)


def moved(grad, spec, first, second):
    new_first = 0.9 * first + 0.1 * grad
    new_second = 0.99 * second + 0.01 * grad * grad
    return spec - step_rate * jnp.tanh(new_first / (jnp.sqrt(new_second) + epsilon)), new_first, new_second


def is_mirrored(row, local_outer):
    return lax.axis_index("seq") * local_outer + row > lax.axis_size("seq")


def filter_kernel(grad_ref, spec_ref, first_ref, second_ref, out_ref):
    _, local_outer, points, width = spec_ref.shape
    for row in range(local_outer):
        eye = square_eye(points, is_mirrored(row, local_outer))
        for part in range(2):
            sent = grad_ref[:, row, part].reshape(width, points)
            grad = lax.dot_general(eye, sent, both_last, preferred_element_type=jnp.float32)
            new_spec, _, _ = moved(grad, spec_ref[part, row], first_ref[part, row], second_ref[part, row])
            turned = lax.dot_general(
                new_spec.astype(jnp.bfloat16), eye, both_first, preferred_element_type=jnp.float32
            )
            out_ref[:, row, part] = turned.astype(jnp.bfloat16).reshape(grad_ref.shape[0], -1, points)


def filter_call(sent, spectrum, first_moment, second_moment):
    return pl.pallas_call(
        filter_kernel,
        in_specs=[whole, whole, whole, whole],
        out_specs=whole,
        out_shape=jax.ShapeDtypeStruct(sent.shape, jnp.bfloat16),
        compiler_params=roomy,
        name="filter",
    )(sent, spectrum, first_moment, second_moment)


def update_kernel(
    grad_ref, spec_ref, first_ref, second_ref, new_spec_ref, new_first_ref, new_second_ref
):
    points, width = spec_ref.shape[2:]
    eye = square_eye(points, is_mirrored(pl.program_id(0), pl.num_programs(0)))
    for part in range(2):
        sent = grad_ref[:, 0, part].reshape(width, points)
        grad = lax.dot_general(eye, sent, both_last, preferred_element_type=jnp.float32)
        new_spec, new_first, new_second = moved(
            grad, spec_ref[part, 0], first_ref[part, 0], second_ref[part, 0]
        )
        new_spec_ref[part, 0] = new_spec
        new_first_ref[part, 0] = new_first
        new_second_ref[part, 0] = new_second


def update_call(sent, spectrum, first_moment, second_moment):
    groups, local_outer, _, narrow, points = sent.shape
    channels = spectrum.shape[3]
    state = pl.BlockSpec((2, 1, points, channels), lambda row: (0, row, 0, 0))
    wire = pl.BlockSpec((groups, 1, 2, narrow, points), lambda row: (0, row, 0, 0, 0))
    return pl.pallas_call(
        update_kernel,
        grid=(local_outer,),
        in_specs=[wire, state, state, state],
        out_specs=[state, state, state],
        out_shape=[jax.ShapeDtypeStruct(spectrum.shape, jnp.float32)] * 3,
        compiler_params=roomy,
        name="update",
    )(sent, spectrum, first_moment, second_moment)


def inverse_kernel(spectra_ref, filter_ref, twist_ref, matrix_ref, out_ref, mid_ref, *, chunk):
    sequences, segments, narrow, points = out_ref.shape
    rows = sequences * narrow

    def mixed(residue, paired):
        filter_re = filter_ref[residue, 0].astype(jnp.float32)
        filter_im = filter_ref[residue, 1].astype(jnp.float32)
        if paired:
            filter_re = filter_re + filter_ref[2 * segments - residue, 0].astype(jnp.float32)
            filter_im = filter_im - filter_ref[2 * segments - residue, 1].astype(jnp.float32)
        signal_re = spectra_ref[residue, 0].reshape(sequences, narrow, points)
        signal_im = spectra_ref[residue, 1].reshape(sequences, narrow, points)
        mixed_re = (signal_re * filter_re - signal_im * filter_im).reshape(rows, points)
        mixed_im = (signal_re * filter_im + signal_im * filter_re).reshape(rows, points)
        return jnp.concatenate([mixed_re.astype(jnp.bfloat16), mixed_im.astype(jnp.bfloat16)], axis=1)

    def emit(base, count, paired):
        values = jnp.concatenate([mixed(base + extra, paired) for extra in range(count)], axis=0)
        full = split_dot(values, matrix_ref).reshape(count, rows, 2 * points)
        for extra in range(count):
            residue = base + extra
            cos = twist_ref[residue, 0:1]
            sin = twist_ref[residue, 1:2]
            mid_ref[residue, 0] = full[extra, :, :points] * cos - full[extra, :, points:] * sin
            mid_ref[residue, 1] = full[extra, :, :points] * sin + full[extra, :, points:] * cos

    over_chunks(emit, segments, chunk)
    tiles = narrow // sub

    def tile_step(step, carry):
        which = step // tiles
        start = pl.multiple_of((step % tiles) * sub, sub)
        source = pl.multiple_of(step * sub, sub)
        for left in range(0, points, lane):
            here = slice(left, left + lane)
            bins = [
                tuple(mid_ref[index, part, pl.ds(source, sub), here] for part in range(2))
                for index in range(segments + 1)
            ]
            for seg, value in enumerate(real_segments(bins)):
                out_ref[which, seg, pl.ds(start, sub), here] = value.astype(jnp.bfloat16)
        return carry

    lax.fori_loop(0, sequences * tiles, tile_step, 0)


def inverse_call(spectra, filters, twist, matrices):
    residues, _, rows, points = spectra.shape
    segments = residues - 1
    narrow = filters.shape[2]
    sequences = rows // narrow
    return pl.pallas_call(
        functools.partial(inverse_kernel, chunk=5),
        in_specs=[whole, whole, whole, whole],
        out_specs=whole,
        out_shape=jax.ShapeDtypeStruct((sequences, segments, narrow, points), jnp.bfloat16),
        scratch_shapes=[pltpu.VMEM((residues, 2, rows, points), jnp.float32)],
        compiler_params=roomy,
        name="inverse",
    )(spectra, filters, twist, matrices)


def pack_plain(signal, cotangent, narrow):
    points, channels = signal.shape
    both = jnp.stack([signal, cotangent]).reshape(2, points, channels // narrow, narrow)
    return both.transpose(2, 0, 3, 1).reshape(channels // narrow, 2 * narrow, points)


def forward_plain(arrived, twist, matrices):
    sequences, segments, pair_rows, points = arrived.shape
    narrow = pair_rows // 2
    rows = sequences * narrow
    parts = arrived.reshape(sequences, segments, 2, narrow, points).astype(jnp.float32)
    parts = parts.transpose(1, 2, 0, 3, 4).reshape(segments, 2 * rows, points)
    bins = half_spectrum([parts[seg] for seg in range(segments)])
    re = jnp.stack([item[0] for item in bins])
    im = jnp.stack([jnp.zeros_like(item[0]) if item[1] is None else item[1] for item in bins])
    cos, sin = twist[:, 0][:, None], twist[:, 1][:, None]
    mid = jnp.concatenate([re * cos + im * sin, im * cos - re * sin], axis=2).astype(jnp.bfloat16)
    full = split_dot(mid, matrices)
    signal_re, signal_im = full[:, :rows, :points], full[:, :rows, points:]
    cotan_re, cotan_im = full[:, rows:, :points], full[:, rows:, points:]
    shape = (segments + 1, sequences, narrow, points)
    scale = 1.0 / (2 * segments * points)
    real = jnp.sum((signal_re * cotan_re + signal_im * cotan_im).reshape(shape), axis=1) * scale
    imag = jnp.sum((signal_re * cotan_im - signal_im * cotan_re).reshape(shape), axis=1) * scale
    real = jnp.concatenate([real, real[1:segments][::-1]])
    imag = jnp.concatenate([imag, -imag[1:segments][::-1]])
    grad = jnp.stack([real, imag], axis=1).astype(jnp.bfloat16)
    return grad, jnp.stack([signal_re, signal_im], axis=1)


def mirrored_rows(local_outer):
    rows = jnp.arange(local_outer, dtype=jnp.int32)
    return is_mirrored(rows, local_outer)[None, :, None, None]


def gradient_plain(sent, shape):
    arrived = sent.astype(jnp.float32).transpose(2, 1, 4, 0, 3).reshape(shape)
    return jnp.where(mirrored_rows(shape[1]), arrived[:, :, ::-1], arrived)


def filter_plain(sent, spectrum, first_moment, second_moment):
    groups, local_outer, _, narrow, points = sent.shape
    grad = gradient_plain(sent, spectrum.shape)
    new_spec, _, _ = moved(grad, spectrum, first_moment, second_moment)
    out = jnp.where(mirrored_rows(local_outer), new_spec[:, :, ::-1], new_spec).astype(jnp.bfloat16)
    return out.reshape(2, local_outer, points, groups, narrow).transpose(3, 1, 0, 4, 2)


def update_plain(sent, spectrum, first_moment, second_moment):
    return moved(gradient_plain(sent, spectrum.shape), spectrum, first_moment, second_moment)


def inverse_plain(spectra, filters, twist, matrices):
    residues, _, rows, points = spectra.shape
    segments = residues - 1
    narrow = filters.shape[2]
    sequences = rows // narrow
    wide = filters.astype(jnp.float32)
    mirrored = jnp.concatenate([jnp.zeros_like(wide[:1]), wide[segments + 1 :][::-1], jnp.zeros_like(wide[:1])])
    filter_re = (wide[: segments + 1, 0] + mirrored[:, 0])[:, None]
    filter_im = (wide[: segments + 1, 1] - mirrored[:, 1])[:, None]
    shape = (residues, sequences, narrow, points)
    signal_re, signal_im = spectra[:, 0].reshape(shape), spectra[:, 1].reshape(shape)
    mixed_re = (signal_re * filter_re - signal_im * filter_im).reshape(residues, rows, points)
    mixed_im = (signal_re * filter_im + signal_im * filter_re).reshape(residues, rows, points)
    full = split_dot(jnp.concatenate([mixed_re, mixed_im], axis=2).astype(jnp.bfloat16), matrices)
    cos, sin = twist[:, 0][:, None], twist[:, 1][:, None]
    mid_re = full[..., :points] * cos - full[..., points:] * sin
    mid_im = full[..., :points] * sin + full[..., points:] * cos
    out = jnp.stack(real_segments([(mid_re[index], mid_im[index]) for index in range(residues)]))
    out = out.reshape(segments, sequences, narrow, points).transpose(1, 0, 2, 3)
    return out.astype(jnp.bfloat16)


def high_low(matrix):
    high = matrix.astype(jnp.bfloat16)
    low = (matrix - high.astype(np.float32)).astype(jnp.bfloat16)
    return np.stack([high, low])


def per_device(inputs, grad_out, spectrum, first_moment, second_moment):
    seq_count = lax.axis_size("seq")
    batch_count = lax.axis_size("batch")
    batch_rows, points, channels = inputs.shape
    narrow = channels // (seq_count * batch_count)
    local_outer = spectrum.shape[1]
    outer = 2 * seq_count
    tiled = narrow % sub == 0 and points % lane == 0 and batch_rows == 1
    twist = jnp.asarray(twist_table(outer, points))
    ahead, back = point_matrices(points, 1.0 / (outer * points))
    ahead, back = jnp.asarray(high_low(ahead)), jnp.asarray(high_low(back))

    pack = pack_call if tiled else pack_plain
    packed = jnp.stack([pack(inputs[row], grad_out[row], narrow) for row in range(batch_rows)], axis=1)
    arrived = lax.all_to_all(packed, ("batch", "seq"), split_axis=0, concat_axis=0, tiled=True)
    arrived = arrived.reshape(batch_count, seq_count, batch_rows, 2 * narrow, points)
    arrived = arrived.transpose(0, 2, 1, 3, 4).reshape(-1, seq_count, 2 * narrow, points)
    sequences = arrived.shape[0]

    grad, spectra = (forward_call if tiled else forward_plain)(arrived, twist, ahead)
    grad = grad.reshape(seq_count, local_outer, 2, narrow, points)
    sent = lax.all_to_all(grad, "seq", split_axis=0, concat_axis=0, tiled=True)

    states = (spectrum, first_moment, second_moment)
    filters = (filter_call if tiled else filter_plain)(sent, *states)
    filters = lax.all_to_all(filters, "seq", split_axis=0, concat_axis=0, tiled=True)
    new_spectrum, new_first, new_second = (update_call if tiled else update_plain)(sent, *states)
    filters = filters.reshape(outer, 2, narrow, points)

    rows = (inverse_call if tiled else inverse_plain)(spectra, filters, twist, back)
    rows = rows.reshape(batch_count, batch_rows, seq_count, narrow, points).transpose(0, 2, 1, 3, 4)
    rows = rows.reshape(batch_count * seq_count, batch_rows, narrow, points)
    rows = lax.all_to_all(rows, ("batch", "seq"), split_axis=0, concat_axis=0, tiled=True)
    if tiled:
        filtered = unpack_call(rows.reshape(channels, points))[None]
    else:
        filtered = rows.transpose(1, 3, 0, 2).reshape(batch_rows, points, channels)
    return new_spectrum, new_first, new_second, filtered


def solution(mesh):
    return jax.shard_map(
        per_device,
        mesh=mesh,
        in_specs=(
            P("batch", "seq", None),
            P("batch", "seq", None),
            P(None, "seq", None, "batch"),
            P(None, "seq", None, "batch"),
            P(None, "seq", None, "batch"),
        ),
        out_specs=(
            P(None, "seq", None, "batch"),
            P(None, "seq", None, "batch"),
            P(None, "seq", None, "batch"),
            P("batch", "seq", None),
        ),
        check_vma=False,
    )
```

```python
import functools
import math

import jax
import jax.numpy as jnp
import numpy as np
from jax import lax
from jax.experimental import pallas as pl
from jax.experimental.pallas import tpu as pltpu
from jax.sharding import PartitionSpec as P

step_rate = 0.5
epsilon = 1e-06
sub = 16
lane = 128


def turn_table(numer, modulus):
    phase = 2.0 * math.pi * (numer % modulus) / modulus
    return np.cos(phase), np.sin(phase)


def twist_table(outer, points):
    half = outer // 2
    index = np.arange(half + 1)[:, None] * np.arange(points)[None, :]
    cos, sin = turn_table(index, outer * points)
    return np.stack([cos, sin], axis=1).astype(np.float32)


def point_matrices(points, scale_back):
    index = np.arange(points)[:, None] * np.arange(points)[None, :]
    cos, sin = turn_table(index, points)
    ahead = np.block([[cos, -sin], [sin, cos]])
    back = np.block([[cos, sin], [-sin, cos]]) * scale_back
    return ahead.astype(np.float32), back.astype(np.float32)


def times_phase(re, im, turns, count):
    if turns == 0:
        return re, im
    if 4 * turns == count:
        return im, -re
    cos = math.cos(2.0 * math.pi * turns / count)
    sin = math.sin(2.0 * math.pi * turns / count)
    return re * cos + im * sin, im * cos - re * sin


def half_spectrum(values):
    total = 2 * len(values)
    if total == 2:
        return [(values[0], None), (values[0], None)]
    even = half_spectrum(values[0::2])
    odd = half_spectrum(values[1::2])
    quarter = total // 4
    out = [None] * (total // 2 + 1)
    for index in range(quarter + 1):
        even_re, even_im = even[index]
        odd_re, odd_im = odd[index]
        if index == 0:
            out[0] = (even_re + odd_re, None)
            out[total // 2] = (even_re - odd_re, None)
        elif index == quarter:
            out[index] = (even_re, -odd_re)
        else:
            turned_re, turned_im = times_phase(odd_re, odd_im, index, total)
            out[index] = (even_re + turned_re, even_im + turned_im)
            out[total // 2 - index] = (even_re - turned_re, turned_im - even_im)
    return out


def real_segments(bins):
    count = 2 * (len(bins) - 1)
    if count == 2:
        return [bins[0][0] + bins[1][0]]
    quarter = count // 4
    even = [None] * (quarter + 1)
    odd = [None] * (quarter + 1)
    for index in range(quarter + 1):
        low_re, low_im = bins[index]
        high_re, high_im = bins[count // 2 - index]
        if index == 0:
            even[0] = (low_re + high_re, None)
            odd[0] = (low_re - high_re, None)
        elif index == quarter:
            even[index] = (low_re, None)
            odd[index] = (-low_im, None)
        else:
            even[index] = (low_re + high_re, low_im - high_im)
            diff_re, diff_im = low_re - high_re, low_im + high_im
            cos = math.cos(2.0 * math.pi * index / count)
            sin = math.sin(2.0 * math.pi * index / count)
            odd[index] = (diff_re * cos - diff_im * sin, diff_re * sin + diff_im * cos)
    first = real_segments(even)
    second = real_segments(odd)
    return [item for pair in zip(first, second) for item in pair]


both_last = (((1,), (1,)), ((), ()))
both_first = (((0,), (0,)), ((), ()))


def square_eye(points, flipped):
    row = lax.broadcasted_iota(jnp.int32, (points, points), 0)
    col = lax.broadcasted_iota(jnp.int32, (points, points), 1)
    picked = jnp.where(flipped, points - 1 - col, col)
    return jnp.where(row == picked, 1.0, 0.0).astype(jnp.bfloat16)


whole = pl.BlockSpec(memory_space=pltpu.VMEM)
roomy = pltpu.CompilerParams(vmem_limit_bytes=24 << 20)


def pack_kernel(signal_ref, cotangent_ref, out_ref, *, narrow, width):
    points, channels = signal_ref.shape
    for part, source in enumerate((signal_ref, cotangent_ref)):
        for left in range(0, channels, width):
            turned = source[:, left : left + width].T.reshape(width // narrow, narrow, points)
            first = left // narrow
            out_ref[first : first + width // narrow, part * narrow : (part + 1) * narrow, :] = turned


def pack_call(signal, cotangent, narrow):
    points, channels = signal.shape
    return pl.pallas_call(
        functools.partial(pack_kernel, narrow=narrow, width=math.gcd(channels, 256)),
        in_specs=[whole, whole],
        out_specs=whole,
        out_shape=jax.ShapeDtypeStruct((channels // narrow, 2 * narrow, points), jnp.bfloat16),
        compiler_params=roomy,
        name="pack",
    )(signal, cotangent)


def unpack_kernel(in_ref, out_ref):
    out_ref[...] = in_ref[...].T


def unpack_call(rows):
    channels, points = rows.shape
    return pl.pallas_call(
        unpack_kernel,
        in_specs=[whole],
        out_specs=whole,
        out_shape=jax.ShapeDtypeStruct((points, channels), jnp.bfloat16),
        compiler_params=roomy,
        name="unpack",
    )(rows)


def over_chunks(emit, segments, chunk):
    emit(0, 1, False)
    emit(segments, 1, False)
    count = (segments - 1) // chunk

    def step(index, carry):
        emit(1 + index * chunk, chunk, True)
        return carry

    lax.fori_loop(0, count, step, 0)
    if (segments - 1) % chunk:
        emit(1 + count * chunk, (segments - 1) % chunk, True)


def forward_kernel(in_ref, twist_ref, matrix_ref, grad_ref, spectra_ref, mid_ref, *, scale, chunk):
    sequences, segments, pair_rows, points = in_ref.shape
    narrow = pair_rows // 2
    rows = sequences * narrow
    tiles = pair_rows // sub

    def tile_step(step, carry):
        which = step // tiles
        piece = step % tiles
        start = pl.multiple_of(piece * sub, sub)
        target = (piece // (tiles // 2)) * rows + which * narrow
        target = pl.multiple_of(target + (piece % (tiles // 2)) * sub, sub)
        for left in range(0, points, lane):
            here = slice(left, left + lane)
            after = slice(points + left, points + left + lane)
            values = [
                in_ref[which, seg, pl.ds(start, sub), here].astype(jnp.float32) for seg in range(segments)
            ]
            for index, (re, im) in enumerate(half_spectrum(values)):
                cos = twist_ref[index, 0:1, here]
                sin = twist_ref[index, 1:2, here]
                if im is None:
                    new_re, new_im = re * cos, -(re * sin)
                else:
                    new_re, new_im = re * cos + im * sin, im * cos - re * sin
                mid_ref[index, pl.ds(target, sub), here] = new_re.astype(jnp.bfloat16)
                mid_ref[index, pl.ds(target, sub), after] = new_im.astype(jnp.bfloat16)
        return carry

    lax.fori_loop(0, sequences * tiles, tile_step, 0)

    def emit(base, count, paired):
        values = mid_ref[pl.ds(base, count)].reshape(count * 2 * rows, 2 * points)
        full = jnp.dot(values, matrix_ref[...], preferred_element_type=jnp.float32).reshape(count, 2 * rows, 2 * points)
        for extra in range(count):
            residue = base + extra
            signal_re, signal_im = full[extra, :rows, :points], full[extra, :rows, points:]
            cotan_re, cotan_im = full[extra, rows:, :points], full[extra, rows:, points:]
            spectra_ref[residue, 0] = signal_re
            spectra_ref[residue, 1] = signal_im
            real_term = signal_re * cotan_re + signal_im * cotan_im
            imag_term = signal_re * cotan_im - signal_im * cotan_re
            real_sum = jnp.sum(real_term.reshape(sequences, narrow, points), axis=0) * scale
            imag_sum = jnp.sum(imag_term.reshape(sequences, narrow, points), axis=0) * scale
            grad_ref[residue, 0] = real_sum.astype(jnp.bfloat16)
            grad_ref[residue, 1] = imag_sum.astype(jnp.bfloat16)
            if paired:
                grad_ref[2 * segments - residue, 0] = real_sum.astype(jnp.bfloat16)
                grad_ref[2 * segments - residue, 1] = (-imag_sum).astype(jnp.bfloat16)

    over_chunks(emit, segments, chunk)


def forward_call(arrived, twist, matrices):
    sequences, segments, pair_rows, points = arrived.shape
    narrow = pair_rows // 2
    outer = 2 * segments
    rows = sequences * narrow
    return pl.pallas_call(
        functools.partial(forward_kernel, scale=1.0 / (outer * points), chunk=8),
        in_specs=[whole, whole, whole],
        out_specs=[whole, whole],
        out_shape=[
            jax.ShapeDtypeStruct((outer, 2, narrow, points), jnp.bfloat16),
            jax.ShapeDtypeStruct((segments + 1, 2, rows, points), jnp.float32),
        ],
        scratch_shapes=[pltpu.VMEM((segments + 1, 2 * rows, 2 * points), jnp.bfloat16)],
        compiler_params=roomy,
        name="forward",
    )(arrived, twist, matrices)


def moved(grad, spec, first, second):
    new_first = 0.9 * first + 0.1 * grad
    new_second = 0.99 * second + 0.01 * grad * grad
    return spec - step_rate * jnp.tanh(new_first / (jnp.sqrt(new_second) + epsilon)), new_first, new_second


def is_mirrored(row, local_outer):
    return lax.axis_index("seq") * local_outer + row > lax.axis_size("seq")


def update_kernel(
    grad_ref, spec_ref, first_ref, second_ref, new_spec_ref, new_first_ref, new_second_ref, out_ref
):
    _, local_outer, points, width = spec_ref.shape
    for row in range(local_outer):
        eye = square_eye(points, is_mirrored(row, local_outer))
        for part in range(2):
            sent = grad_ref[:, row, part].reshape(width, points)
            grad = lax.dot_general(eye, sent, both_last, preferred_element_type=jnp.float32)
            new_spec, new_first, new_second = moved(
                grad, spec_ref[part, row], first_ref[part, row], second_ref[part, row]
            )
            new_spec_ref[part, row] = new_spec
            new_first_ref[part, row] = new_first
            new_second_ref[part, row] = new_second
            turned = lax.dot_general(
                new_spec.astype(jnp.bfloat16), eye, both_first, preferred_element_type=jnp.float32
            )
            out_ref[:, row, part] = turned.astype(jnp.bfloat16).reshape(grad_ref.shape[0], -1, points)


def update_call(sent, spectrum, first_moment, second_moment):
    return pl.pallas_call(
        update_kernel,
        in_specs=[whole, whole, whole, whole],
        out_specs=[whole, whole, whole, whole],
        out_shape=[jax.ShapeDtypeStruct(spectrum.shape, jnp.float32)] * 3
        + [jax.ShapeDtypeStruct(sent.shape, jnp.bfloat16)],
        compiler_params=roomy,
        name="update",
    )(sent, spectrum, first_moment, second_moment)


def inverse_kernel(
    spectra_ref, filter_ref, twist_ref, matrix_ref, *refs, chunk
):
    held, out_ref, final, mid_ref, leaving = refs[:3], refs[3], refs[4:7], refs[7], refs[8]
    sequences, segments, narrow, points = out_ref.shape
    rows = sequences * narrow
    copies = [
        pltpu.make_async_copy(source, target, leaving.at[index])
        for index, (source, target) in enumerate(zip(held, final))
    ]
    for copy in copies:
        copy.start()

    def mixed(residue, paired):
        filter_re = filter_ref[residue, 0].astype(jnp.float32)
        filter_im = filter_ref[residue, 1].astype(jnp.float32)
        if paired:
            filter_re = filter_re + filter_ref[2 * segments - residue, 0].astype(jnp.float32)
            filter_im = filter_im - filter_ref[2 * segments - residue, 1].astype(jnp.float32)
        signal_re = spectra_ref[residue, 0].reshape(sequences, narrow, points)
        signal_im = spectra_ref[residue, 1].reshape(sequences, narrow, points)
        mixed_re = (signal_re * filter_re - signal_im * filter_im).reshape(rows, points)
        mixed_im = (signal_re * filter_im + signal_im * filter_re).reshape(rows, points)
        return jnp.concatenate([mixed_re.astype(jnp.bfloat16), mixed_im.astype(jnp.bfloat16)], axis=1)

    def emit(base, count, paired):
        values = jnp.concatenate([mixed(base + extra, paired) for extra in range(count)], axis=0)
        full = jnp.dot(values, matrix_ref[...], preferred_element_type=jnp.float32).reshape(count, rows, 2 * points)
        for extra in range(count):
            residue = base + extra
            cos = twist_ref[residue, 0:1]
            sin = twist_ref[residue, 1:2]
            mid_ref[residue, 0] = full[extra, :, :points] * cos - full[extra, :, points:] * sin
            mid_ref[residue, 1] = full[extra, :, :points] * sin + full[extra, :, points:] * cos

    over_chunks(emit, segments, chunk)
    tiles = narrow // sub

    def tile_step(step, carry):
        which = step // tiles
        start = pl.multiple_of((step % tiles) * sub, sub)
        source = pl.multiple_of(step * sub, sub)
        for left in range(0, points, lane):
            here = slice(left, left + lane)
            bins = [
                tuple(mid_ref[index, part, pl.ds(source, sub), here] for part in range(2))
                for index in range(segments + 1)
            ]
            for seg, value in enumerate(real_segments(bins)):
                out_ref[which, seg, pl.ds(start, sub), here] = value.astype(jnp.bfloat16)
        return carry

    lax.fori_loop(0, sequences * tiles, tile_step, 0)
    for copy in copies:
        copy.wait()


def inverse_call(spectra, filters, twist, matrices, states):
    residues, _, rows, points = spectra.shape
    segments = residues - 1
    narrow = filters.shape[2]
    sequences = rows // narrow
    out, *states = pl.pallas_call(
        functools.partial(inverse_kernel, chunk=8),
        in_specs=[whole] * 7,
        out_specs=[whole] + [pl.BlockSpec(memory_space=pl.ANY)] * 3,
        out_shape=[jax.ShapeDtypeStruct((sequences, segments, narrow, points), jnp.bfloat16)]
        + [jax.ShapeDtypeStruct(state.shape, state.dtype) for state in states],
        scratch_shapes=[
            pltpu.VMEM((residues, 2, rows, points), jnp.float32),
            pltpu.SemaphoreType.DMA((3,)),
        ],
        compiler_params=roomy,
        name="inverse",
    )(spectra, filters, twist, matrices, *states)
    return out, states


def pack_plain(signal, cotangent, narrow):
    points, channels = signal.shape
    both = jnp.stack([signal, cotangent]).reshape(2, points, channels // narrow, narrow)
    return both.transpose(2, 0, 3, 1).reshape(channels // narrow, 2 * narrow, points)


def forward_plain(arrived, twist, matrices):
    sequences, segments, pair_rows, points = arrived.shape
    narrow = pair_rows // 2
    rows = sequences * narrow
    parts = arrived.reshape(sequences, segments, 2, narrow, points).astype(jnp.float32)
    parts = parts.transpose(1, 2, 0, 3, 4).reshape(segments, 2 * rows, points)
    bins = half_spectrum([parts[seg] for seg in range(segments)])
    re = jnp.stack([item[0] for item in bins])
    im = jnp.stack([jnp.zeros_like(item[0]) if item[1] is None else item[1] for item in bins])
    cos, sin = twist[:, 0][:, None], twist[:, 1][:, None]
    mid = jnp.concatenate([re * cos + im * sin, im * cos - re * sin], axis=2).astype(jnp.bfloat16)
    full = jnp.dot(mid, matrices, preferred_element_type=jnp.float32)
    signal_re, signal_im = full[:, :rows, :points], full[:, :rows, points:]
    cotan_re, cotan_im = full[:, rows:, :points], full[:, rows:, points:]
    shape = (segments + 1, sequences, narrow, points)
    scale = 1.0 / (2 * segments * points)
    real = jnp.sum((signal_re * cotan_re + signal_im * cotan_im).reshape(shape), axis=1) * scale
    imag = jnp.sum((signal_re * cotan_im - signal_im * cotan_re).reshape(shape), axis=1) * scale
    real = jnp.concatenate([real, real[1:segments][::-1]])
    imag = jnp.concatenate([imag, -imag[1:segments][::-1]])
    grad = jnp.stack([real, imag], axis=1).astype(jnp.bfloat16)
    return grad, jnp.stack([signal_re, signal_im], axis=1)


def mirrored_rows(local_outer):
    rows = jnp.arange(local_outer, dtype=jnp.int32)
    return is_mirrored(rows, local_outer)[None, :, None, None]


def gradient_plain(sent, shape):
    arrived = sent.astype(jnp.float32).transpose(2, 1, 4, 0, 3).reshape(shape)
    return jnp.where(mirrored_rows(shape[1]), arrived[:, :, ::-1], arrived)


def update_plain(sent, spectrum, first_moment, second_moment):
    groups, local_outer, _, narrow, points = sent.shape
    grad = gradient_plain(sent, spectrum.shape)
    new_spec, new_first, new_second = moved(grad, spectrum, first_moment, second_moment)
    out = jnp.where(mirrored_rows(local_outer), new_spec[:, :, ::-1], new_spec).astype(jnp.bfloat16)
    out = out.reshape(2, local_outer, points, groups, narrow).transpose(3, 1, 0, 4, 2)
    return new_spec, new_first, new_second, out


def inverse_plain(spectra, filters, twist, matrices, states):
    residues, _, rows, points = spectra.shape
    segments = residues - 1
    narrow = filters.shape[2]
    sequences = rows // narrow
    wide = filters.astype(jnp.float32)
    mirrored = jnp.concatenate([jnp.zeros_like(wide[:1]), wide[segments + 1 :][::-1], jnp.zeros_like(wide[:1])])
    filter_re = (wide[: segments + 1, 0] + mirrored[:, 0])[:, None]
    filter_im = (wide[: segments + 1, 1] - mirrored[:, 1])[:, None]
    shape = (residues, sequences, narrow, points)
    signal_re, signal_im = spectra[:, 0].reshape(shape), spectra[:, 1].reshape(shape)
    mixed_re = (signal_re * filter_re - signal_im * filter_im).reshape(residues, rows, points)
    mixed_im = (signal_re * filter_im + signal_im * filter_re).reshape(residues, rows, points)
    mixed = jnp.concatenate([mixed_re, mixed_im], axis=2).astype(jnp.bfloat16)
    full = jnp.dot(mixed, matrices, preferred_element_type=jnp.float32)
    cos, sin = twist[:, 0][:, None], twist[:, 1][:, None]
    mid_re = full[..., :points] * cos - full[..., points:] * sin
    mid_im = full[..., :points] * sin + full[..., points:] * cos
    out = jnp.stack(real_segments([(mid_re[index], mid_im[index]) for index in range(residues)]))
    out = out.reshape(segments, sequences, narrow, points).transpose(1, 0, 2, 3)
    return out.astype(jnp.bfloat16), states


def per_device(inputs, grad_out, spectrum, first_moment, second_moment):
    seq_count = lax.axis_size("seq")
    batch_count = lax.axis_size("batch")
    batch_rows, points, channels = inputs.shape
    narrow = channels // (seq_count * batch_count)
    local_outer = spectrum.shape[1]
    outer = 2 * seq_count
    tiled = narrow % sub == 0 and points % lane == 0 and batch_rows == 1
    twist = jnp.asarray(twist_table(outer, points))
    ahead, back = point_matrices(points, 1.0 / (outer * points))
    ahead, back = jnp.asarray(ahead, jnp.bfloat16), jnp.asarray(back, jnp.bfloat16)

    pack = pack_call if tiled else pack_plain
    packed = jnp.stack([pack(inputs[row], grad_out[row], narrow) for row in range(batch_rows)], axis=1)
    arrived = lax.all_to_all(packed, ("batch", "seq"), split_axis=0, concat_axis=0, tiled=True)
    arrived = arrived.reshape(batch_count, seq_count, batch_rows, 2 * narrow, points)
    arrived = arrived.transpose(0, 2, 1, 3, 4).reshape(-1, seq_count, 2 * narrow, points)
    sequences = arrived.shape[0]

    grad, spectra = (forward_call if tiled else forward_plain)(arrived, twist, ahead)
    grad = grad.reshape(seq_count, local_outer, 2, narrow, points)
    sent = lax.all_to_all(grad, "seq", split_axis=0, concat_axis=0, tiled=True)

    update = update_call if tiled else update_plain
    *states, filters = update(sent, spectrum, first_moment, second_moment)
    filters = lax.all_to_all(filters, "seq", split_axis=0, concat_axis=0, tiled=True)
    filters = filters.reshape(outer, 2, narrow, points)

    rows, states = (inverse_call if tiled else inverse_plain)(spectra, filters, twist, back, states)
    rows = rows.reshape(batch_count, batch_rows, seq_count, narrow, points).transpose(0, 2, 1, 3, 4)
    rows = rows.reshape(batch_count * seq_count, batch_rows, narrow, points)
    rows = lax.all_to_all(rows, ("batch", "seq"), split_axis=0, concat_axis=0, tiled=True)
    if tiled:
        filtered = unpack_call(rows.reshape(channels, points))[None]
    else:
        filtered = rows.transpose(1, 3, 0, 2).reshape(batch_rows, points, channels)
    return *states, filtered


def solution(mesh):
    return jax.shard_map(
        per_device,
        mesh=mesh,
        in_specs=(
            P("batch", "seq", None),
            P("batch", "seq", None),
            P(None, "seq", None, "batch"),
            P(None, "seq", None, "batch"),
            P(None, "seq", None, "batch"),
        ),
        out_specs=(
            P(None, "seq", None, "batch"),
            P(None, "seq", None, "batch"),
            P(None, "seq", None, "batch"),
            P("batch", "seq", None),
        ),
        check_vma=False,
    )
```

```python
import functools
import math

import jax
import jax.numpy as jnp
import numpy as np
from jax import lax
from jax.experimental import pallas as pl
from jax.experimental.pallas import tpu as pltpu
from jax.sharding import PartitionSpec as P

step_rate = 0.5
epsilon = 1e-06
sub = 16
lane = 128


def turn_table(numer, modulus):
    phase = 2.0 * math.pi * (numer % modulus) / modulus
    return np.cos(phase), np.sin(phase)


def twist_table(outer, points):
    half = outer // 2
    index = np.arange(half + 1)[:, None] * np.arange(points)[None, :]
    cos, sin = turn_table(index, outer * points)
    return np.stack([cos, sin], axis=1).astype(np.float32)


def point_matrices(points, scale_back):
    index = np.arange(points)[:, None] * np.arange(points)[None, :]
    cos, sin = turn_table(index, points)
    ahead = np.block([[cos, -sin], [sin, cos]])
    back = np.block([[cos, sin], [-sin, cos]]) * scale_back
    return ahead.astype(np.float32), back.astype(np.float32)


def times_phase(re, im, turns, count):
    if turns == 0:
        return re, im
    if 4 * turns == count:
        return im, -re
    cos = math.cos(2.0 * math.pi * turns / count)
    sin = math.sin(2.0 * math.pi * turns / count)
    return re * cos + im * sin, im * cos - re * sin


def half_spectrum(values):
    total = 2 * len(values)
    if total == 2:
        return [(values[0], None), (values[0], None)]
    even = half_spectrum(values[0::2])
    odd = half_spectrum(values[1::2])
    quarter = total // 4
    out = [None] * (total // 2 + 1)
    for index in range(quarter + 1):
        even_re, even_im = even[index]
        odd_re, odd_im = odd[index]
        if index == 0:
            out[0] = (even_re + odd_re, None)
            out[total // 2] = (even_re - odd_re, None)
        elif index == quarter:
            out[index] = (even_re, -odd_re)
        else:
            turned_re, turned_im = times_phase(odd_re, odd_im, index, total)
            out[index] = (even_re + turned_re, even_im + turned_im)
            out[total // 2 - index] = (even_re - turned_re, turned_im - even_im)
    return out


def real_segments(bins):
    count = 2 * (len(bins) - 1)
    if count == 2:
        return [bins[0][0] + bins[1][0]]
    quarter = count // 4
    even = [None] * (quarter + 1)
    odd = [None] * (quarter + 1)
    for index in range(quarter + 1):
        low_re, low_im = bins[index]
        high_re, high_im = bins[count // 2 - index]
        if index == 0:
            even[0] = (low_re + high_re, None)
            odd[0] = (low_re - high_re, None)
        elif index == quarter:
            even[index] = (low_re, None)
            odd[index] = (-low_im, None)
        else:
            even[index] = (low_re + high_re, low_im - high_im)
            diff_re, diff_im = low_re - high_re, low_im + high_im
            cos = math.cos(2.0 * math.pi * index / count)
            sin = math.sin(2.0 * math.pi * index / count)
            odd[index] = (diff_re * cos - diff_im * sin, diff_re * sin + diff_im * cos)
    first = real_segments(even)
    second = real_segments(odd)
    return [item for pair in zip(first, second) for item in pair]


both_last = (((1,), (1,)), ((), ()))
both_first = (((0,), (0,)), ((), ()))


def square_eye(points, flipped):
    row = lax.broadcasted_iota(jnp.int32, (points, points), 0)
    col = lax.broadcasted_iota(jnp.int32, (points, points), 1)
    picked = jnp.where(flipped, points - 1 - col, col)
    return jnp.where(row == picked, 1.0, 0.0).astype(jnp.bfloat16)


whole = pl.BlockSpec(memory_space=pltpu.VMEM)
roomy = pltpu.CompilerParams(vmem_limit_bytes=24 << 20)


def pack_kernel(signal_hbm, cotangent_hbm, out_ref, held_ref, arrival, *, narrow):
    blocks, points, width = held_ref.shape[1:]
    each = width // narrow
    copies = [
        [
            pltpu.make_async_copy(
                source.at[:, block * width : (block + 1) * width],
                held_ref.at[part, block],
                arrival.at[part, block],
            )
            for part, source in enumerate((signal_hbm, cotangent_hbm))
        ]
        for block in range(blocks)
    ]
    for pair in copies:
        for copy in pair:
            copy.start()
    for block, pair in enumerate(copies):
        for part, copy in enumerate(pair):
            copy.wait()
            turned = held_ref[part, block].T.reshape(each, narrow, points)
            out_ref[block * each : (block + 1) * each, part * narrow : (part + 1) * narrow, :] = turned


def pack_call(signal, cotangent, narrow):
    points, channels = signal.shape
    width = math.gcd(channels, 1024)
    blocks = channels // width
    signal = pltpu.with_memory_space_constraint(signal, pltpu.HBM)
    cotangent = pltpu.with_memory_space_constraint(cotangent, pltpu.HBM)
    return pl.pallas_call(
        functools.partial(pack_kernel, narrow=narrow),
        in_specs=[pl.BlockSpec(memory_space=pltpu.HBM)] * 2,
        out_specs=whole,
        out_shape=jax.ShapeDtypeStruct((channels // narrow, 2 * narrow, points), jnp.bfloat16),
        scratch_shapes=[
            pltpu.VMEM((2, blocks, points, width), jnp.bfloat16),
            pltpu.SemaphoreType.DMA((2, blocks)),
        ],
        compiler_params=roomy,
        name="pack",
    )(signal, cotangent)


def departures(held, final, leaving):
    return [
        pltpu.make_async_copy(source, target, leaving.at[index])
        for index, (source, target) in enumerate(zip(held, final))
    ]


def unpack_kernel(in_ref, held_ref, out_ref, final_ref, leaving):
    copies = departures([held_ref], [final_ref], leaving)
    copies[0].start()
    out_ref[...] = in_ref[...].T
    copies[0].wait()


def unpack_call(rows, state):
    channels, points = rows.shape
    return pl.pallas_call(
        unpack_kernel,
        in_specs=[whole, whole],
        out_specs=[whole, pl.BlockSpec(memory_space=pl.ANY)],
        out_shape=[
            jax.ShapeDtypeStruct((points, channels), jnp.bfloat16),
            jax.ShapeDtypeStruct(state.shape, state.dtype),
        ],
        scratch_shapes=[pltpu.SemaphoreType.DMA((1,))],
        compiler_params=roomy,
        name="unpack",
    )(rows, state)


def over_chunks(emit, segments, chunk):
    emit(0, 1, False)
    emit(segments, 1, False)
    count = (segments - 1) // chunk

    def step(index, carry):
        emit(1 + index * chunk, chunk, True)
        return carry

    lax.fori_loop(0, count, step, 0)
    if (segments - 1) % chunk:
        emit(1 + count * chunk, (segments - 1) % chunk, True)


def forward_kernel(in_ref, twist_ref, matrix_ref, grad_ref, spectra_ref, mid_ref, *, scale, chunk):
    sequences, segments, pair_rows, points = in_ref.shape
    narrow = pair_rows // 2
    rows = sequences * narrow
    tiles = pair_rows // sub

    def tile_step(step, carry):
        which = step // tiles
        piece = step % tiles
        start = pl.multiple_of(piece * sub, sub)
        target = (piece // (tiles // 2)) * rows + which * narrow
        target = pl.multiple_of(target + (piece % (tiles // 2)) * sub, sub)
        for left in range(0, points, lane):
            here = slice(left, left + lane)
            after = slice(points + left, points + left + lane)
            values = [
                in_ref[which, seg, pl.ds(start, sub), here].astype(jnp.float32) for seg in range(segments)
            ]
            for index, (re, im) in enumerate(half_spectrum(values)):
                cos = twist_ref[index, 0:1, here]
                sin = twist_ref[index, 1:2, here]
                if im is None:
                    new_re, new_im = re * cos, -(re * sin)
                else:
                    new_re, new_im = re * cos + im * sin, im * cos - re * sin
                mid_ref[index, pl.ds(target, sub), here] = new_re.astype(jnp.bfloat16)
                mid_ref[index, pl.ds(target, sub), after] = new_im.astype(jnp.bfloat16)
        return carry

    lax.fori_loop(0, sequences * tiles, tile_step, 0)

    def emit(base, count, paired):
        values = mid_ref[pl.ds(base, count)].reshape(count * 2 * rows, 2 * points)
        full = jnp.dot(values, matrix_ref[...], preferred_element_type=jnp.float32).reshape(count, 2 * rows, 2 * points)
        for extra in range(count):
            residue = base + extra
            signal_re, signal_im = full[extra, :rows, :points], full[extra, :rows, points:]
            cotan_re, cotan_im = full[extra, rows:, :points], full[extra, rows:, points:]
            spectra_ref[residue, 0] = signal_re
            spectra_ref[residue, 1] = signal_im
            real_term = signal_re * cotan_re + signal_im * cotan_im
            imag_term = signal_re * cotan_im - signal_im * cotan_re
            real_sum = jnp.sum(real_term.reshape(sequences, narrow, points), axis=0) * scale
            imag_sum = jnp.sum(imag_term.reshape(sequences, narrow, points), axis=0) * scale
            grad_ref[residue, 0] = real_sum.astype(jnp.bfloat16)
            grad_ref[residue, 1] = imag_sum.astype(jnp.bfloat16)
            if paired:
                grad_ref[2 * segments - residue, 0] = real_sum.astype(jnp.bfloat16)
                grad_ref[2 * segments - residue, 1] = (-imag_sum).astype(jnp.bfloat16)

    over_chunks(emit, segments, chunk)


def forward_call(arrived, twist, matrices):
    sequences, segments, pair_rows, points = arrived.shape
    narrow = pair_rows // 2
    outer = 2 * segments
    rows = sequences * narrow
    return pl.pallas_call(
        functools.partial(forward_kernel, scale=1.0 / (outer * points), chunk=8),
        in_specs=[whole, whole, whole],
        out_specs=[whole, whole],
        out_shape=[
            jax.ShapeDtypeStruct((outer, 2, narrow, points), jnp.bfloat16),
            jax.ShapeDtypeStruct((segments + 1, 2, rows, points), jnp.float32),
        ],
        scratch_shapes=[pltpu.VMEM((segments + 1, 2 * rows, 2 * points), jnp.bfloat16)],
        compiler_params=roomy,
        name="forward",
    )(arrived, twist, matrices)


def moved(grad, spec, first, second):
    new_first = 0.9 * first + 0.1 * grad
    new_second = 0.99 * second + 0.01 * grad * grad
    return spec - step_rate * jnp.tanh(new_first / (jnp.sqrt(new_second) + epsilon)), new_first, new_second


def is_mirrored(row, local_outer):
    return lax.axis_index("seq") * local_outer + row > lax.axis_size("seq")


def update_kernel(
    grad_ref, spec_ref, first_ref, second_ref, new_spec_ref, new_first_ref, new_second_ref, out_ref
):
    _, local_outer, points, width = spec_ref.shape
    for row in range(local_outer):
        eye = square_eye(points, is_mirrored(row, local_outer))
        for part in range(2):
            sent = grad_ref[:, row, part].reshape(width, points)
            grad = lax.dot_general(eye, sent, both_last, preferred_element_type=jnp.float32)
            new_spec, new_first, new_second = moved(
                grad, spec_ref[part, row], first_ref[part, row], second_ref[part, row]
            )
            new_spec_ref[part, row] = new_spec
            new_first_ref[part, row] = new_first
            new_second_ref[part, row] = new_second
            turned = lax.dot_general(
                new_spec.astype(jnp.bfloat16), eye, both_first, preferred_element_type=jnp.float32
            )
            out_ref[:, row, part] = turned.astype(jnp.bfloat16).reshape(grad_ref.shape[0], -1, points)


def update_call(sent, spectrum, first_moment, second_moment):
    return pl.pallas_call(
        update_kernel,
        in_specs=[whole, whole, whole, whole],
        out_specs=[whole, whole, whole, whole],
        out_shape=[jax.ShapeDtypeStruct(spectrum.shape, jnp.float32)] * 3
        + [jax.ShapeDtypeStruct(sent.shape, jnp.bfloat16)],
        compiler_params=roomy,
        name="update",
    )(sent, spectrum, first_moment, second_moment)


def inverse_kernel(spectra_ref, filter_ref, twist_ref, matrix_ref, *refs, chunk):
    *moving, mid_ref, leaving = refs
    count = len(moving) // 2
    out_ref = moving[count]
    copies = departures(moving[:count], moving[count + 1 :], leaving)
    for copy in copies:
        copy.start()
    sequences, segments, narrow, points = out_ref.shape
    rows = sequences * narrow

    def mixed(residue, paired):
        filter_re = filter_ref[residue, 0].astype(jnp.float32)
        filter_im = filter_ref[residue, 1].astype(jnp.float32)
        if paired:
            filter_re = filter_re + filter_ref[2 * segments - residue, 0].astype(jnp.float32)
            filter_im = filter_im - filter_ref[2 * segments - residue, 1].astype(jnp.float32)
        signal_re = spectra_ref[residue, 0].reshape(sequences, narrow, points)
        signal_im = spectra_ref[residue, 1].reshape(sequences, narrow, points)
        mixed_re = (signal_re * filter_re - signal_im * filter_im).reshape(rows, points)
        mixed_im = (signal_re * filter_im + signal_im * filter_re).reshape(rows, points)
        return jnp.concatenate([mixed_re.astype(jnp.bfloat16), mixed_im.astype(jnp.bfloat16)], axis=1)

    def emit(base, count, paired):
        values = jnp.concatenate([mixed(base + extra, paired) for extra in range(count)], axis=0)
        full = jnp.dot(values, matrix_ref[...], preferred_element_type=jnp.float32).reshape(count, rows, 2 * points)
        for extra in range(count):
            residue = base + extra
            cos = twist_ref[residue, 0:1]
            sin = twist_ref[residue, 1:2]
            mid_ref[residue, 0] = full[extra, :, :points] * cos - full[extra, :, points:] * sin
            mid_ref[residue, 1] = full[extra, :, :points] * sin + full[extra, :, points:] * cos

    over_chunks(emit, segments, chunk)
    tiles = narrow // sub

    def tile_step(step, carry):
        which = step // tiles
        start = pl.multiple_of((step % tiles) * sub, sub)
        source = pl.multiple_of(step * sub, sub)
        for left in range(0, points, lane):
            here = slice(left, left + lane)
            bins = [
                tuple(mid_ref[index, part, pl.ds(source, sub), here] for part in range(2))
                for index in range(segments + 1)
            ]
            for seg, value in enumerate(real_segments(bins)):
                out_ref[which, seg, pl.ds(start, sub), here] = value.astype(jnp.bfloat16)
        return carry

    lax.fori_loop(0, sequences * tiles, tile_step, 0)
    for copy in copies:
        copy.wait()


def inverse_call(spectra, filters, twist, matrices, states):
    residues, _, rows, points = spectra.shape
    segments = residues - 1
    narrow = filters.shape[2]
    sequences = rows // narrow
    out, *states = pl.pallas_call(
        functools.partial(inverse_kernel, chunk=8),
        in_specs=[whole] * (4 + len(states)),
        out_specs=[whole] + [pl.BlockSpec(memory_space=pl.ANY)] * len(states),
        out_shape=[jax.ShapeDtypeStruct((sequences, segments, narrow, points), jnp.bfloat16)]
        + [jax.ShapeDtypeStruct(state.shape, state.dtype) for state in states],
        scratch_shapes=[
            pltpu.VMEM((residues, 2, rows, points), jnp.float32),
            pltpu.SemaphoreType.DMA((len(states),)),
        ],
        compiler_params=roomy,
        name="inverse",
    )(spectra, filters, twist, matrices, *states)
    return out, states


def pack_plain(signal, cotangent, narrow):
    points, channels = signal.shape
    both = jnp.stack([signal, cotangent]).reshape(2, points, channels // narrow, narrow)
    return both.transpose(2, 0, 3, 1).reshape(channels // narrow, 2 * narrow, points)


def forward_plain(arrived, twist, matrices):
    sequences, segments, pair_rows, points = arrived.shape
    narrow = pair_rows // 2
    rows = sequences * narrow
    parts = arrived.reshape(sequences, segments, 2, narrow, points).astype(jnp.float32)
    parts = parts.transpose(1, 2, 0, 3, 4).reshape(segments, 2 * rows, points)
    bins = half_spectrum([parts[seg] for seg in range(segments)])
    re = jnp.stack([item[0] for item in bins])
    im = jnp.stack([jnp.zeros_like(item[0]) if item[1] is None else item[1] for item in bins])
    cos, sin = twist[:, 0][:, None], twist[:, 1][:, None]
    mid = jnp.concatenate([re * cos + im * sin, im * cos - re * sin], axis=2).astype(jnp.bfloat16)
    full = jnp.dot(mid, matrices, preferred_element_type=jnp.float32)
    signal_re, signal_im = full[:, :rows, :points], full[:, :rows, points:]
    cotan_re, cotan_im = full[:, rows:, :points], full[:, rows:, points:]
    shape = (segments + 1, sequences, narrow, points)
    scale = 1.0 / (2 * segments * points)
    real = jnp.sum((signal_re * cotan_re + signal_im * cotan_im).reshape(shape), axis=1) * scale
    imag = jnp.sum((signal_re * cotan_im - signal_im * cotan_re).reshape(shape), axis=1) * scale
    real = jnp.concatenate([real, real[1:segments][::-1]])
    imag = jnp.concatenate([imag, -imag[1:segments][::-1]])
    grad = jnp.stack([real, imag], axis=1).astype(jnp.bfloat16)
    return grad, jnp.stack([signal_re, signal_im], axis=1)


def mirrored_rows(local_outer):
    rows = jnp.arange(local_outer, dtype=jnp.int32)
    return is_mirrored(rows, local_outer)[None, :, None, None]


def gradient_plain(sent, shape):
    arrived = sent.astype(jnp.float32).transpose(2, 1, 4, 0, 3).reshape(shape)
    return jnp.where(mirrored_rows(shape[1]), arrived[:, :, ::-1], arrived)


def update_plain(sent, spectrum, first_moment, second_moment):
    groups, local_outer, _, narrow, points = sent.shape
    grad = gradient_plain(sent, spectrum.shape)
    new_spec, new_first, new_second = moved(grad, spectrum, first_moment, second_moment)
    out = jnp.where(mirrored_rows(local_outer), new_spec[:, :, ::-1], new_spec).astype(jnp.bfloat16)
    out = out.reshape(2, local_outer, points, groups, narrow).transpose(3, 1, 0, 4, 2)
    return new_spec, new_first, new_second, out


def inverse_plain(spectra, filters, twist, matrices, states):
    residues, _, rows, points = spectra.shape
    segments = residues - 1
    narrow = filters.shape[2]
    sequences = rows // narrow
    wide = filters.astype(jnp.float32)
    mirrored = jnp.concatenate([jnp.zeros_like(wide[:1]), wide[segments + 1 :][::-1], jnp.zeros_like(wide[:1])])
    filter_re = (wide[: segments + 1, 0] + mirrored[:, 0])[:, None]
    filter_im = (wide[: segments + 1, 1] - mirrored[:, 1])[:, None]
    shape = (residues, sequences, narrow, points)
    signal_re, signal_im = spectra[:, 0].reshape(shape), spectra[:, 1].reshape(shape)
    mixed_re = (signal_re * filter_re - signal_im * filter_im).reshape(residues, rows, points)
    mixed_im = (signal_re * filter_im + signal_im * filter_re).reshape(residues, rows, points)
    mixed = jnp.concatenate([mixed_re, mixed_im], axis=2).astype(jnp.bfloat16)
    full = jnp.dot(mixed, matrices, preferred_element_type=jnp.float32)
    cos, sin = twist[:, 0][:, None], twist[:, 1][:, None]
    mid_re = full[..., :points] * cos - full[..., points:] * sin
    mid_im = full[..., :points] * sin + full[..., points:] * cos
    out = jnp.stack(real_segments([(mid_re[index], mid_im[index]) for index in range(residues)]))
    out = out.reshape(segments, sequences, narrow, points).transpose(1, 0, 2, 3)
    return out.astype(jnp.bfloat16), states


def per_device(inputs, grad_out, spectrum, first_moment, second_moment):
    seq_count = lax.axis_size("seq")
    batch_count = lax.axis_size("batch")
    batch_rows, points, channels = inputs.shape
    narrow = channels // (seq_count * batch_count)
    local_outer = spectrum.shape[1]
    outer = 2 * seq_count
    tiled = narrow % sub == 0 and points % lane == 0 and batch_rows == 1
    twist = jnp.asarray(twist_table(outer, points))
    ahead, back = point_matrices(points, 1.0 / (outer * points))
    ahead, back = jnp.asarray(ahead, jnp.bfloat16), jnp.asarray(back, jnp.bfloat16)

    pack = pack_call if tiled else pack_plain
    packed = jnp.stack([pack(inputs[row], grad_out[row], narrow) for row in range(batch_rows)], axis=1)
    arrived = lax.all_to_all(packed, ("batch", "seq"), split_axis=0, concat_axis=0, tiled=True)
    arrived = arrived.reshape(batch_count, seq_count, batch_rows, 2 * narrow, points)
    arrived = arrived.transpose(0, 2, 1, 3, 4).reshape(-1, seq_count, 2 * narrow, points)
    sequences = arrived.shape[0]

    grad, spectra = (forward_call if tiled else forward_plain)(arrived, twist, ahead)
    grad = grad.reshape(seq_count, local_outer, 2, narrow, points)
    sent = lax.all_to_all(grad, "seq", split_axis=0, concat_axis=0, tiled=True)

    update = update_call if tiled else update_plain
    new_spectrum, new_first, new_second, filters = update(sent, spectrum, first_moment, second_moment)
    filters = lax.all_to_all(filters, "seq", split_axis=0, concat_axis=0, tiled=True)
    filters = filters.reshape(outer, 2, narrow, points)

    early = [new_spectrum, new_first]
    rows, early = (inverse_call if tiled else inverse_plain)(spectra, filters, twist, back, early)
    rows = rows.reshape(batch_count, batch_rows, seq_count, narrow, points).transpose(0, 2, 1, 3, 4)
    rows = rows.reshape(batch_count * seq_count, batch_rows, narrow, points)
    rows = lax.all_to_all(rows, ("batch", "seq"), split_axis=0, concat_axis=0, tiled=True)
    if tiled:
        filtered, new_second = unpack_call(rows.reshape(channels, points), new_second)
        filtered = filtered[None]
    else:
        filtered = rows.transpose(1, 3, 0, 2).reshape(batch_rows, points, channels)
    return *early, new_second, filtered


def solution(mesh):
    return jax.shard_map(
        per_device,
        mesh=mesh,
        in_specs=(
            P("batch", "seq", None),
            P("batch", "seq", None),
            P(None, "seq", None, "batch"),
            P(None, "seq", None, "batch"),
            P(None, "seq", None, "batch"),
        ),
        out_specs=(
            P(None, "seq", None, "batch"),
            P(None, "seq", None, "batch"),
            P(None, "seq", None, "batch"),
            P("batch", "seq", None),
        ),
        check_vma=False,
    )
```

```python
import functools
import math

import jax
import jax.numpy as jnp
import numpy as np
from jax import lax
from jax.experimental import pallas as pl
from jax.experimental.pallas import tpu as pltpu
from jax.sharding import PartitionSpec as P

step_rate = 0.5
epsilon = 1e-06
sub = 16
lane = 128


def turn_table(numer, modulus):
    phase = 2.0 * math.pi * (numer % modulus) / modulus
    return np.cos(phase), np.sin(phase)


def twist_table(outer, points):
    half = outer // 2
    index = np.arange(half + 1)[:, None] * np.arange(points)[None, :]
    cos, sin = turn_table(index, outer * points)
    return np.stack([cos, sin], axis=1).astype(np.float32)


def point_matrices(points, scale_back):
    index = np.arange(points)[:, None] * np.arange(points)[None, :]
    cos, sin = turn_table(index, points)
    ahead = np.block([[cos, -sin], [sin, cos]])
    back = np.block([[cos, sin], [-sin, cos]]) * scale_back
    return ahead.astype(np.float32), back.astype(np.float32)


def times_phase(re, im, turns, count):
    if turns == 0:
        return re, im
    if 4 * turns == count:
        return im, -re
    cos = math.cos(2.0 * math.pi * turns / count)
    sin = math.sin(2.0 * math.pi * turns / count)
    return re * cos + im * sin, im * cos - re * sin


def half_spectrum(values):
    total = 2 * len(values)
    if total == 2:
        return [(values[0], None), (values[0], None)]
    even = half_spectrum(values[0::2])
    odd = half_spectrum(values[1::2])
    quarter = total // 4
    out = [None] * (total // 2 + 1)
    for index in range(quarter + 1):
        even_re, even_im = even[index]
        odd_re, odd_im = odd[index]
        if index == 0:
            out[0] = (even_re + odd_re, None)
            out[total // 2] = (even_re - odd_re, None)
        elif index == quarter:
            out[index] = (even_re, -odd_re)
        else:
            turned_re, turned_im = times_phase(odd_re, odd_im, index, total)
            out[index] = (even_re + turned_re, even_im + turned_im)
            out[total // 2 - index] = (even_re - turned_re, turned_im - even_im)
    return out


def real_segments(bins):
    count = 2 * (len(bins) - 1)
    if count == 2:
        return [bins[0][0] + bins[1][0]]
    quarter = count // 4
    even = [None] * (quarter + 1)
    odd = [None] * (quarter + 1)
    for index in range(quarter + 1):
        low_re, low_im = bins[index]
        high_re, high_im = bins[count // 2 - index]
        if index == 0:
            even[0] = (low_re + high_re, None)
            odd[0] = (low_re - high_re, None)
        elif index == quarter:
            even[index] = (low_re, None)
            odd[index] = (-low_im, None)
        else:
            even[index] = (low_re + high_re, low_im - high_im)
            diff_re, diff_im = low_re - high_re, low_im + high_im
            cos = math.cos(2.0 * math.pi * index / count)
            sin = math.sin(2.0 * math.pi * index / count)
            odd[index] = (diff_re * cos - diff_im * sin, diff_re * sin + diff_im * cos)
    first = real_segments(even)
    second = real_segments(odd)
    return [item for pair in zip(first, second) for item in pair]


both_last = (((1,), (1,)), ((), ()))
both_first = (((0,), (0,)), ((), ()))


def square_eye(points, flipped):
    row = lax.broadcasted_iota(jnp.int32, (points, points), 0)
    col = lax.broadcasted_iota(jnp.int32, (points, points), 1)
    picked = jnp.where(flipped, points - 1 - col, col)
    return jnp.where(row == picked, 1.0, 0.0).astype(jnp.bfloat16)


whole = pl.BlockSpec(memory_space=pltpu.VMEM)
outside = pl.BlockSpec(memory_space=pl.ANY)
roomy = pltpu.CompilerParams(vmem_limit_bytes=24 << 20)


def copies_of(pairs, marks, pieces):
    made = []
    for index, (source, target) in enumerate(pairs):
        length = source.shape[0] // pieces
        for piece in range(pieces):
            here = slice(piece * length, (piece + 1) * length)
            made.append(pltpu.make_async_copy(source.at[here], target.at[here], marks.at[index, piece]))
    return made


def pack_kernel(signal_hbm, cotangent_hbm, out_ref, held_ref, arrival, *, narrow):
    points, channels = signal_hbm.shape
    sources = (signal_hbm, cotangent_hbm)
    copies = copies_of([(source, held_ref.at[part]) for part, source in enumerate(sources)], arrival, 1)
    for copy in copies:
        copy.start()
    for part in range(2):
        for copy in copies[part : part + 1]:
            copy.wait()
        turned = held_ref[part].T.reshape(channels // narrow, narrow, points)
        out_ref[:, part * narrow : (part + 1) * narrow, :] = turned


def pack_call(signal, cotangent, narrow):
    points, channels = signal.shape
    signal = pltpu.with_memory_space_constraint(signal, pltpu.HBM)
    cotangent = pltpu.with_memory_space_constraint(cotangent, pltpu.HBM)
    return pl.pallas_call(
        functools.partial(pack_kernel, narrow=narrow),
        in_specs=[pl.BlockSpec(memory_space=pltpu.HBM)] * 2,
        out_specs=whole,
        out_shape=jax.ShapeDtypeStruct((channels // narrow, 2 * narrow, points), jnp.bfloat16),
        scratch_shapes=[
            pltpu.VMEM((2, points, channels), jnp.bfloat16),
            pltpu.SemaphoreType.DMA((2, 1)),
        ],
        compiler_params=roomy,
        name="pack",
    )(signal, cotangent)


def unpack_kernel(in_ref, out_hbm, held_ref, leaving):
    channels, points = in_ref.shape
    length = points // 2
    copies = copies_of([(held_ref, out_hbm)], leaving, 2)
    for piece, copy in enumerate(copies):
        here = slice(piece * length, (piece + 1) * length)
        held_ref[here, :] = in_ref[:, here].T
        copy.start()
    for copy in copies:
        copy.wait()


def unpack_call(rows):
    channels, points = rows.shape
    return pl.pallas_call(
        unpack_kernel,
        in_specs=[whole],
        out_specs=pl.BlockSpec(memory_space=pl.ANY),
        out_shape=jax.ShapeDtypeStruct((points, channels), jnp.bfloat16),
        scratch_shapes=[pltpu.VMEM((points, channels), jnp.bfloat16), pltpu.SemaphoreType.DMA((1, 2))],
        compiler_params=roomy,
        name="unpack",
    )(rows)


def over_chunks(emit, segments, chunk):
    emit(0, 1, False)
    emit(segments, 1, False)
    count = (segments - 1) // chunk

    def step(index, carry):
        emit(1 + index * chunk, chunk, True)
        return carry

    lax.fori_loop(0, count, step, 0)
    if (segments - 1) % chunk:
        emit(1 + count * chunk, (segments - 1) % chunk, True)


def forward_kernel(in_ref, twist_ref, matrix_ref, grad_ref, spectra_ref, mid_ref, *, scale, chunk):
    sequences, segments, pair_rows, points = in_ref.shape
    narrow = pair_rows // 2
    rows = sequences * narrow
    tiles = pair_rows // sub

    def tile_step(step, carry):
        which = step // tiles
        piece = step % tiles
        start = pl.multiple_of(piece * sub, sub)
        target = (piece // (tiles // 2)) * rows + which * narrow
        target = pl.multiple_of(target + (piece % (tiles // 2)) * sub, sub)
        for left in range(0, points, lane):
            here = slice(left, left + lane)
            after = slice(points + left, points + left + lane)
            values = [
                in_ref[which, seg, pl.ds(start, sub), here].astype(jnp.float32) for seg in range(segments)
            ]
            for index, (re, im) in enumerate(half_spectrum(values)):
                cos = twist_ref[index, 0:1, here]
                sin = twist_ref[index, 1:2, here]
                if im is None:
                    new_re, new_im = re * cos, -(re * sin)
                else:
                    new_re, new_im = re * cos + im * sin, im * cos - re * sin
                mid_ref[index, pl.ds(target, sub), here] = new_re.astype(jnp.bfloat16)
                mid_ref[index, pl.ds(target, sub), after] = new_im.astype(jnp.bfloat16)
        return carry

    lax.fori_loop(0, sequences * tiles, tile_step, 0)

    def emit(base, count, paired):
        values = mid_ref[pl.ds(base, count)].reshape(count * 2 * rows, 2 * points)
        full = jnp.dot(values, matrix_ref[...], preferred_element_type=jnp.float32).reshape(count, 2 * rows, 2 * points)
        for extra in range(count):
            residue = base + extra
            signal_re, signal_im = full[extra, :rows, :points], full[extra, :rows, points:]
            cotan_re, cotan_im = full[extra, rows:, :points], full[extra, rows:, points:]
            spectra_ref[residue, 0] = signal_re
            spectra_ref[residue, 1] = signal_im
            real_term = signal_re * cotan_re + signal_im * cotan_im
            imag_term = signal_re * cotan_im - signal_im * cotan_re
            real_sum = jnp.sum(real_term.reshape(sequences, narrow, points), axis=0) * scale
            imag_sum = jnp.sum(imag_term.reshape(sequences, narrow, points), axis=0) * scale
            grad_ref[residue, 0] = real_sum.astype(jnp.bfloat16)
            grad_ref[residue, 1] = imag_sum.astype(jnp.bfloat16)
            if paired:
                grad_ref[2 * segments - residue, 0] = real_sum.astype(jnp.bfloat16)
                grad_ref[2 * segments - residue, 1] = (-imag_sum).astype(jnp.bfloat16)

    over_chunks(emit, segments, chunk)


def forward_call(arrived, twist, matrices):
    sequences, segments, pair_rows, points = arrived.shape
    narrow = pair_rows // 2
    outer = 2 * segments
    rows = sequences * narrow
    return pl.pallas_call(
        functools.partial(forward_kernel, scale=1.0 / (outer * points), chunk=8),
        in_specs=[whole, whole, whole],
        out_specs=[whole, whole],
        out_shape=[
            jax.ShapeDtypeStruct((outer, 2, narrow, points), jnp.bfloat16),
            jax.ShapeDtypeStruct((segments + 1, 2, rows, points), jnp.float32),
        ],
        scratch_shapes=[pltpu.VMEM((segments + 1, 2 * rows, 2 * points), jnp.bfloat16)],
        compiler_params=roomy,
        name="forward",
    )(arrived, twist, matrices)


def moved(grad, spec, first, second):
    new_first = 0.9 * first + 0.1 * grad
    new_second = 0.99 * second + 0.01 * grad * grad
    return spec - step_rate * jnp.tanh(new_first / (jnp.sqrt(new_second) + epsilon)), new_first, new_second


def is_mirrored(row, local_outer):
    return lax.axis_index("seq") * local_outer + row > lax.axis_size("seq")


def update_kernel(grad_ref, spec_ref, first_ref, second_ref, *refs):
    final, held, (out_ref, *ready, leaving) = refs[:3], refs[3:6], refs[6:]
    _, local_outer, points, width = spec_ref.shape
    early = ready[0].shape[1]
    copies = []
    for row in range(local_outer):
        eye = square_eye(points, is_mirrored(row, local_outer))
        for part in range(2):
            sent = grad_ref[:, row, part].reshape(width, points)
            grad = lax.dot_general(eye, sent, both_last, preferred_element_type=jnp.float32)
            made = moved(grad, spec_ref[part, row], first_ref[part, row], second_ref[part, row])
            for index in range(3):
                if row < early:
                    ready[index][part, row] = made[index]
                    copies.append(
                        pltpu.make_async_copy(
                            ready[index].at[part, row], final[index].at[part, row], leaving.at[index, part, row]
                        )
                    )
                    copies[-1].start()
                else:
                    held[index][part, row - early] = made[index]
            turned = lax.dot_general(
                made[0].astype(jnp.bfloat16), eye, both_first, preferred_element_type=jnp.float32
            )
            out_ref[:, row, part] = turned.astype(jnp.bfloat16).reshape(grad_ref.shape[0], -1, points)
    for copy in copies:
        copy.wait()


def update_call(sent, spectrum, first_moment, second_moment):
    parts, local_outer, points, channels = spectrum.shape
    early = (local_outer + 1) // 2
    late = (parts, local_outer - early, points, channels)
    made = pl.pallas_call(
        update_kernel,
        in_specs=[whole, whole, whole, whole],
        out_specs=[outside] * 3 + [whole] * 4,
        out_shape=[jax.ShapeDtypeStruct(spectrum.shape, jnp.float32)] * 3
        + [jax.ShapeDtypeStruct(late, jnp.float32)] * 3
        + [jax.ShapeDtypeStruct(sent.shape, jnp.bfloat16)],
        scratch_shapes=[pltpu.VMEM((parts, early, points, channels), jnp.float32)] * 3
        + [pltpu.SemaphoreType.DMA((3, parts, early))],
        compiler_params=roomy,
        name="update",
    )(sent, spectrum, first_moment, second_moment)
    return (made[:3], made[3:6]), made[6]


def inverse_kernel(spectra_ref, filter_ref, twist_ref, matrix_ref, *refs, chunk):
    held, out_ref, final, mid_ref, leaving = refs[:3], refs[6], refs[7:10], refs[10], refs[11]
    early = final[0].shape[1] - held[0].shape[1]
    pairs = [
        (source.at[part], target.at[part, early:])
        for source, target in zip(held, final)
        for part in range(source.shape[0])
    ]
    copies = copies_of(pairs, leaving, 1)
    for copy in copies:
        copy.start()
    sequences, segments, narrow, points = out_ref.shape
    rows = sequences * narrow

    def mixed(residue, paired):
        filter_re = filter_ref[residue, 0].astype(jnp.float32)
        filter_im = filter_ref[residue, 1].astype(jnp.float32)
        if paired:
            filter_re = filter_re + filter_ref[2 * segments - residue, 0].astype(jnp.float32)
            filter_im = filter_im - filter_ref[2 * segments - residue, 1].astype(jnp.float32)
        signal_re = spectra_ref[residue, 0].reshape(sequences, narrow, points)
        signal_im = spectra_ref[residue, 1].reshape(sequences, narrow, points)
        mixed_re = (signal_re * filter_re - signal_im * filter_im).reshape(rows, points)
        mixed_im = (signal_re * filter_im + signal_im * filter_re).reshape(rows, points)
        return jnp.concatenate([mixed_re.astype(jnp.bfloat16), mixed_im.astype(jnp.bfloat16)], axis=1)

    def emit(base, count, paired):
        values = jnp.concatenate([mixed(base + extra, paired) for extra in range(count)], axis=0)
        full = jnp.dot(values, matrix_ref[...], preferred_element_type=jnp.float32).reshape(count, rows, 2 * points)
        for extra in range(count):
            residue = base + extra
            cos = twist_ref[residue, 0:1]
            sin = twist_ref[residue, 1:2]
            mid_ref[residue, 0] = full[extra, :, :points] * cos - full[extra, :, points:] * sin
            mid_ref[residue, 1] = full[extra, :, :points] * sin + full[extra, :, points:] * cos

    over_chunks(emit, segments, chunk)
    tiles = narrow // sub

    def tile_step(step, carry):
        which = step // tiles
        start = pl.multiple_of((step % tiles) * sub, sub)
        source = pl.multiple_of(step * sub, sub)
        for left in range(0, points, lane):
            here = slice(left, left + lane)
            bins = [
                tuple(mid_ref[index, part, pl.ds(source, sub), here] for part in range(2))
                for index in range(segments + 1)
            ]
            for seg, value in enumerate(real_segments(bins)):
                out_ref[which, seg, pl.ds(start, sub), here] = value.astype(jnp.bfloat16)
        return carry

    lax.fori_loop(0, sequences * tiles, tile_step, 0)
    for copy in copies:
        copy.wait()


def inverse_call(spectra, filters, twist, matrices, states):
    final, held = states
    residues, _, rows, points = spectra.shape
    segments = residues - 1
    narrow = filters.shape[2]
    sequences = rows // narrow
    out, *final = pl.pallas_call(
        functools.partial(inverse_kernel, chunk=8),
        in_specs=[whole] * 7 + [outside] * 3,
        out_specs=[whole] + [outside] * 3,
        out_shape=[jax.ShapeDtypeStruct((sequences, segments, narrow, points), jnp.bfloat16)]
        + [jax.ShapeDtypeStruct(state.shape, state.dtype) for state in final],
        input_output_aliases={7: 1, 8: 2, 9: 3},
        scratch_shapes=[
            pltpu.VMEM((residues, 2, rows, points), jnp.float32),
            pltpu.SemaphoreType.DMA((6, 1)),
        ],
        compiler_params=roomy,
        name="inverse",
    )(spectra, filters, twist, matrices, *held, *final)
    return out, final


def pack_plain(signal, cotangent, narrow):
    points, channels = signal.shape
    both = jnp.stack([signal, cotangent]).reshape(2, points, channels // narrow, narrow)
    return both.transpose(2, 0, 3, 1).reshape(channels // narrow, 2 * narrow, points)


def forward_plain(arrived, twist, matrices):
    sequences, segments, pair_rows, points = arrived.shape
    narrow = pair_rows // 2
    rows = sequences * narrow
    parts = arrived.reshape(sequences, segments, 2, narrow, points).astype(jnp.float32)
    parts = parts.transpose(1, 2, 0, 3, 4).reshape(segments, 2 * rows, points)
    bins = half_spectrum([parts[seg] for seg in range(segments)])
    re = jnp.stack([item[0] for item in bins])
    im = jnp.stack([jnp.zeros_like(item[0]) if item[1] is None else item[1] for item in bins])
    cos, sin = twist[:, 0][:, None], twist[:, 1][:, None]
    mid = jnp.concatenate([re * cos + im * sin, im * cos - re * sin], axis=2).astype(jnp.bfloat16)
    full = jnp.dot(mid, matrices, preferred_element_type=jnp.float32)
    signal_re, signal_im = full[:, :rows, :points], full[:, :rows, points:]
    cotan_re, cotan_im = full[:, rows:, :points], full[:, rows:, points:]
    shape = (segments + 1, sequences, narrow, points)
    scale = 1.0 / (2 * segments * points)
    real = jnp.sum((signal_re * cotan_re + signal_im * cotan_im).reshape(shape), axis=1) * scale
    imag = jnp.sum((signal_re * cotan_im - signal_im * cotan_re).reshape(shape), axis=1) * scale
    real = jnp.concatenate([real, real[1:segments][::-1]])
    imag = jnp.concatenate([imag, -imag[1:segments][::-1]])
    grad = jnp.stack([real, imag], axis=1).astype(jnp.bfloat16)
    return grad, jnp.stack([signal_re, signal_im], axis=1)


def mirrored_rows(local_outer):
    rows = jnp.arange(local_outer, dtype=jnp.int32)
    return is_mirrored(rows, local_outer)[None, :, None, None]


def gradient_plain(sent, shape):
    arrived = sent.astype(jnp.float32).transpose(2, 1, 4, 0, 3).reshape(shape)
    return jnp.where(mirrored_rows(shape[1]), arrived[:, :, ::-1], arrived)


def update_plain(sent, spectrum, first_moment, second_moment):
    groups, local_outer, _, narrow, points = sent.shape
    grad = gradient_plain(sent, spectrum.shape)
    new_spec, new_first, new_second = moved(grad, spectrum, first_moment, second_moment)
    out = jnp.where(mirrored_rows(local_outer), new_spec[:, :, ::-1], new_spec).astype(jnp.bfloat16)
    out = out.reshape(2, local_outer, points, groups, narrow).transpose(3, 1, 0, 4, 2)
    return (new_spec, new_first, new_second), out


def inverse_plain(spectra, filters, twist, matrices, states):
    residues, _, rows, points = spectra.shape
    segments = residues - 1
    narrow = filters.shape[2]
    sequences = rows // narrow
    wide = filters.astype(jnp.float32)
    mirrored = jnp.concatenate([jnp.zeros_like(wide[:1]), wide[segments + 1 :][::-1], jnp.zeros_like(wide[:1])])
    filter_re = (wide[: segments + 1, 0] + mirrored[:, 0])[:, None]
    filter_im = (wide[: segments + 1, 1] - mirrored[:, 1])[:, None]
    shape = (residues, sequences, narrow, points)
    signal_re, signal_im = spectra[:, 0].reshape(shape), spectra[:, 1].reshape(shape)
    mixed_re = (signal_re * filter_re - signal_im * filter_im).reshape(residues, rows, points)
    mixed_im = (signal_re * filter_im + signal_im * filter_re).reshape(residues, rows, points)
    mixed = jnp.concatenate([mixed_re, mixed_im], axis=2).astype(jnp.bfloat16)
    full = jnp.dot(mixed, matrices, preferred_element_type=jnp.float32)
    cos, sin = twist[:, 0][:, None], twist[:, 1][:, None]
    mid_re = full[..., :points] * cos - full[..., points:] * sin
    mid_im = full[..., :points] * sin + full[..., points:] * cos
    out = jnp.stack(real_segments([(mid_re[index], mid_im[index]) for index in range(residues)]))
    out = out.reshape(segments, sequences, narrow, points).transpose(1, 0, 2, 3)
    return out.astype(jnp.bfloat16), states


def per_device(inputs, grad_out, spectrum, first_moment, second_moment):
    seq_count = lax.axis_size("seq")
    batch_count = lax.axis_size("batch")
    batch_rows, points, channels = inputs.shape
    narrow = channels // (seq_count * batch_count)
    local_outer = spectrum.shape[1]
    outer = 2 * seq_count
    tiled = narrow % sub == 0 and points % lane == 0 and batch_rows == 1
    twist = jnp.asarray(twist_table(outer, points))
    ahead, back = point_matrices(points, 1.0 / (outer * points))
    ahead, back = jnp.asarray(ahead, jnp.bfloat16), jnp.asarray(back, jnp.bfloat16)

    pack = pack_call if tiled else pack_plain
    packed = jnp.stack([pack(inputs[row], grad_out[row], narrow) for row in range(batch_rows)], axis=1)
    arrived = lax.all_to_all(packed, ("batch", "seq"), split_axis=0, concat_axis=0, tiled=True)
    arrived = arrived.reshape(batch_count, seq_count, batch_rows, 2 * narrow, points)
    arrived = arrived.transpose(0, 2, 1, 3, 4).reshape(-1, seq_count, 2 * narrow, points)
    sequences = arrived.shape[0]

    grad, spectra = (forward_call if tiled else forward_plain)(arrived, twist, ahead)
    grad = grad.reshape(seq_count, local_outer, 2, narrow, points)
    sent = lax.all_to_all(grad, "seq", split_axis=0, concat_axis=0, tiled=True)

    update = update_call if tiled else update_plain
    states, filters = update(sent, spectrum, first_moment, second_moment)
    filters = lax.all_to_all(filters, "seq", split_axis=0, concat_axis=0, tiled=True)
    filters = filters.reshape(outer, 2, narrow, points)

    rows, states = (inverse_call if tiled else inverse_plain)(spectra, filters, twist, back, states)
    rows = rows.reshape(batch_count, batch_rows, seq_count, narrow, points).transpose(0, 2, 1, 3, 4)
    rows = rows.reshape(batch_count * seq_count, batch_rows, narrow, points)
    rows = lax.all_to_all(rows, ("batch", "seq"), split_axis=0, concat_axis=0, tiled=True)
    if tiled:
        filtered = unpack_call(rows.reshape(channels, points))[None]
    else:
        filtered = rows.transpose(1, 3, 0, 2).reshape(batch_rows, points, channels)
    return *states, filtered


def solution(mesh):
    return jax.shard_map(
        per_device,
        mesh=mesh,
        in_specs=(
            P("batch", "seq", None),
            P("batch", "seq", None),
            P(None, "seq", None, "batch"),
            P(None, "seq", None, "batch"),
            P(None, "seq", None, "batch"),
        ),
        out_specs=(
            P(None, "seq", None, "batch"),
            P(None, "seq", None, "batch"),
            P(None, "seq", None, "batch"),
            P("batch", "seq", None),
        ),
        check_vma=False,
    )
```

```python
import functools
import math

import jax
import jax.numpy as jnp
import numpy as np
from jax import lax
from jax.experimental import pallas as pl
from jax.experimental.pallas import tpu as pltpu
from jax.sharding import PartitionSpec as P

step_rate = 0.5
epsilon = 1e-06
sub = 16
lane = 128


def turn_table(numer, modulus):
    phase = 2.0 * math.pi * (numer % modulus) / modulus
    return np.cos(phase), np.sin(phase)


def twist_table(outer, points):
    half = outer // 2
    index = np.arange(half + 1)[:, None] * np.arange(points)[None, :]
    cos, sin = turn_table(index, outer * points)
    return np.stack([cos, sin], axis=1).astype(np.float32)


def point_matrices(points, scale_back):
    index = np.arange(points)[:, None] * np.arange(points)[None, :]
    cos, sin = turn_table(index, points)
    ahead = np.block([[cos, -sin], [sin, cos]])
    back = np.block([[cos, sin], [-sin, cos]]) * scale_back
    return ahead.astype(np.float32), back.astype(np.float32)


def times_phase(re, im, turns, count):
    if turns == 0:
        return re, im
    if 4 * turns == count:
        return im, -re
    cos = math.cos(2.0 * math.pi * turns / count)
    sin = math.sin(2.0 * math.pi * turns / count)
    return re * cos + im * sin, im * cos - re * sin


def half_spectrum(values):
    total = 2 * len(values)
    if total == 2:
        return [(values[0], None), (values[0], None)]
    even = half_spectrum(values[0::2])
    odd = half_spectrum(values[1::2])
    quarter = total // 4
    out = [None] * (total // 2 + 1)
    for index in range(quarter + 1):
        even_re, even_im = even[index]
        odd_re, odd_im = odd[index]
        if index == 0:
            out[0] = (even_re + odd_re, None)
            out[total // 2] = (even_re - odd_re, None)
        elif index == quarter:
            out[index] = (even_re, -odd_re)
        else:
            turned_re, turned_im = times_phase(odd_re, odd_im, index, total)
            out[index] = (even_re + turned_re, even_im + turned_im)
            out[total // 2 - index] = (even_re - turned_re, turned_im - even_im)
    return out


def real_segments(bins):
    count = 2 * (len(bins) - 1)
    if count == 2:
        return [bins[0][0] + bins[1][0]]
    quarter = count // 4
    even = [None] * (quarter + 1)
    odd = [None] * (quarter + 1)
    for index in range(quarter + 1):
        low_re, low_im = bins[index]
        high_re, high_im = bins[count // 2 - index]
        if index == 0:
            even[0] = (low_re + high_re, None)
            odd[0] = (low_re - high_re, None)
        elif index == quarter:
            even[index] = (low_re, None)
            odd[index] = (-low_im, None)
        else:
            even[index] = (low_re + high_re, low_im - high_im)
            diff_re, diff_im = low_re - high_re, low_im + high_im
            cos = math.cos(2.0 * math.pi * index / count)
            sin = math.sin(2.0 * math.pi * index / count)
            odd[index] = (diff_re * cos - diff_im * sin, diff_re * sin + diff_im * cos)
    first = real_segments(even)
    second = real_segments(odd)
    return [item for pair in zip(first, second) for item in pair]


both_last = (((1,), (1,)), ((), ()))
both_first = (((0,), (0,)), ((), ()))


def square_eye(points, flipped):
    row = lax.broadcasted_iota(jnp.int32, (points, points), 0)
    col = lax.broadcasted_iota(jnp.int32, (points, points), 1)
    picked = jnp.where(flipped, points - 1 - col, col)
    return jnp.where(row == picked, 1.0, 0.0).astype(jnp.bfloat16)


whole = pl.BlockSpec(memory_space=pltpu.VMEM)
outside = pl.BlockSpec(memory_space=pl.ANY)
roomy = pltpu.CompilerParams(vmem_limit_bytes=24 << 20)


def copies_of(pairs, marks, pieces):
    made = []
    for index, (source, target) in enumerate(pairs):
        length = source.shape[0] // pieces
        for piece in range(pieces):
            here = slice(piece * length, (piece + 1) * length)
            made.append(pltpu.make_async_copy(source.at[here], target.at[here], marks.at[index, piece]))
    return made


def pack_kernel(signal_hbm, cotangent_hbm, out_ref, held_ref, arrival, *, narrow):
    points, channels = signal_hbm.shape
    sources = (signal_hbm, cotangent_hbm)
    copies = copies_of([(source, held_ref.at[part]) for part, source in enumerate(sources)], arrival, 1)
    for copy in copies:
        copy.start()
    for part in range(2):
        for copy in copies[part : part + 1]:
            copy.wait()
        turned = held_ref[part].T.reshape(channels // narrow, narrow, points)
        out_ref[:, part * narrow : (part + 1) * narrow, :] = turned


def pack_call(signal, cotangent, narrow):
    points, channels = signal.shape
    signal = pltpu.with_memory_space_constraint(signal, pltpu.HBM)
    cotangent = pltpu.with_memory_space_constraint(cotangent, pltpu.HBM)
    return pl.pallas_call(
        functools.partial(pack_kernel, narrow=narrow),
        in_specs=[pl.BlockSpec(memory_space=pltpu.HBM)] * 2,
        out_specs=whole,
        out_shape=jax.ShapeDtypeStruct((channels // narrow, 2 * narrow, points), jnp.bfloat16),
        scratch_shapes=[
            pltpu.VMEM((2, points, channels), jnp.bfloat16),
            pltpu.SemaphoreType.DMA((2, 1)),
        ],
        compiler_params=roomy,
        name="pack",
    )(signal, cotangent)


def unpack_kernel(in_ref, out_hbm, held_ref, leaving):
    channels, points = in_ref.shape
    length = points // 2
    copies = copies_of([(held_ref, out_hbm)], leaving, 2)
    for piece, copy in enumerate(copies):
        here = slice(piece * length, (piece + 1) * length)
        held_ref[here, :] = in_ref[:, here].T
        copy.start()
    for copy in copies:
        copy.wait()


def unpack_call(rows):
    channels, points = rows.shape
    return pl.pallas_call(
        unpack_kernel,
        in_specs=[whole],
        out_specs=pl.BlockSpec(memory_space=pl.ANY),
        out_shape=jax.ShapeDtypeStruct((points, channels), jnp.bfloat16),
        scratch_shapes=[pltpu.VMEM((points, channels), jnp.bfloat16), pltpu.SemaphoreType.DMA((1, 2))],
        compiler_params=roomy,
        name="unpack",
    )(rows)


def over_chunks(emit, segments, chunk):
    emit(0, 1, False)
    emit(segments, 1, False)
    count = (segments - 1) // chunk

    def step(index, carry):
        emit(1 + index * chunk, chunk, True)
        return carry

    lax.fori_loop(0, count, step, 0)
    if (segments - 1) % chunk:
        emit(1 + count * chunk, (segments - 1) % chunk, True)


def forward_kernel(in_ref, twist_ref, matrix_ref, grad_ref, spectra_ref, mid_ref, *, scale, chunk):
    sequences, segments, pair_rows, points = in_ref.shape
    narrow = pair_rows // 2
    rows = sequences * narrow
    tiles = pair_rows // sub

    def tile_step(step, carry):
        which = step // tiles
        piece = step % tiles
        start = pl.multiple_of(piece * sub, sub)
        target = (piece // (tiles // 2)) * rows + which * narrow
        target = pl.multiple_of(target + (piece % (tiles // 2)) * sub, sub)
        for left in range(0, points, lane):
            here = slice(left, left + lane)
            after = slice(points + left, points + left + lane)
            values = [
                in_ref[which, seg, pl.ds(start, sub), here].astype(jnp.float32) for seg in range(segments)
            ]
            for index, (re, im) in enumerate(half_spectrum(values)):
                cos = twist_ref[index, 0:1, here]
                sin = twist_ref[index, 1:2, here]
                if im is None:
                    new_re, new_im = re * cos, -(re * sin)
                else:
                    new_re, new_im = re * cos + im * sin, im * cos - re * sin
                mid_ref[index, pl.ds(target, sub), here] = new_re.astype(jnp.bfloat16)
                mid_ref[index, pl.ds(target, sub), after] = new_im.astype(jnp.bfloat16)
        return carry

    lax.fori_loop(0, sequences * tiles, tile_step, 0)

    def emit(base, count, paired):
        values = mid_ref[pl.ds(base, count)].reshape(count * 2 * rows, 2 * points)
        full = jnp.dot(values, matrix_ref[...], preferred_element_type=jnp.float32).reshape(count, 2 * rows, 2 * points)
        for extra in range(count):
            residue = base + extra
            signal_re, signal_im = full[extra, :rows, :points], full[extra, :rows, points:]
            cotan_re, cotan_im = full[extra, rows:, :points], full[extra, rows:, points:]
            spectra_ref[residue, 0] = signal_re
            spectra_ref[residue, 1] = signal_im
            real_term = signal_re * cotan_re + signal_im * cotan_im
            imag_term = signal_re * cotan_im - signal_im * cotan_re
            real_sum = jnp.sum(real_term.reshape(sequences, narrow, points), axis=0) * scale
            imag_sum = jnp.sum(imag_term.reshape(sequences, narrow, points), axis=0) * scale
            grad_ref[residue, 0] = real_sum.astype(jnp.bfloat16)
            grad_ref[residue, 1] = imag_sum.astype(jnp.bfloat16)
            if paired:
                grad_ref[2 * segments - residue, 0] = real_sum.astype(jnp.bfloat16)
                grad_ref[2 * segments - residue, 1] = (-imag_sum).astype(jnp.bfloat16)

    over_chunks(emit, segments, chunk)


def forward_call(arrived, twist, matrices):
    sequences, segments, pair_rows, points = arrived.shape
    narrow = pair_rows // 2
    outer = 2 * segments
    rows = sequences * narrow
    return pl.pallas_call(
        functools.partial(forward_kernel, scale=1.0 / (outer * points), chunk=8),
        in_specs=[whole, whole, whole],
        out_specs=[whole, whole],
        out_shape=[
            jax.ShapeDtypeStruct((outer, 2, narrow, points), jnp.bfloat16),
            jax.ShapeDtypeStruct((segments + 1, 2, rows, points), jnp.float32),
        ],
        scratch_shapes=[pltpu.VMEM((segments + 1, 2 * rows, 2 * points), jnp.bfloat16)],
        compiler_params=roomy,
        name="forward",
    )(arrived, twist, matrices)


def moved(grad, spec, first, second):
    new_first = 0.9 * first + 0.1 * grad
    new_second = 0.99 * second + 0.01 * grad * grad
    root = new_second * lax.rsqrt(new_second)
    return spec - step_rate * jnp.tanh(new_first / (root + epsilon)), new_first, new_second


def is_mirrored(row, local_outer):
    return lax.axis_index("seq") * local_outer + row > lax.axis_size("seq")


early_blocks = 2


def state_blocks(parts, local_outer):
    return [(part, row) for row in range(local_outer) for part in range(parts)]


def update_kernel(grad_ref, spec_ref, first_ref, second_ref, *refs):
    final, held, (out_ref, *ready, leaving) = refs[:3], refs[3:6], refs[6:]
    parts, local_outer, points, width = spec_ref.shape
    copies = []
    for order, (part, row) in enumerate(state_blocks(parts, local_outer)):
        if part == 0:
            eye = square_eye(points, is_mirrored(row, local_outer))
        sent = grad_ref[:, row, part].reshape(width, points)
        grad = lax.dot_general(eye, sent, both_last, preferred_element_type=jnp.float32)
        made = moved(grad, spec_ref[part, row], first_ref[part, row], second_ref[part, row])
        for index in range(3):
            if order < early_blocks:
                ready[index][order] = made[index]
                copies.append(
                    pltpu.make_async_copy(
                        ready[index].at[order], final[index].at[part, row], leaving.at[index, order]
                    )
                )
                copies[-1].start()
            else:
                held[index][order - early_blocks] = made[index]
        turned = lax.dot_general(
            made[0].astype(jnp.bfloat16), eye, both_first, preferred_element_type=jnp.float32
        )
        out_ref[:, row, part] = turned.astype(jnp.bfloat16).reshape(grad_ref.shape[0], -1, points)
    for copy in copies:
        copy.wait()


def update_call(sent, spectrum, first_moment, second_moment):
    parts, local_outer, points, channels = spectrum.shape
    early = (early_blocks, points, channels)
    late = (parts * local_outer - early_blocks, points, channels)
    made = pl.pallas_call(
        update_kernel,
        in_specs=[whole, whole, whole, whole],
        out_specs=[outside] * 3 + [whole] * 4,
        out_shape=[jax.ShapeDtypeStruct(spectrum.shape, jnp.float32)] * 3
        + [jax.ShapeDtypeStruct(late, jnp.float32)] * 3
        + [jax.ShapeDtypeStruct(sent.shape, jnp.bfloat16)],
        scratch_shapes=[pltpu.VMEM(early, jnp.float32)] * 3 + [pltpu.SemaphoreType.DMA((3, early_blocks))],
        compiler_params=roomy,
        name="update",
    )(sent, spectrum, first_moment, second_moment)
    return (made[:3], made[3:6]), made[6]


def inverse_kernel(spectra_ref, filter_ref, twist_ref, matrix_ref, *refs, chunk):
    held, out_ref, final, mid_ref, leaving = refs[:3], refs[6], refs[7:10], refs[10], refs[11]
    late = state_blocks(*final[0].shape[:2])[early_blocks:]
    pairs = [
        (source.at[order], target.at[part, row])
        for source, target in zip(held, final)
        for order, (part, row) in enumerate(late)
    ]
    copies = copies_of(pairs, leaving, 1)
    for copy in copies:
        copy.start()
    sequences, segments, narrow, points = out_ref.shape
    rows = sequences * narrow

    def mixed(residue, paired):
        filter_re = filter_ref[residue, 0].astype(jnp.float32)
        filter_im = filter_ref[residue, 1].astype(jnp.float32)
        if paired:
            filter_re = filter_re + filter_ref[2 * segments - residue, 0].astype(jnp.float32)
            filter_im = filter_im - filter_ref[2 * segments - residue, 1].astype(jnp.float32)
        signal_re = spectra_ref[residue, 0].reshape(sequences, narrow, points)
        signal_im = spectra_ref[residue, 1].reshape(sequences, narrow, points)
        mixed_re = (signal_re * filter_re - signal_im * filter_im).reshape(rows, points)
        mixed_im = (signal_re * filter_im + signal_im * filter_re).reshape(rows, points)
        return jnp.concatenate([mixed_re.astype(jnp.bfloat16), mixed_im.astype(jnp.bfloat16)], axis=1)

    def emit(base, count, paired):
        values = jnp.concatenate([mixed(base + extra, paired) for extra in range(count)], axis=0)
        full = jnp.dot(values, matrix_ref[...], preferred_element_type=jnp.float32).reshape(count, rows, 2 * points)
        for extra in range(count):
            residue = base + extra
            cos = twist_ref[residue, 0:1]
            sin = twist_ref[residue, 1:2]
            mid_ref[residue, 0] = full[extra, :, :points] * cos - full[extra, :, points:] * sin
            mid_ref[residue, 1] = full[extra, :, :points] * sin + full[extra, :, points:] * cos

    over_chunks(emit, segments, chunk)
    tiles = narrow // sub

    def tile_step(step, carry):
        which = step // tiles
        start = pl.multiple_of((step % tiles) * sub, sub)
        source = pl.multiple_of(step * sub, sub)
        for left in range(0, points, lane):
            here = slice(left, left + lane)
            bins = [
                tuple(mid_ref[index, part, pl.ds(source, sub), here] for part in range(2))
                for index in range(segments + 1)
            ]
            for seg, value in enumerate(real_segments(bins)):
                out_ref[which, seg, pl.ds(start, sub), here] = value.astype(jnp.bfloat16)
        return carry

    lax.fori_loop(0, sequences * tiles, tile_step, 0)
    for copy in copies:
        copy.wait()


def inverse_call(spectra, filters, twist, matrices, states):
    final, held = states
    residues, _, rows, points = spectra.shape
    segments = residues - 1
    narrow = filters.shape[2]
    sequences = rows // narrow
    out, *final = pl.pallas_call(
        functools.partial(inverse_kernel, chunk=8),
        in_specs=[whole] * 7 + [outside] * 3,
        out_specs=[whole] + [outside] * 3,
        out_shape=[jax.ShapeDtypeStruct((sequences, segments, narrow, points), jnp.bfloat16)]
        + [jax.ShapeDtypeStruct(state.shape, state.dtype) for state in final],
        input_output_aliases={7: 1, 8: 2, 9: 3},
        scratch_shapes=[
            pltpu.VMEM((residues, 2, rows, points), jnp.float32),
            pltpu.SemaphoreType.DMA((3 * held[0].shape[0], 1)),
        ],
        compiler_params=roomy,
        name="inverse",
    )(spectra, filters, twist, matrices, *held, *final)
    return out, final


def pack_plain(signal, cotangent, narrow):
    points, channels = signal.shape
    both = jnp.stack([signal, cotangent]).reshape(2, points, channels // narrow, narrow)
    return both.transpose(2, 0, 3, 1).reshape(channels // narrow, 2 * narrow, points)


def forward_plain(arrived, twist, matrices):
    sequences, segments, pair_rows, points = arrived.shape
    narrow = pair_rows // 2
    rows = sequences * narrow
    parts = arrived.reshape(sequences, segments, 2, narrow, points).astype(jnp.float32)
    parts = parts.transpose(1, 2, 0, 3, 4).reshape(segments, 2 * rows, points)
    bins = half_spectrum([parts[seg] for seg in range(segments)])
    re = jnp.stack([item[0] for item in bins])
    im = jnp.stack([jnp.zeros_like(item[0]) if item[1] is None else item[1] for item in bins])
    cos, sin = twist[:, 0][:, None], twist[:, 1][:, None]
    mid = jnp.concatenate([re * cos + im * sin, im * cos - re * sin], axis=2).astype(jnp.bfloat16)
    full = jnp.dot(mid, matrices, preferred_element_type=jnp.float32)
    signal_re, signal_im = full[:, :rows, :points], full[:, :rows, points:]
    cotan_re, cotan_im = full[:, rows:, :points], full[:, rows:, points:]
    shape = (segments + 1, sequences, narrow, points)
    scale = 1.0 / (2 * segments * points)
    real = jnp.sum((signal_re * cotan_re + signal_im * cotan_im).reshape(shape), axis=1) * scale
    imag = jnp.sum((signal_re * cotan_im - signal_im * cotan_re).reshape(shape), axis=1) * scale
    real = jnp.concatenate([real, real[1:segments][::-1]])
    imag = jnp.concatenate([imag, -imag[1:segments][::-1]])
    grad = jnp.stack([real, imag], axis=1).astype(jnp.bfloat16)
    return grad, jnp.stack([signal_re, signal_im], axis=1)


def mirrored_rows(local_outer):
    rows = jnp.arange(local_outer, dtype=jnp.int32)
    return is_mirrored(rows, local_outer)[None, :, None, None]


def gradient_plain(sent, shape):
    arrived = sent.astype(jnp.float32).transpose(2, 1, 4, 0, 3).reshape(shape)
    return jnp.where(mirrored_rows(shape[1]), arrived[:, :, ::-1], arrived)


def update_plain(sent, spectrum, first_moment, second_moment):
    groups, local_outer, _, narrow, points = sent.shape
    grad = gradient_plain(sent, spectrum.shape)
    new_spec, new_first, new_second = moved(grad, spectrum, first_moment, second_moment)
    out = jnp.where(mirrored_rows(local_outer), new_spec[:, :, ::-1], new_spec).astype(jnp.bfloat16)
    out = out.reshape(2, local_outer, points, groups, narrow).transpose(3, 1, 0, 4, 2)
    return (new_spec, new_first, new_second), out


def inverse_plain(spectra, filters, twist, matrices, states):
    residues, _, rows, points = spectra.shape
    segments = residues - 1
    narrow = filters.shape[2]
    sequences = rows // narrow
    wide = filters.astype(jnp.float32)
    mirrored = jnp.concatenate([jnp.zeros_like(wide[:1]), wide[segments + 1 :][::-1], jnp.zeros_like(wide[:1])])
    filter_re = (wide[: segments + 1, 0] + mirrored[:, 0])[:, None]
    filter_im = (wide[: segments + 1, 1] - mirrored[:, 1])[:, None]
    shape = (residues, sequences, narrow, points)
    signal_re, signal_im = spectra[:, 0].reshape(shape), spectra[:, 1].reshape(shape)
    mixed_re = (signal_re * filter_re - signal_im * filter_im).reshape(residues, rows, points)
    mixed_im = (signal_re * filter_im + signal_im * filter_re).reshape(residues, rows, points)
    mixed = jnp.concatenate([mixed_re, mixed_im], axis=2).astype(jnp.bfloat16)
    full = jnp.dot(mixed, matrices, preferred_element_type=jnp.float32)
    cos, sin = twist[:, 0][:, None], twist[:, 1][:, None]
    mid_re = full[..., :points] * cos - full[..., points:] * sin
    mid_im = full[..., :points] * sin + full[..., points:] * cos
    out = jnp.stack(real_segments([(mid_re[index], mid_im[index]) for index in range(residues)]))
    out = out.reshape(segments, sequences, narrow, points).transpose(1, 0, 2, 3)
    return out.astype(jnp.bfloat16), states


def per_device(inputs, grad_out, spectrum, first_moment, second_moment):
    seq_count = lax.axis_size("seq")
    batch_count = lax.axis_size("batch")
    batch_rows, points, channels = inputs.shape
    narrow = channels // (seq_count * batch_count)
    local_outer = spectrum.shape[1]
    outer = 2 * seq_count
    tiled = narrow % sub == 0 and points % lane == 0 and batch_rows == 1
    twist = jnp.asarray(twist_table(outer, points))
    ahead, back = point_matrices(points, 1.0 / (outer * points))
    ahead, back = jnp.asarray(ahead, jnp.bfloat16), jnp.asarray(back, jnp.bfloat16)

    pack = pack_call if tiled else pack_plain
    packed = jnp.stack([pack(inputs[row], grad_out[row], narrow) for row in range(batch_rows)], axis=1)
    arrived = lax.all_to_all(packed, ("batch", "seq"), split_axis=0, concat_axis=0, tiled=True)
    arrived = arrived.reshape(batch_count, seq_count, batch_rows, 2 * narrow, points)
    arrived = arrived.transpose(0, 2, 1, 3, 4).reshape(-1, seq_count, 2 * narrow, points)
    sequences = arrived.shape[0]

    grad, spectra = (forward_call if tiled else forward_plain)(arrived, twist, ahead)
    grad = grad.reshape(seq_count, local_outer, 2, narrow, points)
    sent = lax.all_to_all(grad, "seq", split_axis=0, concat_axis=0, tiled=True)

    update = update_call if tiled else update_plain
    states, filters = update(sent, spectrum, first_moment, second_moment)
    filters = lax.all_to_all(filters, "seq", split_axis=0, concat_axis=0, tiled=True)
    filters = filters.reshape(outer, 2, narrow, points)

    rows, states = (inverse_call if tiled else inverse_plain)(spectra, filters, twist, back, states)
    rows = rows.reshape(batch_count, batch_rows, seq_count, narrow, points).transpose(0, 2, 1, 3, 4)
    rows = rows.reshape(batch_count * seq_count, batch_rows, narrow, points)
    rows = lax.all_to_all(rows, ("batch", "seq"), split_axis=0, concat_axis=0, tiled=True)
    if tiled:
        filtered = unpack_call(rows.reshape(channels, points))[None]
    else:
        filtered = rows.transpose(1, 3, 0, 2).reshape(batch_rows, points, channels)
    return *states, filtered


def solution(mesh):
    return jax.shard_map(
        per_device,
        mesh=mesh,
        in_specs=(
            P("batch", "seq", None),
            P("batch", "seq", None),
            P(None, "seq", None, "batch"),
            P(None, "seq", None, "batch"),
            P(None, "seq", None, "batch"),
        ),
        out_specs=(
            P(None, "seq", None, "batch"),
            P(None, "seq", None, "batch"),
            P(None, "seq", None, "batch"),
            P("batch", "seq", None),
        ),
        check_vma=False,
    )
```

```python
import functools
import math

import jax
import jax.numpy as jnp
import numpy as np
from jax import lax
from jax.experimental import pallas as pl
from jax.experimental.pallas import tpu as pltpu
from jax.sharding import PartitionSpec as P

step_rate = 0.5
epsilon = 1e-06
sub = 16
lane = 128


def turn_table(numer, modulus):
    phase = 2.0 * math.pi * (numer % modulus) / modulus
    return np.cos(phase), np.sin(phase)


def twist_table(outer, points):
    half = outer // 2
    index = np.arange(half + 1)[:, None] * np.arange(points)[None, :]
    cos, sin = turn_table(index, outer * points)
    return np.stack([cos, sin], axis=1).astype(np.float32)


def point_matrices(points, scale_back):
    index = np.arange(points)[:, None] * np.arange(points)[None, :]
    cos, sin = turn_table(index, points)
    ahead = np.block([[cos, -sin], [sin, cos]])
    back = np.block([[cos, sin], [-sin, cos]]) * scale_back
    return ahead.astype(np.float32), back.astype(np.float32)


def times_phase(re, im, turns, count):
    if turns == 0:
        return re, im
    if 4 * turns == count:
        return im, -re
    cos = math.cos(2.0 * math.pi * turns / count)
    sin = math.sin(2.0 * math.pi * turns / count)
    return re * cos + im * sin, im * cos - re * sin


def half_spectrum(values):
    total = 2 * len(values)
    if total == 2:
        return [(values[0], None), (values[0], None)]
    even = half_spectrum(values[0::2])
    odd = half_spectrum(values[1::2])
    quarter = total // 4
    out = [None] * (total // 2 + 1)
    for index in range(quarter + 1):
        even_re, even_im = even[index]
        odd_re, odd_im = odd[index]
        if index == 0:
            out[0] = (even_re + odd_re, None)
            out[total // 2] = (even_re - odd_re, None)
        elif index == quarter:
            out[index] = (even_re, -odd_re)
        else:
            turned_re, turned_im = times_phase(odd_re, odd_im, index, total)
            out[index] = (even_re + turned_re, even_im + turned_im)
            out[total // 2 - index] = (even_re - turned_re, turned_im - even_im)
    return out


def real_segments(bins):
    count = 2 * (len(bins) - 1)
    if count == 2:
        return [bins[0][0] + bins[1][0]]
    quarter = count // 4
    even = [None] * (quarter + 1)
    odd = [None] * (quarter + 1)
    for index in range(quarter + 1):
        low_re, low_im = bins[index]
        high_re, high_im = bins[count // 2 - index]
        if index == 0:
            even[0] = (low_re + high_re, None)
            odd[0] = (low_re - high_re, None)
        elif index == quarter:
            even[index] = (low_re, None)
            odd[index] = (-low_im, None)
        else:
            even[index] = (low_re + high_re, low_im - high_im)
            diff_re, diff_im = low_re - high_re, low_im + high_im
            cos = math.cos(2.0 * math.pi * index / count)
            sin = math.sin(2.0 * math.pi * index / count)
            odd[index] = (diff_re * cos - diff_im * sin, diff_re * sin + diff_im * cos)
    first = real_segments(even)
    second = real_segments(odd)
    return [item for pair in zip(first, second) for item in pair]


both_last = (((1,), (1,)), ((), ()))
both_first = (((0,), (0,)), ((), ()))


def square_eye(points, flipped):
    row = lax.broadcasted_iota(jnp.int32, (points, points), 0)
    col = lax.broadcasted_iota(jnp.int32, (points, points), 1)
    picked = jnp.where(flipped, points - 1 - col, col)
    return jnp.where(row == picked, 1.0, 0.0).astype(jnp.bfloat16)


whole = pl.BlockSpec(memory_space=pltpu.VMEM)
outside = pl.BlockSpec(memory_space=pl.ANY)
roomy = pltpu.CompilerParams(vmem_limit_bytes=24 << 20)
planned = pltpu.CompilerParams(vmem_limit_bytes=24 << 20)


def copies_of(pairs, marks, pieces):
    made = []
    for index, (source, target) in enumerate(pairs):
        length = source.shape[0] // pieces
        for piece in range(pieces):
            here = slice(piece * length, (piece + 1) * length)
            made.append(pltpu.make_async_copy(source.at[here], target.at[here], marks.at[index, piece]))
    return made


def pack_kernel(signal_hbm, cotangent_hbm, out_ref, held_ref, arrival, *, narrow):
    points, channels = signal_hbm.shape
    sources = (signal_hbm, cotangent_hbm)
    copies = copies_of([(source, held_ref.at[part]) for part, source in enumerate(sources)], arrival, 1)
    for copy in copies:
        copy.start()
    for part in range(2):
        for copy in copies[part : part + 1]:
            copy.wait()
        turned = held_ref[part].T.reshape(channels // narrow, narrow, points)
        out_ref[:, part * narrow : (part + 1) * narrow, :] = turned


def pack_call(signal, cotangent, narrow):
    points, channels = signal.shape
    signal = pltpu.with_memory_space_constraint(signal, pltpu.HBM)
    cotangent = pltpu.with_memory_space_constraint(cotangent, pltpu.HBM)
    return pl.pallas_call(
        functools.partial(pack_kernel, narrow=narrow),
        in_specs=[pl.BlockSpec(memory_space=pltpu.HBM)] * 2,
        out_specs=whole,
        out_shape=jax.ShapeDtypeStruct((channels // narrow, 2 * narrow, points), jnp.bfloat16),
        scratch_shapes=[
            pltpu.VMEM((2, points, channels), jnp.bfloat16),
            pltpu.SemaphoreType.DMA((2, 1)),
        ],
        compiler_params=roomy,
        name="pack",
    )(signal, cotangent)


def unpack_kernel(in_ref, out_hbm, held_ref, leaving):
    channels, points = in_ref.shape
    length = points // 2
    copies = copies_of([(held_ref, out_hbm)], leaving, 2)
    for piece, copy in enumerate(copies):
        here = slice(piece * length, (piece + 1) * length)
        held_ref[here, :] = in_ref[:, here].T
        copy.start()
    for copy in copies:
        copy.wait()


def unpack_call(rows):
    channels, points = rows.shape
    return pl.pallas_call(
        unpack_kernel,
        in_specs=[whole],
        out_specs=pl.BlockSpec(memory_space=pl.ANY),
        out_shape=jax.ShapeDtypeStruct((points, channels), jnp.bfloat16),
        scratch_shapes=[pltpu.VMEM((points, channels), jnp.bfloat16), pltpu.SemaphoreType.DMA((1, 2))],
        compiler_params=roomy,
        name="unpack",
    )(rows)


def over_chunks(emit, segments, chunk):
    emit(0, 1, False)
    emit(segments, 1, False)
    count = (segments - 1) // chunk

    def step(index, carry):
        emit(1 + index * chunk, chunk, True)
        return carry

    lax.fori_loop(0, count, step, 0)
    if (segments - 1) % chunk:
        emit(1 + count * chunk, (segments - 1) % chunk, True)


def forward_kernel(in_ref, twist_ref, matrix_ref, grad_ref, spectra_ref, *mid_refs, scale, chunk):
    sequences, segments, pair_rows, points = in_ref.shape
    narrow = pair_rows // 2
    rows = sequences * sub
    residues = segments + 1

    def sums(group, step, left):
        signal, which = step // sequences, step % sequences
        start = pl.multiple_of(signal * narrow + group * sub, sub)
        target = pl.multiple_of(step * sub, sub)
        here = slice(left, left + lane)
        after = slice(points + left, points + left + lane)
        values = [in_ref[which, seg, pl.ds(start, sub), here].astype(jnp.float32) for seg in range(segments)]
        for index, (re, im) in enumerate(half_spectrum(values)):
            cos = twist_ref[index, 0:1, here]
            sin = twist_ref[index, 1:2, here]
            if im is None:
                new_re, new_im = re * cos, -(re * sin)
            else:
                new_re, new_im = re * cos + im * sin, im * cos - re * sin
            mid_refs[group][index, pl.ds(target, sub), here] = new_re.astype(jnp.bfloat16)
            mid_refs[group][index, pl.ds(target, sub), after] = new_im.astype(jnp.bfloat16)

    def emit(group, base, count):
        values = mid_refs[group][base : base + count].reshape(count * 2 * rows, 2 * points)
        full = jnp.dot(values, matrix_ref[...], preferred_element_type=jnp.float32)
        full = full.reshape(count, 2 * rows, 2 * points)
        mine = slice(group * sub, (group + 1) * sub)
        for extra in range(count):
            residue = base + extra
            signal_re, signal_im = full[extra, :rows, :points], full[extra, :rows, points:]
            cotan_re, cotan_im = full[extra, rows:, :points], full[extra, rows:, points:]
            for which in range(sequences):
                part = slice(which * sub, (which + 1) * sub)
                there = slice(which * narrow + group * sub, which * narrow + (group + 1) * sub)
                spectra_ref[residue, 0, there] = signal_re[part]
                spectra_ref[residue, 1, there] = signal_im[part]
            real_term = signal_re * cotan_re + signal_im * cotan_im
            imag_term = signal_re * cotan_im - signal_im * cotan_re
            real_sum = jnp.sum(real_term.reshape(sequences, sub, points), axis=0) * scale
            imag_sum = jnp.sum(imag_term.reshape(sequences, sub, points), axis=0) * scale
            grad_ref[residue, 0, mine] = real_sum.astype(jnp.bfloat16)
            grad_ref[residue, 1, mine] = imag_sum.astype(jnp.bfloat16)
            if 0 < residue < segments:
                grad_ref[2 * segments - residue, 0, mine] = real_sum.astype(jnp.bfloat16)
                grad_ref[2 * segments - residue, 1, mine] = (-imag_sum).astype(jnp.bfloat16)

    def tile_step(step, carry):
        for left in range(0, points, lane):
            sums(0, step, left)
        return carry

    lax.fori_loop(0, 2 * sequences, tile_step, 0)
    groups = narrow // sub
    pieces = [(base, min(chunk, residues - base)) for base in range(0, residues, chunk)]
    for group in range(groups):
        coming = [(step, left) for step in range(2 * sequences) for left in range(0, points, lane)]
        coming = coming if group + 1 < groups else []
        each = -(-len(coming) // len(pieces))
        for number, (base, count) in enumerate(pieces):
            for step, left in coming[number * each : (number + 1) * each]:
                sums(group + 1, step, left)
            emit(group, base, count)


def forward_call(arrived, twist, matrices):
    sequences, segments, pair_rows, points = arrived.shape
    narrow = pair_rows // 2
    outer = 2 * segments
    rows = sequences * narrow
    return pl.pallas_call(
        functools.partial(forward_kernel, scale=1.0 / (outer * points), chunk=2 * outer),
        in_specs=[whole, whole, whole],
        out_specs=[whole, whole],
        out_shape=[
            jax.ShapeDtypeStruct((outer, 2, narrow, points), jnp.bfloat16),
            jax.ShapeDtypeStruct((segments + 1, 2, rows, points), jnp.float32),
        ],
        scratch_shapes=[pltpu.VMEM((segments + 1, 2 * sequences * sub, 2 * points), jnp.bfloat16)]
        * (narrow // sub),
        compiler_params=roomy,
        name="forward",
    )(arrived, twist, matrices)


def moved(grad, spec, first, second):
    new_first = 0.9 * first + 0.1 * grad
    new_second = 0.99 * second + 0.01 * grad * grad
    root = new_second * lax.rsqrt(new_second)
    return spec - step_rate * jnp.tanh(new_first / (root + epsilon)), new_first, new_second


def is_mirrored(row, local_outer):
    return lax.axis_index("seq") * local_outer + row > lax.axis_size("seq")


early_blocks = 2


def state_blocks(parts, local_outer):
    return [(part, row) for row in range(local_outer) for part in range(parts)]


def update_kernel(grad_ref, spec_ref, first_ref, second_ref, *refs):
    final, held, (out_ref, *ready, leaving) = refs[:3], refs[3:6], refs[6:]
    parts, local_outer, points, width = spec_ref.shape
    copies = []
    for order, (part, row) in enumerate(state_blocks(parts, local_outer)):
        if part == 0:
            eye = square_eye(points, is_mirrored(row, local_outer))
        sent = grad_ref[:, row, part].reshape(width, points)
        grad = lax.dot_general(eye, sent, both_last, preferred_element_type=jnp.float32)
        made = moved(grad, spec_ref[part, row], first_ref[part, row], second_ref[part, row])
        for index in range(3):
            if order < early_blocks:
                ready[index][order] = made[index]
                copies.append(
                    pltpu.make_async_copy(
                        ready[index].at[order], final[index].at[part, row], leaving.at[index, order]
                    )
                )
                copies[-1].start()
            else:
                held[index][order - early_blocks] = made[index]
        turned = lax.dot_general(
            made[0].astype(jnp.bfloat16), eye, both_first, preferred_element_type=jnp.float32
        )
        out_ref[:, row, part] = turned.astype(jnp.bfloat16).reshape(grad_ref.shape[0], -1, points)
    for copy in copies:
        copy.wait()


def update_call(sent, spectrum, first_moment, second_moment):
    parts, local_outer, points, channels = spectrum.shape
    early = (early_blocks, points, channels)
    late = (parts * local_outer - early_blocks, points, channels)
    made = pl.pallas_call(
        update_kernel,
        in_specs=[whole, whole, whole, whole],
        out_specs=[outside] * 3 + [whole] * 4,
        out_shape=[jax.ShapeDtypeStruct(spectrum.shape, jnp.float32)] * 3
        + [jax.ShapeDtypeStruct(late, jnp.float32)] * 3
        + [jax.ShapeDtypeStruct(sent.shape, jnp.bfloat16)],
        scratch_shapes=[pltpu.VMEM(early, jnp.float32)] * 3 + [pltpu.SemaphoreType.DMA((3, early_blocks))],
        compiler_params=planned,
        name="update",
    )(sent, spectrum, first_moment, second_moment)
    return (made[:3], made[3:6]), made[6]


def inverse_kernel(spectra_ref, filter_ref, twist_ref, matrix_ref, *refs, chunk):
    held, out_ref, final, mid_ref, leaving = refs[:3], refs[6], refs[7:10], refs[10], refs[11]
    late = state_blocks(*final[0].shape[:2])[early_blocks:]
    pairs = [
        (source.at[order], target.at[part, row])
        for source, target in zip(held, final)
        for order, (part, row) in enumerate(late)
    ]
    copies = copies_of(pairs, leaving, 1)
    for copy in copies:
        copy.start()
    sequences, segments, narrow, points = out_ref.shape
    rows = sequences * narrow

    def mixed(residue, paired):
        filter_re = filter_ref[residue, 0].astype(jnp.float32)
        filter_im = filter_ref[residue, 1].astype(jnp.float32)
        if paired:
            filter_re = filter_re + filter_ref[2 * segments - residue, 0].astype(jnp.float32)
            filter_im = filter_im - filter_ref[2 * segments - residue, 1].astype(jnp.float32)
        signal_re = spectra_ref[residue, 0].reshape(sequences, narrow, points)
        signal_im = spectra_ref[residue, 1].reshape(sequences, narrow, points)
        mixed_re = (signal_re * filter_re - signal_im * filter_im).reshape(rows, points)
        mixed_im = (signal_re * filter_im + signal_im * filter_re).reshape(rows, points)
        return jnp.concatenate([mixed_re.astype(jnp.bfloat16), mixed_im.astype(jnp.bfloat16)], axis=1)

    def emit(base, count, paired):
        values = jnp.concatenate([mixed(base + extra, paired) for extra in range(count)], axis=0)
        full = jnp.dot(values, matrix_ref[...], preferred_element_type=jnp.float32).reshape(count, rows, 2 * points)
        for extra in range(count):
            residue = base + extra
            cos = twist_ref[residue, 0:1]
            sin = twist_ref[residue, 1:2]
            mid_ref[residue, 0] = full[extra, :, :points] * cos - full[extra, :, points:] * sin
            mid_ref[residue, 1] = full[extra, :, :points] * sin + full[extra, :, points:] * cos

    over_chunks(emit, segments, chunk)
    tiles = narrow // sub

    def tile_step(step, carry):
        which = step // tiles
        start = pl.multiple_of((step % tiles) * sub, sub)
        source = pl.multiple_of(step * sub, sub)
        for left in range(0, points, lane):
            here = slice(left, left + lane)
            bins = [
                tuple(mid_ref[index, part, pl.ds(source, sub), here] for part in range(2))
                for index in range(segments + 1)
            ]
            for seg, value in enumerate(real_segments(bins)):
                out_ref[which, seg, pl.ds(start, sub), here] = value.astype(jnp.bfloat16)
        return carry

    lax.fori_loop(0, sequences * tiles, tile_step, 0)
    for copy in copies:
        copy.wait()


def inverse_call(spectra, filters, twist, matrices, states):
    final, held = states
    residues, _, rows, points = spectra.shape
    segments = residues - 1
    narrow = filters.shape[2]
    sequences = rows // narrow
    out, *final = pl.pallas_call(
        functools.partial(inverse_kernel, chunk=8),
        in_specs=[whole] * 7 + [outside] * 3,
        out_specs=[whole] + [outside] * 3,
        out_shape=[jax.ShapeDtypeStruct((sequences, segments, narrow, points), jnp.bfloat16)]
        + [jax.ShapeDtypeStruct(state.shape, state.dtype) for state in final],
        input_output_aliases={7: 1, 8: 2, 9: 3},
        scratch_shapes=[
            pltpu.VMEM((residues, 2, rows, points), jnp.float32),
            pltpu.SemaphoreType.DMA((3 * held[0].shape[0], 1)),
        ],
        compiler_params=roomy,
        name="inverse",
    )(spectra, filters, twist, matrices, *held, *final)
    return out, final


def pack_plain(signal, cotangent, narrow):
    points, channels = signal.shape
    both = jnp.stack([signal, cotangent]).reshape(2, points, channels // narrow, narrow)
    return both.transpose(2, 0, 3, 1).reshape(channels // narrow, 2 * narrow, points)


def forward_plain(arrived, twist, matrices):
    sequences, segments, pair_rows, points = arrived.shape
    narrow = pair_rows // 2
    rows = sequences * narrow
    parts = arrived.reshape(sequences, segments, 2, narrow, points).astype(jnp.float32)
    parts = parts.transpose(1, 2, 0, 3, 4).reshape(segments, 2 * rows, points)
    bins = half_spectrum([parts[seg] for seg in range(segments)])
    re = jnp.stack([item[0] for item in bins])
    im = jnp.stack([jnp.zeros_like(item[0]) if item[1] is None else item[1] for item in bins])
    cos, sin = twist[:, 0][:, None], twist[:, 1][:, None]
    mid = jnp.concatenate([re * cos + im * sin, im * cos - re * sin], axis=2).astype(jnp.bfloat16)
    full = jnp.dot(mid, matrices, preferred_element_type=jnp.float32)
    signal_re, signal_im = full[:, :rows, :points], full[:, :rows, points:]
    cotan_re, cotan_im = full[:, rows:, :points], full[:, rows:, points:]
    shape = (segments + 1, sequences, narrow, points)
    scale = 1.0 / (2 * segments * points)
    real = jnp.sum((signal_re * cotan_re + signal_im * cotan_im).reshape(shape), axis=1) * scale
    imag = jnp.sum((signal_re * cotan_im - signal_im * cotan_re).reshape(shape), axis=1) * scale
    real = jnp.concatenate([real, real[1:segments][::-1]])
    imag = jnp.concatenate([imag, -imag[1:segments][::-1]])
    grad = jnp.stack([real, imag], axis=1).astype(jnp.bfloat16)
    return grad, jnp.stack([signal_re, signal_im], axis=1)


def mirrored_rows(local_outer):
    rows = jnp.arange(local_outer, dtype=jnp.int32)
    return is_mirrored(rows, local_outer)[None, :, None, None]


def gradient_plain(sent, shape):
    arrived = sent.astype(jnp.float32).transpose(2, 1, 4, 0, 3).reshape(shape)
    return jnp.where(mirrored_rows(shape[1]), arrived[:, :, ::-1], arrived)


def update_plain(sent, spectrum, first_moment, second_moment):
    groups, local_outer, _, narrow, points = sent.shape
    grad = gradient_plain(sent, spectrum.shape)
    new_spec, new_first, new_second = moved(grad, spectrum, first_moment, second_moment)
    out = jnp.where(mirrored_rows(local_outer), new_spec[:, :, ::-1], new_spec).astype(jnp.bfloat16)
    out = out.reshape(2, local_outer, points, groups, narrow).transpose(3, 1, 0, 4, 2)
    return (new_spec, new_first, new_second), out


def inverse_plain(spectra, filters, twist, matrices, states):
    residues, _, rows, points = spectra.shape
    segments = residues - 1
    narrow = filters.shape[2]
    sequences = rows // narrow
    wide = filters.astype(jnp.float32)
    mirrored = jnp.concatenate([jnp.zeros_like(wide[:1]), wide[segments + 1 :][::-1], jnp.zeros_like(wide[:1])])
    filter_re = (wide[: segments + 1, 0] + mirrored[:, 0])[:, None]
    filter_im = (wide[: segments + 1, 1] - mirrored[:, 1])[:, None]
    shape = (residues, sequences, narrow, points)
    signal_re, signal_im = spectra[:, 0].reshape(shape), spectra[:, 1].reshape(shape)
    mixed_re = (signal_re * filter_re - signal_im * filter_im).reshape(residues, rows, points)
    mixed_im = (signal_re * filter_im + signal_im * filter_re).reshape(residues, rows, points)
    mixed = jnp.concatenate([mixed_re, mixed_im], axis=2).astype(jnp.bfloat16)
    full = jnp.dot(mixed, matrices, preferred_element_type=jnp.float32)
    cos, sin = twist[:, 0][:, None], twist[:, 1][:, None]
    mid_re = full[..., :points] * cos - full[..., points:] * sin
    mid_im = full[..., :points] * sin + full[..., points:] * cos
    out = jnp.stack(real_segments([(mid_re[index], mid_im[index]) for index in range(residues)]))
    out = out.reshape(segments, sequences, narrow, points).transpose(1, 0, 2, 3)
    return out.astype(jnp.bfloat16), states


def per_device(inputs, grad_out, spectrum, first_moment, second_moment):
    seq_count = lax.axis_size("seq")
    batch_count = lax.axis_size("batch")
    batch_rows, points, channels = inputs.shape
    narrow = channels // (seq_count * batch_count)
    local_outer = spectrum.shape[1]
    outer = 2 * seq_count
    tiled = narrow % sub == 0 and points % lane == 0 and batch_rows == 1
    twist = jnp.asarray(twist_table(outer, points))
    ahead, back = point_matrices(points, 1.0 / (outer * points))
    ahead, back = jnp.asarray(ahead, jnp.bfloat16), jnp.asarray(back, jnp.bfloat16)

    pack = pack_call if tiled else pack_plain
    packed = jnp.stack([pack(inputs[row], grad_out[row], narrow) for row in range(batch_rows)], axis=1)
    arrived = lax.all_to_all(packed, ("batch", "seq"), split_axis=0, concat_axis=0, tiled=True)
    arrived = arrived.reshape(batch_count, seq_count, batch_rows, 2 * narrow, points)
    arrived = arrived.transpose(0, 2, 1, 3, 4).reshape(-1, seq_count, 2 * narrow, points)
    sequences = arrived.shape[0]

    grad, spectra = (forward_call if tiled else forward_plain)(arrived, twist, ahead)
    grad = grad.reshape(seq_count, local_outer, 2, narrow, points)
    sent = lax.all_to_all(grad, "seq", split_axis=0, concat_axis=0, tiled=True)

    update = update_call if tiled else update_plain
    states, filters = update(sent, spectrum, first_moment, second_moment)
    filters = lax.all_to_all(filters, "seq", split_axis=0, concat_axis=0, tiled=True)
    filters = filters.reshape(outer, 2, narrow, points)

    rows, states = (inverse_call if tiled else inverse_plain)(spectra, filters, twist, back, states)
    rows = rows.reshape(batch_count, batch_rows, seq_count, narrow, points).transpose(0, 2, 1, 3, 4)
    rows = rows.reshape(batch_count * seq_count, batch_rows, narrow, points)
    rows = lax.all_to_all(rows, ("batch", "seq"), split_axis=0, concat_axis=0, tiled=True)
    if tiled:
        filtered = unpack_call(rows.reshape(channels, points))[None]
    else:
        filtered = rows.transpose(1, 3, 0, 2).reshape(batch_rows, points, channels)
    return *states, filtered


def solution(mesh):
    return jax.shard_map(
        per_device,
        mesh=mesh,
        in_specs=(
            P("batch", "seq", None),
            P("batch", "seq", None),
            P(None, "seq", None, "batch"),
            P(None, "seq", None, "batch"),
            P(None, "seq", None, "batch"),
        ),
        out_specs=(
            P(None, "seq", None, "batch"),
            P(None, "seq", None, "batch"),
            P(None, "seq", None, "batch"),
            P("batch", "seq", None),
        ),
        check_vma=False,
    )
```

```python
import functools
import math

import jax
import jax.numpy as jnp
import numpy as np
from jax import lax
from jax.experimental import pallas as pl
from jax.experimental.pallas import tpu as pltpu
from jax.sharding import PartitionSpec as P

step_rate = 0.5
epsilon = 1e-06
sub = 16
lane = 128


def turn_table(numer, modulus):
    phase = 2.0 * math.pi * (numer % modulus) / modulus
    return np.cos(phase), np.sin(phase)


def twist_table(outer, points):
    half = outer // 2
    index = np.arange(half + 1)[:, None] * np.arange(points)[None, :]
    cos, sin = turn_table(index, outer * points)
    return np.stack([cos, sin], axis=1).astype(np.float32)


def point_matrices(points, scale_back):
    index = np.arange(points)[:, None] * np.arange(points)[None, :]
    cos, sin = turn_table(index, points)
    ahead = np.block([[cos, -sin], [sin, cos]])
    back = np.block([[cos, sin], [-sin, cos]]) * scale_back
    return ahead.astype(np.float32), back.astype(np.float32)


def times_phase(re, im, turns, count):
    if turns == 0:
        return re, im
    if 4 * turns == count:
        return im, -re
    cos = math.cos(2.0 * math.pi * turns / count)
    sin = math.sin(2.0 * math.pi * turns / count)
    return re * cos + im * sin, im * cos - re * sin


def half_spectrum(values):
    total = 2 * len(values)
    if total == 2:
        return [(values[0], None), (values[0], None)]
    even = half_spectrum(values[0::2])
    odd = half_spectrum(values[1::2])
    quarter = total // 4
    out = [None] * (total // 2 + 1)
    for index in range(quarter + 1):
        even_re, even_im = even[index]
        odd_re, odd_im = odd[index]
        if index == 0:
            out[0] = (even_re + odd_re, None)
            out[total // 2] = (even_re - odd_re, None)
        elif index == quarter:
            out[index] = (even_re, -odd_re)
        else:
            turned_re, turned_im = times_phase(odd_re, odd_im, index, total)
            out[index] = (even_re + turned_re, even_im + turned_im)
            out[total // 2 - index] = (even_re - turned_re, turned_im - even_im)
    return out


def real_segments(bins):
    count = 2 * (len(bins) - 1)
    if count == 2:
        return [bins[0][0] + bins[1][0]]
    quarter = count // 4
    even = [None] * (quarter + 1)
    odd = [None] * (quarter + 1)
    for index in range(quarter + 1):
        low_re, low_im = bins[index]
        high_re, high_im = bins[count // 2 - index]
        if index == 0:
            even[0] = (low_re + high_re, None)
            odd[0] = (low_re - high_re, None)
        elif index == quarter:
            even[index] = (low_re, None)
            odd[index] = (-low_im, None)
        else:
            even[index] = (low_re + high_re, low_im - high_im)
            diff_re, diff_im = low_re - high_re, low_im + high_im
            cos = math.cos(2.0 * math.pi * index / count)
            sin = math.sin(2.0 * math.pi * index / count)
            odd[index] = (diff_re * cos - diff_im * sin, diff_re * sin + diff_im * cos)
    first = real_segments(even)
    second = real_segments(odd)
    return [item for pair in zip(first, second) for item in pair]


both_last = (((1,), (1,)), ((), ()))
both_first = (((0,), (0,)), ((), ()))


def square_eye(points, flipped):
    row = lax.broadcasted_iota(jnp.int32, (points, points), 0)
    col = lax.broadcasted_iota(jnp.int32, (points, points), 1)
    picked = jnp.where(flipped, points - 1 - col, col)
    return jnp.where(row == picked, 1.0, 0.0).astype(jnp.bfloat16)


whole = pl.BlockSpec(memory_space=pltpu.VMEM)
outside = pl.BlockSpec(memory_space=pl.ANY)
roomy = pltpu.CompilerParams(vmem_limit_bytes=24 << 20)
planned = pltpu.CompilerParams(vmem_limit_bytes=24 << 20)


def copies_of(pairs, marks, pieces):
    made = []
    for index, (source, target) in enumerate(pairs):
        length = source.shape[0] // pieces
        for piece in range(pieces):
            here = slice(piece * length, (piece + 1) * length)
            made.append(pltpu.make_async_copy(source.at[here], target.at[here], marks.at[index, piece]))
    return made


def pack_kernel(signal_hbm, cotangent_hbm, out_ref, held_ref, arrival, *, narrow):
    points, channels = signal_hbm.shape
    sources = (signal_hbm, cotangent_hbm)
    copies = copies_of([(source, held_ref.at[part]) for part, source in enumerate(sources)], arrival, 1)
    for copy in copies:
        copy.start()
    for part in range(2):
        for copy in copies[part : part + 1]:
            copy.wait()
        turned = held_ref[part].T.reshape(channels // narrow, narrow, points)
        out_ref[:, part * narrow : (part + 1) * narrow, :] = turned


def pack_call(signal, cotangent, narrow):
    points, channels = signal.shape
    signal = pltpu.with_memory_space_constraint(signal, pltpu.HBM)
    cotangent = pltpu.with_memory_space_constraint(cotangent, pltpu.HBM)
    return pl.pallas_call(
        functools.partial(pack_kernel, narrow=narrow),
        in_specs=[pl.BlockSpec(memory_space=pltpu.HBM)] * 2,
        out_specs=whole,
        out_shape=jax.ShapeDtypeStruct((channels // narrow, 2 * narrow, points), jnp.bfloat16),
        scratch_shapes=[
            pltpu.VMEM((2, points, channels), jnp.bfloat16),
            pltpu.SemaphoreType.DMA((2, 1)),
        ],
        compiler_params=roomy,
        name="pack",
    )(signal, cotangent)


def unpack_kernel(in_ref, out_hbm, held_ref, leaving):
    channels, points = in_ref.shape
    length = points // 2
    copies = copies_of([(held_ref, out_hbm)], leaving, 2)
    for piece, copy in enumerate(copies):
        here = slice(piece * length, (piece + 1) * length)
        held_ref[here, :] = in_ref[:, here].T
        copy.start()
    for copy in copies:
        copy.wait()


def unpack_call(rows):
    channels, points = rows.shape
    return pl.pallas_call(
        unpack_kernel,
        in_specs=[whole],
        out_specs=pl.BlockSpec(memory_space=pl.ANY),
        out_shape=jax.ShapeDtypeStruct((points, channels), jnp.bfloat16),
        scratch_shapes=[pltpu.VMEM((points, channels), jnp.bfloat16), pltpu.SemaphoreType.DMA((1, 2))],
        compiler_params=roomy,
        name="unpack",
    )(rows)


def over_chunks(emit, segments, chunk):
    emit(0, 1, False)
    emit(segments, 1, False)
    count = (segments - 1) // chunk

    def step(index, carry):
        emit(1 + index * chunk, chunk, True)
        return carry

    lax.fori_loop(0, count, step, 0)
    if (segments - 1) % chunk:
        emit(1 + count * chunk, (segments - 1) % chunk, True)


def forward_kernel(in_ref, twist_ref, matrix_ref, grad_ref, spectra_ref, *mid_refs, scale, chunk):
    sequences, segments, pair_rows, points = in_ref.shape
    narrow = pair_rows // 2
    rows = sequences * sub
    residues = segments + 1

    def sums(group, step, left):
        signal, which = step // sequences, step % sequences
        start = pl.multiple_of(signal * narrow + group * sub, sub)
        target = pl.multiple_of(step * sub, sub)
        here = slice(left, left + lane)
        after = slice(points + left, points + left + lane)
        values = [in_ref[which, seg, pl.ds(start, sub), here].astype(jnp.float32) for seg in range(segments)]
        for index, (re, im) in enumerate(half_spectrum(values)):
            cos = twist_ref[index, 0:1, here]
            sin = twist_ref[index, 1:2, here]
            if im is None:
                new_re, new_im = re * cos, -(re * sin)
            else:
                new_re, new_im = re * cos + im * sin, im * cos - re * sin
            mid_refs[group][index, pl.ds(target, sub), here] = new_re.astype(jnp.bfloat16)
            mid_refs[group][index, pl.ds(target, sub), after] = new_im.astype(jnp.bfloat16)

    def emit(group, base, count):
        values = mid_refs[group][base : base + count].reshape(count * 2 * rows, 2 * points)
        full = jnp.dot(values, matrix_ref[...], preferred_element_type=jnp.float32)
        full = full.reshape(count, 2 * rows, 2 * points)
        mine = slice(group * sub, (group + 1) * sub)
        for extra in range(count):
            residue = base + extra
            signal_re, signal_im = full[extra, :rows, :points], full[extra, :rows, points:]
            cotan_re, cotan_im = full[extra, rows:, :points], full[extra, rows:, points:]
            for which in range(sequences):
                part = slice(which * sub, (which + 1) * sub)
                there = slice(which * narrow + group * sub, which * narrow + (group + 1) * sub)
                spectra_ref[residue, 0, there] = signal_re[part]
                spectra_ref[residue, 1, there] = signal_im[part]
            real_term = signal_re * cotan_re + signal_im * cotan_im
            imag_term = signal_re * cotan_im - signal_im * cotan_re
            real_sum = jnp.sum(real_term.reshape(sequences, sub, points), axis=0) * scale
            imag_sum = jnp.sum(imag_term.reshape(sequences, sub, points), axis=0) * scale
            grad_ref[residue, 0, mine] = real_sum.astype(jnp.bfloat16)
            grad_ref[residue, 1, mine] = imag_sum.astype(jnp.bfloat16)
            if 0 < residue < segments:
                grad_ref[2 * segments - residue, 0, mine] = real_sum.astype(jnp.bfloat16)
                grad_ref[2 * segments - residue, 1, mine] = (-imag_sum).astype(jnp.bfloat16)

    def tile_step(step, carry):
        for left in range(0, points, lane):
            sums(0, step, left)
        return carry

    lax.fori_loop(0, 2 * sequences, tile_step, 0, unroll=True)
    groups = narrow // sub
    pieces = [(base, min(chunk, residues - base)) for base in range(0, residues, chunk)]
    for group in range(groups):
        coming = [(step, left) for step in range(2 * sequences) for left in range(0, points, lane)]
        coming = coming if group + 1 < groups else []
        each = -(-len(coming) // len(pieces))
        for number, (base, count) in enumerate(pieces):
            for step, left in coming[number * each : (number + 1) * each]:
                sums(group + 1, step, left)
            emit(group, base, count)


def forward_call(arrived, twist, matrices):
    sequences, segments, pair_rows, points = arrived.shape
    narrow = pair_rows // 2
    outer = 2 * segments
    rows = sequences * narrow
    return pl.pallas_call(
        functools.partial(forward_kernel, scale=1.0 / (outer * points), chunk=2 * outer),
        in_specs=[whole, whole, whole],
        out_specs=[whole, whole],
        out_shape=[
            jax.ShapeDtypeStruct((outer, 2, narrow, points), jnp.bfloat16),
            jax.ShapeDtypeStruct((segments + 1, 2, rows, points), jnp.float32),
        ],
        scratch_shapes=[pltpu.VMEM((segments + 1, 2 * sequences * sub, 2 * points), jnp.bfloat16)]
        * (narrow // sub),
        compiler_params=roomy,
        name="forward",
    )(arrived, twist, matrices)


def moved(grad, spec, first, second):
    new_first = 0.9 * first + 0.1 * grad
    new_second = 0.99 * second + 0.01 * grad * grad
    root = new_second * lax.rsqrt(new_second)
    return spec - step_rate * jnp.tanh(new_first / (root + epsilon)), new_first, new_second


def is_mirrored(row, local_outer):
    return lax.axis_index("seq") * local_outer + row > lax.axis_size("seq")


early_blocks = 2


def state_blocks(parts, local_outer):
    return [(part, row) for row in range(local_outer) for part in range(parts)]


def update_kernel(grad_ref, spec_ref, first_ref, second_ref, *refs):
    final, held, (out_ref, *ready, leaving) = refs[:3], refs[3:6], refs[6:]
    parts, local_outer, points, width = spec_ref.shape
    copies = []
    for order, (part, row) in enumerate(state_blocks(parts, local_outer)):
        if part == 0:
            eye = square_eye(points, is_mirrored(row, local_outer))
        sent = grad_ref[:, row, part].reshape(width, points)
        grad = lax.dot_general(eye, sent, both_last, preferred_element_type=jnp.float32)
        made = moved(grad, spec_ref[part, row], first_ref[part, row], second_ref[part, row])
        for index in range(3):
            if order < early_blocks:
                ready[index][order] = made[index]
                copies.append(
                    pltpu.make_async_copy(
                        ready[index].at[order], final[index].at[part, row], leaving.at[index, order]
                    )
                )
                copies[-1].start()
            else:
                held[index][order - early_blocks] = made[index]
        turned = lax.dot_general(
            made[0].astype(jnp.bfloat16), eye, both_first, preferred_element_type=jnp.float32
        )
        out_ref[:, row, part] = turned.astype(jnp.bfloat16).reshape(grad_ref.shape[0], -1, points)
    for copy in copies:
        copy.wait()


def update_call(sent, spectrum, first_moment, second_moment):
    parts, local_outer, points, channels = spectrum.shape
    early = (early_blocks, points, channels)
    late = (parts * local_outer - early_blocks, points, channels)
    made = pl.pallas_call(
        update_kernel,
        in_specs=[whole, whole, whole, whole],
        out_specs=[outside] * 3 + [whole] * 4,
        out_shape=[jax.ShapeDtypeStruct(spectrum.shape, jnp.float32)] * 3
        + [jax.ShapeDtypeStruct(late, jnp.float32)] * 3
        + [jax.ShapeDtypeStruct(sent.shape, jnp.bfloat16)],
        scratch_shapes=[pltpu.VMEM(early, jnp.float32)] * 3 + [pltpu.SemaphoreType.DMA((3, early_blocks))],
        compiler_params=planned,
        name="update",
    )(sent, spectrum, first_moment, second_moment)
    return (made[:3], made[3:6]), made[6]


def inverse_kernel(spectra_ref, filter_ref, twist_ref, matrix_ref, *refs, chunk):
    held, out_ref, final, mid_ref, leaving = refs[:3], refs[6], refs[7:10], refs[10], refs[11]
    late = state_blocks(*final[0].shape[:2])[early_blocks:]
    pairs = [
        (source.at[order], target.at[part, row])
        for source, target in zip(held, final)
        for order, (part, row) in enumerate(late)
    ]
    copies = copies_of(pairs, leaving, 1)
    for copy in copies:
        copy.start()
    sequences, segments, narrow, points = out_ref.shape
    rows = sequences * narrow

    def mixed(residue, paired):
        filter_re = filter_ref[residue, 0].astype(jnp.float32)
        filter_im = filter_ref[residue, 1].astype(jnp.float32)
        if paired:
            filter_re = filter_re + filter_ref[2 * segments - residue, 0].astype(jnp.float32)
            filter_im = filter_im - filter_ref[2 * segments - residue, 1].astype(jnp.float32)
        signal_re = spectra_ref[residue, 0].reshape(sequences, narrow, points)
        signal_im = spectra_ref[residue, 1].reshape(sequences, narrow, points)
        mixed_re = (signal_re * filter_re - signal_im * filter_im).reshape(rows, points)
        mixed_im = (signal_re * filter_im + signal_im * filter_re).reshape(rows, points)
        return jnp.concatenate([mixed_re.astype(jnp.bfloat16), mixed_im.astype(jnp.bfloat16)], axis=1)

    def emit(base, count, paired):
        values = jnp.concatenate([mixed(base + extra, paired) for extra in range(count)], axis=0)
        full = jnp.dot(values, matrix_ref[...], preferred_element_type=jnp.float32).reshape(count, rows, 2 * points)
        for extra in range(count):
            residue = base + extra
            cos = twist_ref[residue, 0:1]
            sin = twist_ref[residue, 1:2]
            mid_ref[residue, 0] = full[extra, :, :points] * cos - full[extra, :, points:] * sin
            mid_ref[residue, 1] = full[extra, :, :points] * sin + full[extra, :, points:] * cos

    over_chunks(emit, segments, chunk)
    tiles = narrow // sub

    def tile_step(step, carry):
        which = step // tiles
        start = pl.multiple_of((step % tiles) * sub, sub)
        source = pl.multiple_of(step * sub, sub)
        for left in range(0, points, lane):
            here = slice(left, left + lane)
            bins = [
                tuple(mid_ref[index, part, pl.ds(source, sub), here] for part in range(2))
                for index in range(segments + 1)
            ]
            for seg, value in enumerate(real_segments(bins)):
                out_ref[which, seg, pl.ds(start, sub), here] = value.astype(jnp.bfloat16)
        return carry

    lax.fori_loop(0, sequences * tiles, tile_step, 0)
    for copy in copies:
        copy.wait()


def inverse_call(spectra, filters, twist, matrices, states):
    final, held = states
    residues, _, rows, points = spectra.shape
    segments = residues - 1
    narrow = filters.shape[2]
    sequences = rows // narrow
    out, *final = pl.pallas_call(
        functools.partial(inverse_kernel, chunk=8),
        in_specs=[whole] * 7 + [outside] * 3,
        out_specs=[whole] + [outside] * 3,
        out_shape=[jax.ShapeDtypeStruct((sequences, segments, narrow, points), jnp.bfloat16)]
        + [jax.ShapeDtypeStruct(state.shape, state.dtype) for state in final],
        input_output_aliases={7: 1, 8: 2, 9: 3},
        scratch_shapes=[
            pltpu.VMEM((residues, 2, rows, points), jnp.float32),
            pltpu.SemaphoreType.DMA((3 * held[0].shape[0], 1)),
        ],
        compiler_params=roomy,
        name="inverse",
    )(spectra, filters, twist, matrices, *held, *final)
    return out, final


def pack_plain(signal, cotangent, narrow):
    points, channels = signal.shape
    both = jnp.stack([signal, cotangent]).reshape(2, points, channels // narrow, narrow)
    return both.transpose(2, 0, 3, 1).reshape(channels // narrow, 2 * narrow, points)


def forward_plain(arrived, twist, matrices):
    sequences, segments, pair_rows, points = arrived.shape
    narrow = pair_rows // 2
    rows = sequences * narrow
    parts = arrived.reshape(sequences, segments, 2, narrow, points).astype(jnp.float32)
    parts = parts.transpose(1, 2, 0, 3, 4).reshape(segments, 2 * rows, points)
    bins = half_spectrum([parts[seg] for seg in range(segments)])
    re = jnp.stack([item[0] for item in bins])
    im = jnp.stack([jnp.zeros_like(item[0]) if item[1] is None else item[1] for item in bins])
    cos, sin = twist[:, 0][:, None], twist[:, 1][:, None]
    mid = jnp.concatenate([re * cos + im * sin, im * cos - re * sin], axis=2).astype(jnp.bfloat16)
    full = jnp.dot(mid, matrices, preferred_element_type=jnp.float32)
    signal_re, signal_im = full[:, :rows, :points], full[:, :rows, points:]
    cotan_re, cotan_im = full[:, rows:, :points], full[:, rows:, points:]
    shape = (segments + 1, sequences, narrow, points)
    scale = 1.0 / (2 * segments * points)
    real = jnp.sum((signal_re * cotan_re + signal_im * cotan_im).reshape(shape), axis=1) * scale
    imag = jnp.sum((signal_re * cotan_im - signal_im * cotan_re).reshape(shape), axis=1) * scale
    real = jnp.concatenate([real, real[1:segments][::-1]])
    imag = jnp.concatenate([imag, -imag[1:segments][::-1]])
    grad = jnp.stack([real, imag], axis=1).astype(jnp.bfloat16)
    return grad, jnp.stack([signal_re, signal_im], axis=1)


def mirrored_rows(local_outer):
    rows = jnp.arange(local_outer, dtype=jnp.int32)
    return is_mirrored(rows, local_outer)[None, :, None, None]


def gradient_plain(sent, shape):
    arrived = sent.astype(jnp.float32).transpose(2, 1, 4, 0, 3).reshape(shape)
    return jnp.where(mirrored_rows(shape[1]), arrived[:, :, ::-1], arrived)


def update_plain(sent, spectrum, first_moment, second_moment):
    groups, local_outer, _, narrow, points = sent.shape
    grad = gradient_plain(sent, spectrum.shape)
    new_spec, new_first, new_second = moved(grad, spectrum, first_moment, second_moment)
    out = jnp.where(mirrored_rows(local_outer), new_spec[:, :, ::-1], new_spec).astype(jnp.bfloat16)
    out = out.reshape(2, local_outer, points, groups, narrow).transpose(3, 1, 0, 4, 2)
    return (new_spec, new_first, new_second), out


def inverse_plain(spectra, filters, twist, matrices, states):
    residues, _, rows, points = spectra.shape
    segments = residues - 1
    narrow = filters.shape[2]
    sequences = rows // narrow
    wide = filters.astype(jnp.float32)
    mirrored = jnp.concatenate([jnp.zeros_like(wide[:1]), wide[segments + 1 :][::-1], jnp.zeros_like(wide[:1])])
    filter_re = (wide[: segments + 1, 0] + mirrored[:, 0])[:, None]
    filter_im = (wide[: segments + 1, 1] - mirrored[:, 1])[:, None]
    shape = (residues, sequences, narrow, points)
    signal_re, signal_im = spectra[:, 0].reshape(shape), spectra[:, 1].reshape(shape)
    mixed_re = (signal_re * filter_re - signal_im * filter_im).reshape(residues, rows, points)
    mixed_im = (signal_re * filter_im + signal_im * filter_re).reshape(residues, rows, points)
    mixed = jnp.concatenate([mixed_re, mixed_im], axis=2).astype(jnp.bfloat16)
    full = jnp.dot(mixed, matrices, preferred_element_type=jnp.float32)
    cos, sin = twist[:, 0][:, None], twist[:, 1][:, None]
    mid_re = full[..., :points] * cos - full[..., points:] * sin
    mid_im = full[..., :points] * sin + full[..., points:] * cos
    out = jnp.stack(real_segments([(mid_re[index], mid_im[index]) for index in range(residues)]))
    out = out.reshape(segments, sequences, narrow, points).transpose(1, 0, 2, 3)
    return out.astype(jnp.bfloat16), states


def per_device(inputs, grad_out, spectrum, first_moment, second_moment):
    seq_count = lax.axis_size("seq")
    batch_count = lax.axis_size("batch")
    batch_rows, points, channels = inputs.shape
    narrow = channels // (seq_count * batch_count)
    local_outer = spectrum.shape[1]
    outer = 2 * seq_count
    tiled = narrow % sub == 0 and points % lane == 0 and batch_rows == 1
    twist = jnp.asarray(twist_table(outer, points))
    ahead, back = point_matrices(points, 1.0 / (outer * points))
    ahead, back = jnp.asarray(ahead, jnp.bfloat16), jnp.asarray(back, jnp.bfloat16)

    pack = pack_call if tiled else pack_plain
    packed = jnp.stack([pack(inputs[row], grad_out[row], narrow) for row in range(batch_rows)], axis=1)
    arrived = lax.all_to_all(packed, ("batch", "seq"), split_axis=0, concat_axis=0, tiled=True)
    arrived = arrived.reshape(batch_count, seq_count, batch_rows, 2 * narrow, points)
    arrived = arrived.transpose(0, 2, 1, 3, 4).reshape(-1, seq_count, 2 * narrow, points)
    sequences = arrived.shape[0]

    grad, spectra = (forward_call if tiled else forward_plain)(arrived, twist, ahead)
    grad = grad.reshape(seq_count, local_outer, 2, narrow, points)
    sent = lax.all_to_all(grad, "seq", split_axis=0, concat_axis=0, tiled=True)

    update = update_call if tiled else update_plain
    states, filters = update(sent, spectrum, first_moment, second_moment)
    filters = lax.all_to_all(filters, "seq", split_axis=0, concat_axis=0, tiled=True)
    filters = filters.reshape(outer, 2, narrow, points)

    rows, states = (inverse_call if tiled else inverse_plain)(spectra, filters, twist, back, states)
    rows = rows.reshape(batch_count, batch_rows, seq_count, narrow, points).transpose(0, 2, 1, 3, 4)
    rows = rows.reshape(batch_count * seq_count, batch_rows, narrow, points)
    rows = lax.all_to_all(rows, ("batch", "seq"), split_axis=0, concat_axis=0, tiled=True)
    if tiled:
        filtered = unpack_call(rows.reshape(channels, points))[None]
    else:
        filtered = rows.transpose(1, 3, 0, 2).reshape(batch_rows, points, channels)
    return *states, filtered


def solution(mesh):
    return jax.shard_map(
        per_device,
        mesh=mesh,
        in_specs=(
            P("batch", "seq", None),
            P("batch", "seq", None),
            P(None, "seq", None, "batch"),
            P(None, "seq", None, "batch"),
            P(None, "seq", None, "batch"),
        ),
        out_specs=(
            P(None, "seq", None, "batch"),
            P(None, "seq", None, "batch"),
            P(None, "seq", None, "batch"),
            P("batch", "seq", None),
        ),
        check_vma=False,
    )
```

```python
import functools
import math

import jax
import jax.numpy as jnp
import numpy as np
from jax import lax
from jax.experimental import pallas as pl
from jax.experimental.pallas import tpu as pltpu
from jax.sharding import PartitionSpec as P

step_rate = 0.5
epsilon = 1e-06
sub = 16
lane = 128


def turn_table(numer, modulus):
    phase = 2.0 * math.pi * (numer % modulus) / modulus
    return np.cos(phase), np.sin(phase)


def twist_table(outer, points):
    half = outer // 2
    index = np.arange(half + 1)[:, None] * np.arange(points)[None, :]
    cos, sin = turn_table(index, outer * points)
    return np.stack([cos, sin], axis=1).astype(np.float32)


def point_matrices(points, scale_back):
    index = np.arange(points)[:, None] * np.arange(points)[None, :]
    cos, sin = turn_table(index, points)
    ahead = np.block([[cos, -sin], [sin, cos]])
    back = np.block([[cos, sin], [-sin, cos]]) * scale_back
    return ahead.astype(np.float32), back.astype(np.float32)


def times_phase(re, im, turns, count):
    if turns == 0:
        return re, im
    if 4 * turns == count:
        return im, -re
    cos = math.cos(2.0 * math.pi * turns / count)
    sin = math.sin(2.0 * math.pi * turns / count)
    return re * cos + im * sin, im * cos - re * sin


def half_spectrum(values):
    total = 2 * len(values)
    if total == 2:
        return [(values[0], None), (values[0], None)]
    even = half_spectrum(values[0::2])
    odd = half_spectrum(values[1::2])
    quarter = total // 4
    out = [None] * (total // 2 + 1)
    for index in range(quarter + 1):
        even_re, even_im = even[index]
        odd_re, odd_im = odd[index]
        if index == 0:
            out[0] = (even_re + odd_re, None)
            out[total // 2] = (even_re - odd_re, None)
        elif index == quarter:
            out[index] = (even_re, -odd_re)
        else:
            turned_re, turned_im = times_phase(odd_re, odd_im, index, total)
            out[index] = (even_re + turned_re, even_im + turned_im)
            out[total // 2 - index] = (even_re - turned_re, turned_im - even_im)
    return out


def real_segments(bins):
    count = 2 * (len(bins) - 1)
    if count == 2:
        return [bins[0][0] + bins[1][0]]
    quarter = count // 4
    even = [None] * (quarter + 1)
    odd = [None] * (quarter + 1)
    for index in range(quarter + 1):
        low_re, low_im = bins[index]
        high_re, high_im = bins[count // 2 - index]
        if index == 0:
            even[0] = (low_re + high_re, None)
            odd[0] = (low_re - high_re, None)
        elif index == quarter:
            even[index] = (low_re, None)
            odd[index] = (-low_im, None)
        else:
            even[index] = (low_re + high_re, low_im - high_im)
            diff_re, diff_im = low_re - high_re, low_im + high_im
            cos = math.cos(2.0 * math.pi * index / count)
            sin = math.sin(2.0 * math.pi * index / count)
            odd[index] = (diff_re * cos - diff_im * sin, diff_re * sin + diff_im * cos)
    first = real_segments(even)
    second = real_segments(odd)
    return [item for pair in zip(first, second) for item in pair]


both_last = (((1,), (1,)), ((), ()))
both_first = (((0,), (0,)), ((), ()))


def square_eye(points, flipped):
    row = lax.broadcasted_iota(jnp.int32, (points, points), 0)
    col = lax.broadcasted_iota(jnp.int32, (points, points), 1)
    picked = jnp.where(flipped, points - 1 - col, col)
    return jnp.where(row == picked, 1.0, 0.0).astype(jnp.bfloat16)


whole = pl.BlockSpec(memory_space=pltpu.VMEM)
outside = pl.BlockSpec(memory_space=pl.ANY)
roomy = pltpu.CompilerParams(vmem_limit_bytes=24 << 20)
planned = pltpu.CompilerParams(vmem_limit_bytes=24 << 20)


def copies_of(pairs, marks, pieces):
    made = []
    for index, (source, target) in enumerate(pairs):
        length = source.shape[0] // pieces
        for piece in range(pieces):
            here = slice(piece * length, (piece + 1) * length)
            made.append(pltpu.make_async_copy(source.at[here], target.at[here], marks.at[index, piece]))
    return made


def pack_kernel(signal_hbm, cotangent_hbm, out_ref, held_ref, arrival, *, narrow):
    points, channels = signal_hbm.shape
    sources = (signal_hbm, cotangent_hbm)
    copies = copies_of([(source, held_ref.at[part]) for part, source in enumerate(sources)], arrival, 1)
    for copy in copies:
        copy.start()
    for part in range(2):
        for copy in copies[part : part + 1]:
            copy.wait()
        turned = held_ref[part].T.reshape(channels // narrow, narrow, points)
        out_ref[:, part * narrow : (part + 1) * narrow, :] = turned


def pack_call(signal, cotangent, narrow):
    points, channels = signal.shape
    signal = pltpu.with_memory_space_constraint(signal, pltpu.HBM)
    cotangent = pltpu.with_memory_space_constraint(cotangent, pltpu.HBM)
    return pl.pallas_call(
        functools.partial(pack_kernel, narrow=narrow),
        in_specs=[pl.BlockSpec(memory_space=pltpu.HBM)] * 2,
        out_specs=whole,
        out_shape=jax.ShapeDtypeStruct((channels // narrow, 2 * narrow, points), jnp.bfloat16),
        scratch_shapes=[
            pltpu.VMEM((2, points, channels), jnp.bfloat16),
            pltpu.SemaphoreType.DMA((2, 1)),
        ],
        compiler_params=roomy,
        name="pack",
    )(signal, cotangent)


def unpack_kernel(in_ref, out_hbm, held_ref, leaving):
    channels, points = in_ref.shape
    length = points // 2
    copies = copies_of([(held_ref, out_hbm)], leaving, 2)
    for piece, copy in enumerate(copies):
        here = slice(piece * length, (piece + 1) * length)
        held_ref[here, :] = in_ref[:, here].T
        copy.start()
    for copy in copies:
        copy.wait()


def unpack_call(rows):
    channels, points = rows.shape
    return pl.pallas_call(
        unpack_kernel,
        in_specs=[whole],
        out_specs=pl.BlockSpec(memory_space=pl.ANY),
        out_shape=jax.ShapeDtypeStruct((points, channels), jnp.bfloat16),
        scratch_shapes=[pltpu.VMEM((points, channels), jnp.bfloat16), pltpu.SemaphoreType.DMA((1, 2))],
        compiler_params=roomy,
        name="unpack",
    )(rows)


def over_chunks(emit, segments, chunk):
    emit(0, 1, False)
    emit(segments, 1, False)
    count = (segments - 1) // chunk

    def step(index, carry):
        emit(1 + index * chunk, chunk, True)
        return carry

    lax.fori_loop(0, count, step, 0)
    if (segments - 1) % chunk:
        emit(1 + count * chunk, (segments - 1) % chunk, True)


def forward_kernel(in_ref, twist_ref, matrix_ref, grad_ref, spectra_ref, *mid_refs, scale, chunk):
    sequences, segments, pair_rows, points = in_ref.shape
    narrow = pair_rows // 2
    rows = sequences * sub
    residues = segments + 1

    def sums(group, step, left):
        signal, which = step // sequences, step % sequences
        start = pl.multiple_of(signal * narrow + group * sub, sub)
        target = pl.multiple_of(step * sub, sub)
        here = slice(left, left + lane)
        after = slice(points + left, points + left + lane)
        values = [in_ref[which, seg, pl.ds(start, sub), here].astype(jnp.float32) for seg in range(segments)]
        for index, (re, im) in enumerate(half_spectrum(values)):
            cos = twist_ref[index, 0:1, here]
            sin = twist_ref[index, 1:2, here]
            if index == 0:
                new_re, new_im = re, jnp.zeros_like(re)
            elif im is None:
                new_re, new_im = re * cos, -(re * sin)
            else:
                new_re, new_im = re * cos + im * sin, im * cos - re * sin
            mid_refs[group][index, pl.ds(target, sub), here] = new_re.astype(jnp.bfloat16)
            mid_refs[group][index, pl.ds(target, sub), after] = new_im.astype(jnp.bfloat16)

    def emit(group, base, count):
        values = mid_refs[group][base : base + count].reshape(count * 2 * rows, 2 * points)
        full = jnp.dot(values, matrix_ref[...], preferred_element_type=jnp.float32)
        full = full.reshape(count, 2 * rows, 2 * points)
        mine = slice(group * sub, (group + 1) * sub)
        for extra in range(count):
            residue = base + extra
            signal_re, signal_im = full[extra, :rows, :points], full[extra, :rows, points:]
            cotan_re, cotan_im = full[extra, rows:, :points], full[extra, rows:, points:]
            for which in range(sequences):
                part = slice(which * sub, (which + 1) * sub)
                there = slice(which * narrow + group * sub, which * narrow + (group + 1) * sub)
                spectra_ref[residue, 0, there] = signal_re[part]
                spectra_ref[residue, 1, there] = signal_im[part]
            real_term = signal_re * cotan_re + signal_im * cotan_im
            imag_term = signal_re * cotan_im - signal_im * cotan_re
            real_sum = jnp.sum(real_term.reshape(sequences, sub, points), axis=0) * scale
            imag_sum = jnp.sum(imag_term.reshape(sequences, sub, points), axis=0) * scale
            grad_ref[residue, 0, mine] = real_sum.astype(jnp.bfloat16)
            grad_ref[residue, 1, mine] = imag_sum.astype(jnp.bfloat16)
            if 0 < residue < segments:
                grad_ref[2 * segments - residue, 0, mine] = real_sum.astype(jnp.bfloat16)
                grad_ref[2 * segments - residue, 1, mine] = (-imag_sum).astype(jnp.bfloat16)

    def tile_step(step, carry):
        for left in range(0, points, lane):
            sums(0, step, left)
        return carry

    lax.fori_loop(0, 2 * sequences, tile_step, 0, unroll=True)
    groups = narrow // sub
    pieces = [(base, min(chunk, residues - base)) for base in range(0, residues, chunk)]
    for group in range(groups):
        coming = [(step, left) for step in range(2 * sequences) for left in range(0, points, lane)]
        coming = coming if group + 1 < groups else []
        each = -(-len(coming) // len(pieces))
        for number, (base, count) in enumerate(pieces):
            for step, left in coming[number * each : (number + 1) * each]:
                sums(group + 1, step, left)
            emit(group, base, count)


def forward_call(arrived, twist, matrices):
    sequences, segments, pair_rows, points = arrived.shape
    narrow = pair_rows // 2
    outer = 2 * segments
    rows = sequences * narrow
    return pl.pallas_call(
        functools.partial(forward_kernel, scale=1.0 / (outer * points), chunk=2 * outer),
        in_specs=[whole, whole, whole],
        out_specs=[whole, whole],
        out_shape=[
            jax.ShapeDtypeStruct((outer, 2, narrow, points), jnp.bfloat16),
            jax.ShapeDtypeStruct((segments + 1, 2, rows, points), jnp.float32),
        ],
        scratch_shapes=[pltpu.VMEM((segments + 1, 2 * sequences * sub, 2 * points), jnp.bfloat16)]
        * (narrow // sub),
        compiler_params=roomy,
        name="forward",
    )(arrived, twist, matrices)


def moved(grad, spec, first, second):
    new_first = 0.9 * first + 0.1 * grad
    new_second = 0.99 * second + 0.01 * grad * grad
    root = new_second * lax.rsqrt(new_second)
    return spec - step_rate * jnp.tanh(new_first / (root + epsilon)), new_first, new_second


def is_mirrored(row, local_outer):
    return lax.axis_index("seq") * local_outer + row > lax.axis_size("seq")


early_blocks = 2


def state_blocks(parts, local_outer):
    return [(part, row) for row in range(local_outer) for part in range(parts)]


def update_kernel(grad_ref, spec_ref, first_ref, second_ref, *refs):
    final, held, (out_ref, *ready, leaving) = refs[:3], refs[3:6], refs[6:]
    parts, local_outer, points, width = spec_ref.shape
    copies = []
    for order, (part, row) in enumerate(state_blocks(parts, local_outer)):
        if part == 0:
            eye = square_eye(points, is_mirrored(row, local_outer))
        sent = grad_ref[:, row, part].reshape(width, points)
        grad = lax.dot_general(eye, sent, both_last, preferred_element_type=jnp.float32)
        made = moved(grad, spec_ref[part, row], first_ref[part, row], second_ref[part, row])
        for index in range(3):
            if order < early_blocks:
                ready[index][order] = made[index]
                copies.append(
                    pltpu.make_async_copy(
                        ready[index].at[order], final[index].at[part, row], leaving.at[index, order]
                    )
                )
                copies[-1].start()
            else:
                held[index][order - early_blocks] = made[index]
        turned = lax.dot_general(
            made[0].astype(jnp.bfloat16), eye, both_first, preferred_element_type=jnp.float32
        )
        out_ref[:, row, part] = turned.astype(jnp.bfloat16).reshape(grad_ref.shape[0], -1, points)
    for copy in copies:
        copy.wait()


def update_call(sent, spectrum, first_moment, second_moment):
    parts, local_outer, points, channels = spectrum.shape
    early = (early_blocks, points, channels)
    late = (parts * local_outer - early_blocks, points, channels)
    made = pl.pallas_call(
        update_kernel,
        in_specs=[whole, whole, whole, whole],
        out_specs=[outside] * 3 + [whole] * 4,
        out_shape=[jax.ShapeDtypeStruct(spectrum.shape, jnp.float32)] * 3
        + [jax.ShapeDtypeStruct(late, jnp.float32)] * 3
        + [jax.ShapeDtypeStruct(sent.shape, jnp.bfloat16)],
        scratch_shapes=[pltpu.VMEM(early, jnp.float32)] * 3 + [pltpu.SemaphoreType.DMA((3, early_blocks))],
        compiler_params=planned,
        name="update",
    )(sent, spectrum, first_moment, second_moment)
    return (made[:3], made[3:6]), made[6]


def inverse_kernel(spectra_ref, filter_ref, twist_ref, matrix_ref, *refs, chunk):
    held, out_ref, final, mid_ref, leaving = refs[:3], refs[6], refs[7:10], refs[10], refs[11]
    late = state_blocks(*final[0].shape[:2])[early_blocks:]
    pairs = [
        (source.at[order], target.at[part, row])
        for source, target in zip(held, final)
        for order, (part, row) in enumerate(late)
    ]
    copies = copies_of(pairs, leaving, 1)
    for copy in copies:
        copy.start()
    sequences, segments, narrow, points = out_ref.shape
    rows = sequences * narrow

    def mixed(residue, paired):
        filter_re = filter_ref[residue, 0].astype(jnp.float32)
        filter_im = filter_ref[residue, 1].astype(jnp.float32)
        if paired:
            filter_re = filter_re + filter_ref[2 * segments - residue, 0].astype(jnp.float32)
            filter_im = filter_im - filter_ref[2 * segments - residue, 1].astype(jnp.float32)
        signal_re = spectra_ref[residue, 0].reshape(sequences, narrow, points)
        signal_im = spectra_ref[residue, 1].reshape(sequences, narrow, points)
        mixed_re = (signal_re * filter_re - signal_im * filter_im).reshape(rows, points)
        mixed_im = (signal_re * filter_im + signal_im * filter_re).reshape(rows, points)
        return jnp.concatenate([mixed_re.astype(jnp.bfloat16), mixed_im.astype(jnp.bfloat16)], axis=1)

    def emit(base, count, paired):
        values = jnp.concatenate([mixed(base + extra, paired) for extra in range(count)], axis=0)
        full = jnp.dot(values, matrix_ref[...], preferred_element_type=jnp.float32).reshape(count, rows, 2 * points)
        for extra in range(count):
            residue = base + extra
            cos = twist_ref[residue, 0:1]
            sin = twist_ref[residue, 1:2]
            mid_ref[residue, 0] = full[extra, :, :points] * cos - full[extra, :, points:] * sin
            mid_ref[residue, 1] = full[extra, :, :points] * sin + full[extra, :, points:] * cos

    over_chunks(emit, segments, chunk)
    tiles = narrow // sub

    def tile_step(step, carry):
        which = step // tiles
        start = pl.multiple_of((step % tiles) * sub, sub)
        source = pl.multiple_of(step * sub, sub)
        for left in range(0, points, lane):
            here = slice(left, left + lane)
            bins = [
                tuple(mid_ref[index, part, pl.ds(source, sub), here] for part in range(2))
                for index in range(segments + 1)
            ]
            for seg, value in enumerate(real_segments(bins)):
                out_ref[which, seg, pl.ds(start, sub), here] = value.astype(jnp.bfloat16)
        return carry

    lax.fori_loop(0, sequences * tiles, tile_step, 0)
    for copy in copies:
        copy.wait()


def inverse_call(spectra, filters, twist, matrices, states):
    final, held = states
    residues, _, rows, points = spectra.shape
    segments = residues - 1
    narrow = filters.shape[2]
    sequences = rows // narrow
    out, *final = pl.pallas_call(
        functools.partial(inverse_kernel, chunk=8),
        in_specs=[whole] * 7 + [outside] * 3,
        out_specs=[whole] + [outside] * 3,
        out_shape=[jax.ShapeDtypeStruct((sequences, segments, narrow, points), jnp.bfloat16)]
        + [jax.ShapeDtypeStruct(state.shape, state.dtype) for state in final],
        input_output_aliases={7: 1, 8: 2, 9: 3},
        scratch_shapes=[
            pltpu.VMEM((residues, 2, rows, points), jnp.float32),
            pltpu.SemaphoreType.DMA((3 * held[0].shape[0], 1)),
        ],
        compiler_params=roomy,
        name="inverse",
    )(spectra, filters, twist, matrices, *held, *final)
    return out, final


def pack_plain(signal, cotangent, narrow):
    points, channels = signal.shape
    both = jnp.stack([signal, cotangent]).reshape(2, points, channels // narrow, narrow)
    return both.transpose(2, 0, 3, 1).reshape(channels // narrow, 2 * narrow, points)


def forward_plain(arrived, twist, matrices):
    sequences, segments, pair_rows, points = arrived.shape
    narrow = pair_rows // 2
    rows = sequences * narrow
    parts = arrived.reshape(sequences, segments, 2, narrow, points).astype(jnp.float32)
    parts = parts.transpose(1, 2, 0, 3, 4).reshape(segments, 2 * rows, points)
    bins = half_spectrum([parts[seg] for seg in range(segments)])
    re = jnp.stack([item[0] for item in bins])
    im = jnp.stack([jnp.zeros_like(item[0]) if item[1] is None else item[1] for item in bins])
    cos, sin = twist[:, 0][:, None], twist[:, 1][:, None]
    mid = jnp.concatenate([re * cos + im * sin, im * cos - re * sin], axis=2).astype(jnp.bfloat16)
    full = jnp.dot(mid, matrices, preferred_element_type=jnp.float32)
    signal_re, signal_im = full[:, :rows, :points], full[:, :rows, points:]
    cotan_re, cotan_im = full[:, rows:, :points], full[:, rows:, points:]
    shape = (segments + 1, sequences, narrow, points)
    scale = 1.0 / (2 * segments * points)
    real = jnp.sum((signal_re * cotan_re + signal_im * cotan_im).reshape(shape), axis=1) * scale
    imag = jnp.sum((signal_re * cotan_im - signal_im * cotan_re).reshape(shape), axis=1) * scale
    real = jnp.concatenate([real, real[1:segments][::-1]])
    imag = jnp.concatenate([imag, -imag[1:segments][::-1]])
    grad = jnp.stack([real, imag], axis=1).astype(jnp.bfloat16)
    return grad, jnp.stack([signal_re, signal_im], axis=1)


def mirrored_rows(local_outer):
    rows = jnp.arange(local_outer, dtype=jnp.int32)
    return is_mirrored(rows, local_outer)[None, :, None, None]


def gradient_plain(sent, shape):
    arrived = sent.astype(jnp.float32).transpose(2, 1, 4, 0, 3).reshape(shape)
    return jnp.where(mirrored_rows(shape[1]), arrived[:, :, ::-1], arrived)


def update_plain(sent, spectrum, first_moment, second_moment):
    groups, local_outer, _, narrow, points = sent.shape
    grad = gradient_plain(sent, spectrum.shape)
    new_spec, new_first, new_second = moved(grad, spectrum, first_moment, second_moment)
    out = jnp.where(mirrored_rows(local_outer), new_spec[:, :, ::-1], new_spec).astype(jnp.bfloat16)
    out = out.reshape(2, local_outer, points, groups, narrow).transpose(3, 1, 0, 4, 2)
    return (new_spec, new_first, new_second), out


def inverse_plain(spectra, filters, twist, matrices, states):
    residues, _, rows, points = spectra.shape
    segments = residues - 1
    narrow = filters.shape[2]
    sequences = rows // narrow
    wide = filters.astype(jnp.float32)
    mirrored = jnp.concatenate([jnp.zeros_like(wide[:1]), wide[segments + 1 :][::-1], jnp.zeros_like(wide[:1])])
    filter_re = (wide[: segments + 1, 0] + mirrored[:, 0])[:, None]
    filter_im = (wide[: segments + 1, 1] - mirrored[:, 1])[:, None]
    shape = (residues, sequences, narrow, points)
    signal_re, signal_im = spectra[:, 0].reshape(shape), spectra[:, 1].reshape(shape)
    mixed_re = (signal_re * filter_re - signal_im * filter_im).reshape(residues, rows, points)
    mixed_im = (signal_re * filter_im + signal_im * filter_re).reshape(residues, rows, points)
    mixed = jnp.concatenate([mixed_re, mixed_im], axis=2).astype(jnp.bfloat16)
    full = jnp.dot(mixed, matrices, preferred_element_type=jnp.float32)
    cos, sin = twist[:, 0][:, None], twist[:, 1][:, None]
    mid_re = full[..., :points] * cos - full[..., points:] * sin
    mid_im = full[..., :points] * sin + full[..., points:] * cos
    out = jnp.stack(real_segments([(mid_re[index], mid_im[index]) for index in range(residues)]))
    out = out.reshape(segments, sequences, narrow, points).transpose(1, 0, 2, 3)
    return out.astype(jnp.bfloat16), states


def per_device(inputs, grad_out, spectrum, first_moment, second_moment):
    seq_count = lax.axis_size("seq")
    batch_count = lax.axis_size("batch")
    batch_rows, points, channels = inputs.shape
    narrow = channels // (seq_count * batch_count)
    local_outer = spectrum.shape[1]
    outer = 2 * seq_count
    tiled = narrow % sub == 0 and points % lane == 0 and batch_rows == 1
    twist = jnp.asarray(twist_table(outer, points))
    ahead, back = point_matrices(points, 1.0 / (outer * points))
    ahead, back = jnp.asarray(ahead, jnp.bfloat16), jnp.asarray(back, jnp.bfloat16)

    pack = pack_call if tiled else pack_plain
    packed = jnp.stack([pack(inputs[row], grad_out[row], narrow) for row in range(batch_rows)], axis=1)
    arrived = lax.all_to_all(packed, ("batch", "seq"), split_axis=0, concat_axis=0, tiled=True)
    arrived = arrived.reshape(batch_count, seq_count, batch_rows, 2 * narrow, points)
    arrived = arrived.transpose(0, 2, 1, 3, 4).reshape(-1, seq_count, 2 * narrow, points)
    sequences = arrived.shape[0]

    grad, spectra = (forward_call if tiled else forward_plain)(arrived, twist, ahead)
    grad = grad.reshape(seq_count, local_outer, 2, narrow, points)
    sent = lax.all_to_all(grad, "seq", split_axis=0, concat_axis=0, tiled=True)

    update = update_call if tiled else update_plain
    states, filters = update(sent, spectrum, first_moment, second_moment)
    filters = lax.all_to_all(filters, "seq", split_axis=0, concat_axis=0, tiled=True)
    filters = filters.reshape(outer, 2, narrow, points)

    rows, states = (inverse_call if tiled else inverse_plain)(spectra, filters, twist, back, states)
    rows = rows.reshape(batch_count, batch_rows, seq_count, narrow, points).transpose(0, 2, 1, 3, 4)
    rows = rows.reshape(batch_count * seq_count, batch_rows, narrow, points)
    rows = lax.all_to_all(rows, ("batch", "seq"), split_axis=0, concat_axis=0, tiled=True)
    if tiled:
        filtered = unpack_call(rows.reshape(channels, points))[None]
    else:
        filtered = rows.transpose(1, 3, 0, 2).reshape(batch_rows, points, channels)
    return *states, filtered


def solution(mesh):
    return jax.shard_map(
        per_device,
        mesh=mesh,
        in_specs=(
            P("batch", "seq", None),
            P("batch", "seq", None),
            P(None, "seq", None, "batch"),
            P(None, "seq", None, "batch"),
            P(None, "seq", None, "batch"),
        ),
        out_specs=(
            P(None, "seq", None, "batch"),
            P(None, "seq", None, "batch"),
            P(None, "seq", None, "batch"),
            P("batch", "seq", None),
        ),
        check_vma=False,
    )
```
